512 devices in a mesh: rep: 4 (over y), expert: 128 (over x, z, core).
Axes of the slice: x: 4, y: 4, z: 16, core: 2. Of those that a mesh axis runs over, the one named last changes fastest.
Arguments:
- positions: float32 [3, 98304], P(None, ('rep', 'expert')), may hold values from -4 to 4
- frequencies: float32 [3, 256], replicated, may hold values from -8 to 8
- phases: float32 [256], replicated, may hold values from -3.140625 to 3.140625
- w_first: bfloat16 [128, 256, 256], P('expert'), may hold values from -0.375 to 0.375
- w_second: bfloat16 [128, 256, 256], P('expert'), may hold values from -0.375 to 0.375
- w_head: bfloat16 [128, 4, 256], P('expert'), may hold values from -0.375 to 0.375
- spacing: float32 [98304], P(('rep', 'expert')), may hold values from 0.05 to 0.6
- expert_ids: int32 [98304, 1], P(('rep', 'expert')), may hold values from 0 to 127; in each aligned block of 192 rows (0 to 191, 192 to 383, ...) at most 3 rows name the same one
- ray_lengths: int32 [512, 96], P(('rep', 'expert')), may hold values from 1 to 4, 192 in all within a row
- target: float32 [3, 49152], P(None, ('rep', 'expert')), may hold values from 0 to 1
- cam_owner: int32 [49152, 1], P(('rep', 'expert')), may hold values from 0 to 127; in each aligned block of 96 rows (0 to 95, 96 to 191, ...) at most 2 rows name the same one
- cam_slot: int32 [49152], P(('rep', 'expert')), may hold values from 0 to 8191
Outputs:
- grad_first: float32 [128, 256, 256], P('expert')
- grad_second: float32 [128, 256, 256], P('expert')
- grad_head: float32 [128, 4, 256], P('expert')
- pose_normal: float32 [36, 1048576], P(None, 'expert')
- pose_force: float32 [6, 1048576], P(None, 'expert')
The draws below stay inside these ranges and needn't reach their ends.
Inputs may be any that keep to these rules, and one draw needn't show every extreme that they name: `expert_ids`: at most 3 samples of one device name the same expert, and some device has an expert named exactly 3 times. `cam_owner`: at most 2 rays of one device name the same camera shard, and some device reaches 2. `ray_lengths`: the lengths of one device's rays sum to 192; some ray has exactly 4 samples.
All inputs are finite; a program needn't handle non-finite values.
Results may differ from the reference program's by a relative error of at most 0.0065.
Values may be sent and summed in bfloat16 or wider, within the bound.
No kernel may reach another device: no remote copies, remote signals or barrier semaphores. Data moves between devices by JAX's collectives and lax.ppermute only.
A program may use at most 64 MiB of HBM per device.

```python
import math
from functools import partial
import jax
import jax.numpy as jnp
import numpy as np
from jax import lax

HID = 256
EXPERTS = 128
SAMP_DEV = 192
RAYS_DEV = 96
MAXS = 4
CAP = 3
CAPC = 2
CAM_DEV = 8192
CAMERAS = 1048576
SAMPLES = 98304
RAYS = 49152
N_REP = 4
N_EXPERT = 128


def touch_ends(values, rng, smallest, top_value):
    shape = values.shape
    place = [jax.random.randint(jax.random.fold_in(rng, axis), (), 0, shape[axis]) for axis in range(len(shape))]
    values = values.at[tuple(place)].set(smallest)
    longest = shape.index(max(shape))
    place[longest] = (place[longest] + 1) % shape[longest]
    return values.at[tuple(place)].set(top_value)


def level_of(stream_key, dims, shards, least, top_value):
    def one(position, blocks):
        draws = jax.random.uniform(jax.random.fold_in(jax.random.fold_in(stream_key, 6), position), (blocks,), jnp.float32, least / len(shards), top_value / len(shards))
        return jnp.repeat(jnp.exp(draws), dims[position] // blocks).reshape((-1,) + (1,) * (len(dims) - position - 1))

    gain = one(*shards[0])
    for cut in shards[1:]:
        gain = gain * one(*cut)
    return gain


def split_up(count, total, bound, lean):
    portions = [(1 << 20) // math.isqrt(grade ** lean) + 1 for grade in range(2, count + 1)]
    surplus, counts = total - bound - (count - 1), [1] * (count - 1)
    while surplus > 0:
        free = [i for i in range(count - 1) if counts[i] < bound]
        pool, budget = sum([portions[i] for i in free]), surplus
        for i in free:
            addition = min(bound - counts[i], max(1, budget * portions[i] // pool), surplus)
            counts[i] = counts[i] + addition
            surplus = surplus - addition
    return np.array([bound] + counts)


def ragged_sizes(own_key, number_of, total, bound, skew):
    if number_of == 2:
        one = jax.random.randint(own_key, (), max(1, total - bound), min(bound, total - 1) + 1)
        return jnp.stack([one, total - one])
    tallies = jnp.asarray(split_up(number_of, total, bound, skew), jnp.int32)
    couples = (number_of - 1) // 2
    donor, receiver = tallies[1:1 + 2 * couples:2], tallies[2:2 + 2 * couples:2]
    margin = jnp.minimum(donor - 1, bound - receiver)
    shifted = jax.random.randint(jax.random.fold_in(own_key, 1), (couples,), 0, 1 << 20) % (margin + 1)
    tallies = tallies.at[1:1 + 2 * couples:2].set(donor - shifted).at[2:2 + 2 * couples:2].set(receiver + shifted)
    return tallies[jax.random.permutation(jax.random.fold_in(own_key, 2), number_of)]


def assign_block(key, own, number, rows, count, top, reach, lean):
    order = jax.random.permutation(key, count)
    heavy_load, usual = shares(count, rows * top, reach, lean, True), shares(count, rows * top, reach, lean, False)
    places = jnp.arange(count)

    def named(sizes, turn):
        used = int((sizes > 0).sum())
        fixed = max(1, used // 4)
        moved = fixed + (places - fixed + turn * (used - fixed)) % max(1, count - fixed)
        return jnp.zeros((count,), jnp.int32).at[order[jnp.where(places < fixed, places, moved)]].set(jnp.asarray(sizes, jnp.int32))

    sizes = jnp.where(number % 4 == 0, named(heavy_load, number // 4), named(usual, number - number // 4 - 1))
    mixed = jax.random.permutation(jax.random.fold_in(own, 3), count)
    donor, receiver = mixed[0:count // 2 * 2:2], mixed[1:count // 2 * 2:2]
    margin = jnp.minimum(sizes[donor] - 1, reach - sizes[receiver]) // 2
    margin = jnp.where((donor == order[0]) | (receiver == order[0]) | (sizes[receiver] == 0), 0, jnp.maximum(margin, 0))
    moved = jax.random.randint(jax.random.fold_in(own, 4), (count // 2,), 0, 1 << 20) % (margin + 1)
    sizes = sizes.at[donor].add(-moved).at[receiver].add(moved)
    labels = jnp.searchsorted(jnp.cumsum(sizes), jnp.arange(rows * top), side="right").astype(jnp.int32)
    table = labels.reshape(top, rows).T
    table = table[jax.random.permutation(jax.random.fold_in(own, 1), rows)]
    turn = jax.random.randint(jax.random.fold_in(own, 2), (rows, 1), 0, top)
    return jnp.take_along_axis(table, (jnp.arange(top)[None, :] + turn) % top, axis=1)


def shares(number_of, total, most, skew, full):
    weights = [(1 << 20) // math.isqrt(standing ** skew) + 1 for standing in range(1, number_of + 1)]
    largest = most if full else min(most, max(-(-total // number_of), total * weights[0] // sum(weights)))
    least = 1 if total - largest >= number_of - 1 else 0
    counts, rest = [largest] + [least] * (number_of - 1), total - largest - least * (number_of - 1)
    while rest > 0:
        candidates = [i for i in range(1, number_of) if counts[i] < largest] or [i for i in range(1, number_of) if counts[i] < most]
        mass, remaining = sum([weights[i] for i in candidates]), rest
        for i in candidates:
            more = min(most - counts[i], max(1, remaining * weights[i] // mass), rest)
            counts[i] = counts[i] + more
            rest = rest - more
    return np.array(counts)


def bell_draw(key, dims, spread, most, cuts=(), held_as=jnp.bfloat16):
    values = spread * jax.random.normal(key, dims, jnp.float32)
    if cuts:
        values = values * level_of(key, dims, cuts, -0.22, 0.18)
    return jnp.clip(values, -most, most).astype(held_as)


def setup_inputs(seed: int = 0) -> dict:
    splits = jax.random.split(jax.random.key(seed), 13)
    positions = bell_draw(splits[0], (3, SAMPLES), 1.0, 4.0, ((1, 512),), jnp.float32)
    frequencies = bell_draw(splits[1], (3, HID), 2.0, 8.0, (), jnp.float32)
    phases = jnp.clip(jax.random.uniform(splits[2], (HID,), jnp.float32, -3.140625, 3.140625), -3.140625, 3.140625)
    w_first = bell_draw(splits[3], (EXPERTS, HID, HID), HID ** -0.5, 0.375, ((0, 128),))
    w_second = bell_draw(splits[4], (EXPERTS, HID, HID), HID ** -0.5, 0.375, ((0, 128),))
    w_head = bell_draw(splits[5], (EXPERTS, 4, HID), HID ** -0.5, 0.375, ((0, 128),))
    spacing = jnp.clip(jnp.exp(math.log(0.6) - 2.4849067 * jax.random.uniform(splits[6], (SAMPLES,), jnp.float32) ** level_of(splits[6], (SAMPLES,), ((0, 512),), -0.2, 0.2)), 0.05, 0.6)
    expert_ids_keys = jax.random.split(jax.random.fold_in(splits[7], 1), SAMPLES // SAMP_DEV)
    expert_ids_turns = jax.random.permutation(jax.random.fold_in(splits[7], 3), SAMPLES // SAMP_DEV)
    expert_ids = jax.vmap(lambda own, number: assign_block(jax.random.fold_in(splits[7], 2), own, number, SAMP_DEV, EXPERTS, 1, CAP, 2))(expert_ids_keys, expert_ids_turns).reshape((SAMPLES, 1))
    ray_lengths = jax.vmap(lambda own: ragged_sizes(own, RAYS_DEV, SAMP_DEV, MAXS, 2))(jax.random.split(splits[8], (N_REP * N_EXPERT))).reshape((N_REP * N_EXPERT, RAYS_DEV)).astype(jnp.int32)
    target = jnp.clip(1.0 * jax.random.uniform(splits[9], (3, RAYS), jnp.float32) ** level_of(splits[9], (3, RAYS), ((1, 512),), -0.2, 0.2), 0.0, 1.0)
    cam_owner_keys = jax.random.split(jax.random.fold_in(splits[10], 1), RAYS // RAYS_DEV)
    cam_owner_turns = jax.random.permutation(jax.random.fold_in(splits[10], 3), RAYS // RAYS_DEV)
    cam_owner = jax.vmap(lambda own, number: assign_block(jax.random.fold_in(splits[10], 2), own, number, RAYS_DEV, N_EXPERT, 1, CAPC, 1))(cam_owner_keys, cam_owner_turns).reshape((RAYS, 1))
    cam_slot = touch_ends(jax.random.randint(splits[11], (RAYS,), 0, CAM_DEV), jax.random.fold_in(splits[11], 1), 0, CAM_DEV - 1).astype(jnp.int32)
    return {"positions": positions, "frequencies": frequencies, "phases": phases, "w_first": w_first, "w_second": w_second, "w_head": w_head, "spacing": spacing, "expert_ids": expert_ids, "ray_lengths": ray_lengths, "target": target, "cam_owner": cam_owner, "cam_slot": cam_slot}


HIGHEST = lax.Precision.HIGHEST

def silu_slope(value):
    sig = jax.nn.sigmoid(value)
    return sig * (1.0 + value * (1.0 - sig))

def encode_stack(points, frequencies, phases):
    angle = frequencies[0][:, None] * points[0][None, :] + frequencies[1][:, None] * points[1][None, :]
    angle = angle + frequencies[2][:, None] * points[2][None, :] + phases[:, None]
    wave = jnp.sin(angle)
    slope = jnp.cos(angle)
    return jnp.stack([wave, slope * frequencies[0][:, None], slope * frequencies[1][:, None], slope * frequencies[2][:, None]])

def membership(lengths, sample_count):
    index = jnp.arange(sample_count, dtype=jnp.int32)
    ends = jnp.cumsum(lengths).astype(jnp.int32)
    starts = (ends - lengths).astype(jnp.int32)
    member = ((index[None, :] >= starts[:, None]) & (index[None, :] < ends[:, None])).astype(jnp.float32)
    return (member, starts)

def composite(raw, spacing, lengths):
    member, starts = membership(lengths, raw.shape[1])
    density = jax.nn.softplus(raw[0])
    colors = jax.nn.sigmoid(raw[1:4])
    depth = density * spacing
    before = jnp.cumsum(depth) - depth
    anchor = jnp.dot(jnp.take(before, starts), member, precision=HIGHEST)
    weights = jnp.exp(anchor - before) * (1.0 - jnp.exp(-depth))
    return jnp.einsum('cs,rs->cr', weights[None, :] * colors, member, precision=HIGHEST)

def device_terms(fields, points, spacing, lengths, target, scale):
    raw = fields[:4]
    motion = fields[4:].reshape(3, 4, fields.shape[1])
    color, pullback = jax.vjp(partial(composite, spacing=spacing, lengths=lengths), raw)
    residual = color - target
    grad_raw = pullback(scale * residual)[0]

    def pull_channel(cotangent):
        return pullback(cotangent)[0]
    basis = jnp.eye(3, dtype=jnp.float32)[:, :, None] * jnp.ones_like(color)[None]
    sensitivity = jax.vmap(pull_channel)(basis)
    point_x, point_y, point_z = (points[0], points[1], points[2])
    turn_x = motion[2] * point_y - motion[1] * point_z
    turn_y = motion[0] * point_z - motion[2] * point_x
    turn_z = motion[1] * point_x - motion[0] * point_y
    along = jnp.stack([turn_x, turn_y, turn_z, motion[0], motion[1], motion[2]])
    contrib = jnp.einsum('cms,kms->cks', sensitivity, along, precision=HIGHEST)
    member, starts = membership(lengths, raw.shape[1])
    jacobian = jnp.einsum('cks,rs->ckr', contrib, member, precision=HIGHEST)
    normal = jnp.einsum('car,cbr->abr', jacobian, jacobian, precision=HIGHEST).reshape(36, jacobian.shape[2])
    force = jnp.einsum('car,cr->ar', jacobian, residual, precision=HIGHEST)
    return (grad_raw, jnp.concatenate([normal, force], axis=0))

def ref_fields(stack, first_weight, second_weight, head_weight):
    layer_one = jnp.einsum('chm,hk->cmk', stack.astype(jnp.float32), first_weight.astype(jnp.float32))
    slope_one = silu_slope(layer_one[0])
    hidden_one = jnp.concatenate([jax.nn.silu(layer_one[0])[None], layer_one[1:] * slope_one[None]]).astype(jnp.bfloat16)
    layer_two = jnp.einsum('cmh,hk->cmk', hidden_one.astype(jnp.float32), second_weight.astype(jnp.float32))
    slope_two = silu_slope(layer_two[0])
    hidden_two = jnp.concatenate([jax.nn.silu(layer_two[0])[None], layer_two[1:] * slope_two[None]]).astype(jnp.bfloat16)
    result = jnp.einsum('cmh,oh->com', hidden_two.astype(jnp.float32), head_weight.astype(jnp.float32))
    return result.reshape(16, result.shape[2])

def ref_grads(stack, slopes, first_weight, second_weight, head_weight):
    features = stack[0].astype(jnp.float32)
    layer_one = jnp.einsum('hm,hk->mk', features, first_weight.astype(jnp.float32))
    hidden_one = jax.nn.silu(layer_one).astype(jnp.bfloat16)
    layer_two = jnp.dot(hidden_one.astype(jnp.float32), second_weight.astype(jnp.float32))
    hidden_two = jax.nn.silu(layer_two).astype(jnp.bfloat16)
    slopes_f = slopes.astype(jnp.float32)
    grad_head = jnp.dot(slopes_f, hidden_two.astype(jnp.float32))
    back_two = (jnp.einsum('om,oh->mh', slopes_f, head_weight.astype(jnp.float32)) * silu_slope(layer_two)).astype(jnp.bfloat16)
    grad_second = jnp.einsum('mh,mk->hk', hidden_one.astype(jnp.float32), back_two.astype(jnp.float32))
    back_one = (jnp.einsum('mk,hk->mh', back_two.astype(jnp.float32), second_weight.astype(jnp.float32)) * silu_slope(layer_one)).astype(jnp.bfloat16)
    grad_first = jnp.einsum('hm,mk->hk', features, back_one.astype(jnp.float32))
    return (grad_first, grad_second, grad_head)

def bucket_table(sample_expert, row_count, bucket):
    order = jnp.argsort(sample_expert, stable=True).astype(jnp.int32)
    ordered = sample_expert[order]
    totals = jnp.zeros((EXPERTS,), jnp.int32).at[sample_expert].add(1)
    offsets = (jnp.cumsum(totals) - totals).astype(jnp.int32)
    within = jnp.arange(row_count, dtype=jnp.int32) - offsets[ordered]
    return jnp.full((EXPERTS, bucket), row_count, jnp.int32).at[ordered, within].set(order)

def reference(positions, frequencies, phases, w_first, w_second, w_head, spacing, expert_ids, ray_lengths, target, cam_owner, cam_slot):
    row_count = N_EXPERT * SAMP_DEV
    bucket = N_EXPERT * CAP
    devices = N_REP * N_EXPERT
    scale = float(EXPERTS) / float(RAYS)
    sample_expert = expert_ids[:, 0]
    tables = []
    field_rows = []
    for group in range(N_REP):
        points = positions[:, group * row_count:(group + 1) * row_count]
        table = bucket_table(sample_expert[group * row_count:(group + 1) * row_count], row_count, bucket)
        padded = jnp.concatenate([points, jnp.zeros((3, 1), jnp.float32)], axis=1)

        def one_forward(inputs):
            slots, first_weight, second_weight, head_weight = inputs
            stack = encode_stack(padded[:, slots], frequencies, phases).astype(jnp.bfloat16)
            return ref_fields(stack, first_weight, second_weight, head_weight)
        fields = lax.map(one_forward, (table, w_first, w_second, w_head))
        flat = jnp.transpose(fields, (1, 0, 2)).reshape(16, EXPERTS * bucket)
        placed = jnp.zeros((16, row_count + 1), jnp.float32).at[:, table.reshape(-1)].set(flat)[:, :row_count]
        field_rows.append(placed)
        tables.append(table)
    fields_all = jnp.concatenate(field_rows, axis=1)
    per_fields = jnp.moveaxis(fields_all.reshape(16, devices, SAMP_DEV), 1, 0)
    per_points = jnp.moveaxis(positions.reshape(3, devices, SAMP_DEV), 1, 0)
    per_spacing = spacing.reshape(devices, SAMP_DEV)
    per_target = jnp.moveaxis(target.reshape(3, devices, RAYS_DEV), 1, 0)
    grad_raw, blocks = jax.vmap(partial(device_terms, scale=scale))(per_fields, per_points, per_spacing, ray_lengths, per_target)
    slope_all = jnp.moveaxis(grad_raw, 0, 1).reshape(4, SAMPLES).astype(jnp.bfloat16)
    totals = None
    for group in range(N_REP):
        points = positions[:, group * row_count:(group + 1) * row_count]
        padded = jnp.concatenate([points, jnp.zeros((3, 1), jnp.float32)], axis=1)
        slopes_row = jnp.concatenate([slope_all[:, group * row_count:(group + 1) * row_count], jnp.zeros((4, 1), jnp.bfloat16)], axis=1)

        def one_backward(inputs):
            slots, first_weight, second_weight, head_weight = inputs
            stack = encode_stack(padded[:, slots], frequencies, phases).astype(jnp.bfloat16)
            return ref_grads(stack, slopes_row[:, slots], first_weight, second_weight, head_weight)
        parts = lax.map(one_backward, (tables[group], w_first, w_second, w_head))
        if totals is None:
            totals = tuple(parts)
        else:
            totals = tuple((total + extra for total, extra in zip(totals, parts)))
    ray_blocks = jnp.moveaxis(blocks, 0, 1).reshape(42, RAYS)
    camera = cam_owner[:, 0] * CAM_DEV + cam_slot
    camera_table = jnp.zeros((42, CAMERAS), jnp.float32).at[:, camera].add(ray_blocks)
    return (totals[0], totals[1], totals[2], camera_table[:36], camera_table[36:])
```

```python
import jax
import jax.numpy as jnp
from jax import lax
from jax.experimental import pallas as pl
from jax.experimental.pallas import tpu as pltpu
from jax.sharding import PartitionSpec as P

HID = 256
PEERS = 128
REPS = 4
SAMP = 192
RAYS = 96
LANES = 256
CAP = 3
CAPC = 2
CAM_DEV = 8192
LOW = 256
SLOPE_LANE = 96
LABEL_ROW = 36
FORCE_ROW = 40

F32 = jnp.float32
BF16 = jnp.bfloat16


def iota(shape, axis):
    return lax.broadcasted_iota(jnp.int32, shape, axis)


def dot_nn(left, right):
    return jnp.dot(left, right, preferred_element_type=F32)


def dot_nt(left, right):
    return lax.dot_general(left, right, (((1,), (1,)), ((), ())), preferred_element_type=F32)


def dot_tn(left, right):
    return lax.dot_general(left, right, (((0,), (0,)), ((), ())), preferred_element_type=F32)


def split_three(value):
    high = value.astype(BF16)
    rest = value - high.astype(F32)
    middle = rest.astype(BF16)
    low = (rest - middle.astype(F32)).astype(BF16)
    return high, middle, low


def sin_cos(angle):
    turns = jnp.round(angle * 0.6366197723675814)
    rest = angle - turns * 1.5703125
    rest = rest - turns * 4.8375129699707031e-4
    rest = rest - turns * 7.549789954891882e-8
    square = rest * rest
    sine = rest + rest * square * (
        -1.6666654611e-1 + square * (8.3321608736e-3 - square * 1.9515295891e-4)
    )
    cosine = (
        1.0
        - 0.5 * square
        + square
        * square
        * (4.166664568298827e-2 + square * (-1.388731625493765e-3 + square * 2.443315711809948e-5))
    )
    quarter = turns.astype(jnp.int32)
    odd = (quarter & 1) == 1
    sin_value = jnp.where(odd, cosine, sine)
    cos_value = jnp.where(odd, sine, cosine)
    sin_value = jnp.where((quarter & 2) == 2, -sin_value, sin_value)
    cos_value = jnp.where(((quarter + 1) & 2) == 2, -cos_value, cos_value)
    return sin_value, cos_value


def angles_of(points, slot, freq, phase):
    base = 4 * slot
    angle = freq[0:1] * points[:, base : base + 1] + freq[1:2] * points[:, base + 1 : base + 2]
    return angle + freq[2:3] * points[:, base + 2 : base + 3] + phase


def silu_pair(value):
    sig = jax.nn.sigmoid(value)
    return value * sig, sig * (1.0 + value * (1.0 - sig))


def expert_rank(ids_row, width):
    hot = (iota((PEERS, width), 0) == ids_row).astype(F32)
    earlier = (iota((width, width), 0) < iota((width, width), 1)).astype(BF16)
    counts = dot_nn(hot.astype(BF16), earlier)
    rank = jnp.sum(counts * hot, axis=0, keepdims=True)
    return hot, rank


def prep_kernel(ids_ref, pos_ref, out_ref, rows_ref):
    hot, rank = expert_rank(ids_ref[...], SAMP)
    rows_ref[...] = jnp.zeros_like(rows_ref)
    points = pos_ref[...]
    for slot in range(CAP):
        rows_ref[4 * slot : 4 * slot + 3, :] = jnp.where(rank == float(slot), points, 0.0)
    hot = hot.astype(BF16)
    high, middle, low = split_three(rows_ref[...])
    out_ref[...] = dot_nt(hot, high) + (dot_nt(hot, middle) + dot_nt(hot, low))


def forward_kernel(points_ref, freq_ref, phase_ref, first_ref, second_ref, head_ref, out_ref):
    points = points_ref[...]
    freq = freq_ref[...]
    phase = phase_ref[...]
    first = first_ref[0]
    second = second_ref[0]
    head_row = iota((PEERS, 4), 0)
    head_pick = ((head_row // 4) % 4 == iota((PEERS, 4), 1)).astype(BF16)
    head_all = dot_nn(head_pick, head_ref[0]).astype(BF16)
    lane_row = iota((PEERS, HID), 0)
    total = None
    for slot in range(CAP):
        sine, cosine = sin_cos(angles_of(points, slot, freq, phase))
        stack = [sine.astype(BF16)] + [(cosine * freq[c : c + 1]).astype(BF16) for c in range(3)]
        one = [dot_nn(part, first) for part in stack]
        value, slope = silu_pair(one[0])
        hidden = [value.astype(BF16)] + [(one[k] * slope).astype(BF16) for k in range(1, 4)]
        two = [dot_nn(part, second) for part in hidden]
        value, slope = silu_pair(two[0])
        hidden = [value.astype(BF16)] + [(two[k] * slope).astype(BF16) for k in range(1, 4)]
        for k in range(4):
            keep = (lane_row // 16 == slot) & (lane_row % 4 == k)
            head = jnp.where(keep, head_all, jnp.zeros_like(head_all))
            term = dot_nt(hidden[k], head)
            total = term if total is None else total + term
    out_ref[...] = total


def device_kernel(
    fields_ref,
    ids_ref,
    pos_ref,
    space_ref,
    length_ref,
    target_ref,
    owner_ref,
    slot_ref,
    out_ref,
    wide_ref,
    stack_ref,
    ray_ref,
    samp_ref,
):
    wide_ref[...] = jnp.zeros_like(wide_ref)
    wide_ref[0:3, 0:SAMP] = pos_ref[...]
    wide_ref[3:4, 0:SAMP] = space_ref[...]
    wide_ref[4:5, :] = jnp.full((1, LANES), -1.0, F32)
    wide_ref[4:5, 0:SAMP] = ids_ref[...].astype(F32)
    px = wide_ref[0:1, :]
    py = wide_ref[1:2, :]
    pz = wide_ref[2:3, :]
    spacing = wide_ref[3:4, :]
    ids = wide_ref[4:5, :].astype(jnp.int32)
    hot, rank = expert_rank(ids, LANES)
    hot = hot.astype(BF16)
    turned = jnp.transpose(fields_ref[...])[0 : 16 * CAP]
    high, middle, low = split_three(turned)
    gathered = dot_nn(high, hot) + (dot_nn(middle, hot) + dot_nn(low, hot))
    fields = jnp.where(rank == 0.0, gathered[0:16], 0.0)
    for slot in range(1, CAP):
        fields = jnp.where(rank == float(slot), gathered[16 * slot : 16 * slot + 16], fields)

    lengths = length_ref[...].astype(F32)
    ray_a = iota((RAYS, RAYS), 0)
    ray_b = iota((RAYS, RAYS), 1)
    starts = jnp.sum(jnp.where(ray_b < ray_a, lengths, 0.0), axis=1, keepdims=True)
    ends = jnp.sum(jnp.where(ray_b <= ray_a, lengths, 0.0), axis=1, keepdims=True)
    index = iota((RAYS, LANES), 1).astype(F32)
    member = ((index >= starts) & (index < ends)).astype(BF16)
    begin = jnp.sum((index == starts).astype(F32), axis=0, keepdims=True)
    near_one = 1.0 - begin
    near_two = near_one * pltpu.roll(near_one, 1, 1)
    near_three = near_two * pltpu.roll(near_one, 2, 1)

    def preceding(value):
        return (
            pltpu.roll(value, 1, 1) * near_one
            + pltpu.roll(value, 2, 1) * near_two
            + pltpu.roll(value, 3, 1) * near_three
        )

    def following(value):
        return (
            pltpu.roll(value * near_one, LANES - 1, 1)
            + pltpu.roll(value * near_two, LANES - 2, 1)
            + pltpu.roll(value * near_three, LANES - 3, 1)
        )

    raw = [fields[4 * o : 4 * o + 1] for o in range(4)]
    moved = [[fields[4 * o + 1 + c : 4 * o + 2 + c] for c in range(3)] for o in range(4)]
    density = jnp.maximum(raw[0], 0.0) + jnp.log1p(jnp.exp(-jnp.abs(raw[0])))
    depth = density * spacing
    through = jnp.exp(-preceding(depth))
    fade = jnp.exp(-depth)
    weight = through * (1.0 - fade)
    depth_slope = spacing * jax.nn.sigmoid(raw[0])
    high, middle, low = split_three(target_ref[...])
    aims = dot_nn(high, member) + (dot_nn(middle, member) + dot_nn(low, member))
    along = []
    for o in range(4):
        m0, m1, m2 = moved[o]
        along.append(
            [m2 * py - m1 * pz, m0 * pz - m2 * px, m1 * px - m0 * py, m0, m1, m2]
        )
    stack_ref[...] = jnp.zeros_like(stack_ref)
    samp_ref[...] = jnp.zeros_like(samp_ref)
    scale = 1.0 / float(RAYS * REPS)
    slope_zero = None
    slope_rest = []
    for c in range(3):
        tint = jax.nn.sigmoid(raw[1 + c])
        share = weight * tint
        later = following(share)
        sense_zero = (through * fade * tint - later) * depth_slope
        sense_own = share * (1.0 - tint)
        miss = share + preceding(share) + later - aims[c : c + 1]
        part = miss * sense_zero
        slope_zero = part if slope_zero is None else slope_zero + part
        slope_rest.append(scale * miss * sense_own)
        for k in range(6):
            stack_ref[8 * c + k : 8 * c + k + 1, :] = (
                sense_zero * along[0][k] + sense_own * along[1 + c][k]
            )
        stack_ref[8 * c + 6 : 8 * c + 7, :] = share
    slopes = [scale * slope_zero] + slope_rest
    for slot in range(CAP):
        for o in range(4):
            samp_ref[SLOPE_LANE + 8 * slot + o : SLOPE_LANE + 8 * slot + o + 1, :] = jnp.where(
                rank == float(slot), slopes[o], 0.0
            )

    high, middle, low = split_three(stack_ref[...])
    rays = dot_nt(high, member) + (dot_nt(middle, member) + dot_nt(low, member))
    owners = owner_ref[...]
    camera_hot, camera_rank = expert_rank(owners, RAYS)
    camera_hot = camera_hot.astype(BF16)
    targets = target_ref[...]
    blocks = []
    for c in range(3):
        block = rays[8 * c : 8 * c + 8]
        row = iota((8, RAYS), 0)
        blocks.append(jnp.where(row == 6, block - targets[c : c + 1], block))
    ray_ref[...] = jnp.zeros_like(ray_ref)
    label = slot_ref[...].astype(F32)
    for a in range(6):
        outer = blocks[0][a : a + 1] * blocks[0]
        outer = outer + blocks[1][a : a + 1] * blocks[1]
        outer = outer + blocks[2][a : a + 1] * blocks[2]
        for slot in range(CAPC):
            kept = jnp.where(camera_rank == float(slot), outer, 0.0)
            base = 48 * slot
            ray_ref[base + 6 * a : base + 6 * a + 6, :] = kept[0:6]
            ray_ref[base + FORCE_ROW + a : base + FORCE_ROW + a + 1, :] = kept[6:7]
    for slot in range(CAPC):
        base = 48 * slot
        ray_ref[base + LABEL_ROW : base + LABEL_ROW + 1, :] = jnp.where(
            camera_rank == float(slot), label, 0.0
        )
    high, middle, low = split_three(ray_ref[...])
    message = dot_nt(camera_hot, high) + (dot_nt(camera_hot, middle) + dot_nt(camera_hot, low))
    out_ref[...] = message + dot_nt(hot, samp_ref[...].astype(BF16))


def final_kernel(
    got_ref,
    points_ref,
    freq_ref,
    phase_ref,
    first_ref,
    second_ref,
    head_ref,
    grad_first_ref,
    grad_second_ref,
    grad_head_ref,
    normal_ref,
    force_ref,
    feature_ref,
    back_one_ref,
    one_ref,
    back_two_ref,
):
    freq = freq_ref[...]
    phase = phase_ref[...]
    first = first_ref[0]
    second = second_ref[0]
    lane_row = iota((PEERS, 4), 0)
    head_all = dot_nn((lane_row % 8 == iota((PEERS, 4), 1)).astype(BF16), head_ref[0]).astype(BF16)
    wide_row = iota((PEERS, HID), 0)
    heads = []
    for slot in range(CAP):
        keep = (wide_row >= SLOPE_LANE + 8 * slot) & (wide_row < SLOPE_LANE + 8 * slot + 8)
        heads.append(jnp.where(keep, head_all, jnp.zeros_like(head_all)))
    lane = iota((PEERS, PEERS), 1)
    turned = []
    head_sum = jnp.zeros((4, HID), F32)
    head_parts = [None] * CAP
    for rep in range(REPS):
        got = got_ref[rep]
        slopes = jnp.where(lane >= SLOPE_LANE, got, 0.0).astype(BF16)
        flipped = jnp.transpose(got)
        turned.append(flipped)
        slopes_flipped = flipped[SLOPE_LANE:PEERS].astype(BF16)
        points = points_ref[rep]
        for slot in range(CAP):
            row = (rep * CAP + slot) * PEERS
            sine, _ = sin_cos(angles_of(points, slot, freq, phase))
            feature = sine.astype(BF16)
            value_one, slope_one = silu_pair(dot_nn(feature, first))
            hidden_one = value_one.astype(BF16)
            value_two, slope_two = silu_pair(dot_nn(hidden_one, second))
            hidden_two = value_two.astype(BF16)
            back_two = (dot_nn(slopes, heads[slot]) * slope_two).astype(BF16)
            back_one = (dot_nt(back_two, second) * slope_one).astype(BF16)
            term = dot_nn(slopes_flipped, hidden_two)
            head_parts[slot] = term if head_parts[slot] is None else head_parts[slot] + term
            feature_ref[row : row + PEERS, :] = feature
            one_ref[row : row + PEERS, :] = hidden_one
            back_one_ref[row : row + PEERS, :] = back_one
            back_two_ref[row : row + PEERS, :] = back_two
    for slot in range(CAP):
        head_sum = head_sum + head_parts[slot][8 * slot : 8 * slot + 4]
    grad_head_ref[0] = head_sum
    grad_first_ref[0] = dot_tn(feature_ref[...], back_one_ref[...])
    grad_second_ref[0] = dot_tn(one_ref[...], back_two_ref[...])

    values = []
    labels_row = []
    low_hot = []
    low_lane = iota((PEERS, LOW), 1)
    for rep in range(REPS):
        for slot in range(CAPC):
            base = 48 * slot
            values.append(turned[rep][base : base + 48])
            labels_row.append(turned[rep][base + LABEL_ROW : base + LABEL_ROW + 1])
            column = got_ref[rep][:, base + LABEL_ROW : base + LABEL_ROW + 1].astype(jnp.int32)
            low_hot.append(((column & (LOW - 1)) == low_lane).astype(BF16))
    values = jnp.concatenate(values, axis=1)
    rows = jnp.concatenate(labels_row, axis=1).astype(jnp.int32)
    group = rows // LOW
    low_hot = jnp.concatenate(low_hot, axis=0)
    high = values.astype(BF16).astype(F32)
    rest = values - high
    for block in range(CAM_DEV // LOW):
        here = group == block
        top = jnp.where(here, high, 0.0).astype(BF16)
        bottom = jnp.where(here, rest, 0.0).astype(BF16)
        table = dot_nn(top, low_hot) + dot_nn(bottom, low_hot)
        normal_ref[:, block * LOW : (block + 1) * LOW] = table[0:36]
        force_ref[:, block * LOW : (block + 1) * LOW] = table[FORCE_ROW : FORCE_ROW + 6]


def call(kernel, out_shape, *args, scratch=()):
    return pl.pallas_call(
        kernel,
        out_shape=out_shape,
        scratch_shapes=list(scratch),
        compiler_params=pltpu.CompilerParams(vmem_limit_bytes=40 * 1024 * 1024),
    )(*args)


def shape(*dims):
    return jax.ShapeDtypeStruct(dims, F32)


def exchange(value):
    return lax.all_to_all(value, "expert", split_axis=0, concat_axis=0, tiled=True)


def per_device(
    positions,
    frequencies,
    phases,
    w_first,
    w_second,
    w_head,
    spacing,
    expert_ids,
    ray_lengths,
    target,
    cam_owner,
    cam_slot,
):
    ids_row = expert_ids.reshape(1, SAMP)
    phase_row = phases.reshape(1, HID)
    weights = (w_first, w_second, w_head)
    square = shape(PEERS, PEERS)
    outgoing = call(
        prep_kernel, square, ids_row, positions, scratch=[pltpu.VMEM((PEERS, SAMP), F32)]
    )
    points = exchange(outgoing)
    fields = call(forward_kernel, square, points, frequencies, phase_row, *weights)
    all_points = lax.all_gather(points, "rep", axis=0, tiled=False)
    returned = exchange(fields)
    message = call(
        device_kernel,
        square,
        returned,
        ids_row,
        positions,
        spacing.reshape(1, SAMP),
        ray_lengths,
        target,
        cam_owner.reshape(1, RAYS),
        cam_slot.reshape(1, RAYS),
        scratch=[
            pltpu.VMEM((8, LANES), F32),
            pltpu.VMEM((24, LANES), F32),
            pltpu.VMEM((PEERS, RAYS), F32),
            pltpu.VMEM((PEERS, LANES), F32),
        ],
    )
    arrived = exchange(message)
    everything = lax.all_gather(arrived, "rep", axis=0, tiled=False)
    rows = REPS * CAP * PEERS
    return call(
        final_kernel,
        (
            shape(1, HID, HID),
            shape(1, HID, HID),
            shape(1, 4, HID),
            shape(36, CAM_DEV),
            shape(6, CAM_DEV),
        ),
        everything,
        all_points,
        frequencies,
        phase_row,
        *weights,
        scratch=[pltpu.VMEM((rows, HID), BF16)] * 4,
    )


def solution(mesh):
    in_specs = (
        P(None, ("rep", "expert")),
        P(),
        P(),
        P("expert", None, None),
        P("expert", None, None),
        P("expert", None, None),
        P(("rep", "expert")),
        P(("rep", "expert"), None),
        P(("rep", "expert"), None),
        P(None, ("rep", "expert")),
        P(("rep", "expert"), None),
        P(("rep", "expert")),
    )
    out_specs = (
        P("expert", None, None),
        P("expert", None, None),
        P("expert", None, None),
        P(None, "expert"),
        P(None, "expert"),
    )
    return jax.shard_map(
        per_device, mesh=mesh, in_specs=in_specs, out_specs=out_specs, check_vma=False
    )
```

```python
import jax
import jax.numpy as jnp
from jax import lax
from jax.experimental import pallas as pl
from jax.experimental.pallas import tpu as pltpu
from jax.sharding import PartitionSpec as P

HID = 256
PEERS = 128
REPS = 4
SAMP = 192
RAYS = 96
LANES = 256
CAP = 3
CAPC = 2
CAM_DEV = 8192
LOW = 256
SLOPE_LANE = 96
LABEL_ROW = 36
FORCE_ROW = 40

F32 = jnp.float32
BF16 = jnp.bfloat16


def iota(shape, axis):
    return lax.broadcasted_iota(jnp.int32, shape, axis)


def dot_nn(left, right):
    return jnp.dot(left, right, preferred_element_type=F32)


def dot_nt(left, right):
    return lax.dot_general(left, right, (((1,), (1,)), ((), ())), preferred_element_type=F32)


def dot_tn(left, right):
    return lax.dot_general(left, right, (((0,), (0,)), ((), ())), preferred_element_type=F32)


def split_three(value):
    high = value.astype(BF16)
    rest = value - high.astype(F32)
    middle = rest.astype(BF16)
    low = (rest - middle.astype(F32)).astype(BF16)
    return high, middle, low


def sin_cos(angle):
    turns = jnp.round(angle * 0.6366197723675814)
    rest = angle - turns * 1.5703125
    rest = rest - turns * 4.8375129699707031e-4
    rest = rest - turns * 7.549789954891882e-8
    square = rest * rest
    sine = rest + rest * square * (
        -1.6666654611e-1 + square * (8.3321608736e-3 - square * 1.9515295891e-4)
    )
    cosine = (
        1.0
        - 0.5 * square
        + square
        * square
        * (4.166664568298827e-2 + square * (-1.388731625493765e-3 + square * 2.443315711809948e-5))
    )
    quarter = turns.astype(jnp.int32)
    odd = (quarter & 1) == 1
    sin_value = jnp.where(odd, cosine, sine)
    cos_value = jnp.where(odd, sine, cosine)
    sin_value = jnp.where((quarter & 2) == 2, -sin_value, sin_value)
    cos_value = jnp.where(((quarter + 1) & 2) == 2, -cos_value, cos_value)
    return sin_value, cos_value


def angles_of(points, slot, freq, phase):
    base = 4 * slot
    angle = freq[0:1] * points[:, base : base + 1] + freq[1:2] * points[:, base + 1 : base + 2]
    return angle + freq[2:3] * points[:, base + 2 : base + 3] + phase


def silu_pair(value):
    sig = jax.nn.sigmoid(value)
    return value * sig, sig * (1.0 + value * (1.0 - sig))


def expert_rank(ids_row, width):
    hot = (iota((PEERS, width), 0) == ids_row).astype(F32)
    earlier = (iota((width, width), 0) < iota((width, width), 1)).astype(BF16)
    counts = dot_nn(hot.astype(BF16), earlier)
    rank = jnp.sum(counts * hot, axis=0, keepdims=True)
    return hot, rank


def fetch(pairs, sems):
    copies = [
        pltpu.make_async_copy(source, place, sems.at[number])
        for number, (source, place) in enumerate(pairs)
    ]
    for copy in copies:
        copy.start()
    for copy in copies:
        copy.wait()


def prep_kernel(ids_hbm, pos_hbm, out_ref, ids_ref, pos_ref, rows_ref, sems):
    fetch([(ids_hbm, ids_ref), (pos_hbm, pos_ref)], sems)
    hot, rank = expert_rank(ids_ref[...], SAMP)
    rows_ref[...] = jnp.zeros_like(rows_ref)
    points = pos_ref[...]
    for slot in range(CAP):
        rows_ref[4 * slot : 4 * slot + 3, :] = jnp.where(rank == float(slot), points, 0.0)
    hot = hot.astype(BF16)
    high, middle, low = split_three(rows_ref[...])
    out_ref[...] = dot_nt(hot, high) + (dot_nt(hot, middle) + dot_nt(hot, low))


def setup_kernel(
    ids_hbm,
    pos_hbm,
    space_hbm,
    length_hbm,
    target_hbm,
    owner_hbm,
    slot_hbm,
    freq_hbm,
    phase_hbm,
    first_hbm,
    second_hbm,
    head_hbm,
    after_hbm,
    wide_ref,
    ray_ref,
    wave_ref,
    hot_ref,
    member_ref,
    camera_ref,
    first_ref,
    second_ref,
    flipped_ref,
    head_out_ref,
    head_back_ref,
    ids_ref,
    pos_ref,
    space_ref,
    length_ref,
    target_ref,
    owner_ref,
    slot_ref,
    freq_ref,
    phase_ref,
    one_ref,
    two_ref,
    head_ref,
    sems,
):
    fetch(
        [
            (ids_hbm, ids_ref),
            (pos_hbm, pos_ref),
            (space_hbm, space_ref),
            (length_hbm, length_ref),
            (target_hbm, target_ref),
            (owner_hbm, owner_ref),
            (slot_hbm, slot_ref),
            (freq_hbm, freq_ref),
            (phase_hbm, phase_ref),
            (first_hbm, one_ref),
            (second_hbm, two_ref),
            (head_hbm, head_ref),
        ],
        sems,
    )
    first_ref[...] = one_ref[0]
    second_ref[...] = two_ref[0]
    flipped_ref[...] = jnp.transpose(two_ref[0].astype(F32)).astype(BF16)
    wave_ref[...] = jnp.zeros_like(wave_ref)
    wave_ref[0:3, :] = freq_ref[...]
    wave_ref[3:4, :] = phase_ref[...]
    row = iota((PEERS, 4), 0)
    column = iota((PEERS, 4), 1)
    head = head_ref[0]
    head_out_ref[...] = dot_nn(((row // 4) % 4 == column).astype(BF16), head).astype(BF16)
    head_back_ref[...] = dot_nn((row % 8 == column).astype(BF16), head).astype(BF16)

    wide_ref[...] = jnp.zeros_like(wide_ref)
    wide_ref[0:3, 0:SAMP] = pos_ref[...]
    wide_ref[3:4, 0:SAMP] = space_ref[...]
    wide_ref[4:5, :] = jnp.full((1, LANES), -1.0, F32)
    wide_ref[4:5, 0:SAMP] = ids_ref[...].astype(F32)
    ids = wide_ref[4:5, :].astype(jnp.int32)
    hot, rank = expert_rank(ids, LANES)
    hot_ref[...] = hot.astype(BF16)
    wide_ref[4:5, :] = rank

    lengths = length_ref[...].astype(F32)
    ray_a = iota((RAYS, RAYS), 0)
    ray_b = iota((RAYS, RAYS), 1)
    starts = jnp.sum(jnp.where(ray_b < ray_a, lengths, 0.0), axis=1, keepdims=True)
    ends = jnp.sum(jnp.where(ray_b <= ray_a, lengths, 0.0), axis=1, keepdims=True)
    index = iota((RAYS, LANES), 1).astype(F32)
    member = ((index >= starts) & (index < ends)).astype(BF16)
    member_ref[...] = member
    begin = jnp.sum((index == starts).astype(F32), axis=0, keepdims=True)
    near_one = 1.0 - begin
    near_two = near_one * pltpu.roll(near_one, 1, 1)
    near_three = near_two * pltpu.roll(near_one, 2, 1)
    wide_ref[5:6, :] = near_one
    wide_ref[6:7, :] = near_two
    wide_ref[7:8, :] = near_three
    targets = target_ref[...]
    high, middle, low = split_three(targets)
    wide_ref[8:11, :] = dot_nn(high, member) + (dot_nn(middle, member) + dot_nn(low, member))

    ray_ref[...] = jnp.zeros_like(ray_ref)
    ray_ref[0:3, 0:RAYS] = targets
    ray_ref[3:4, :] = jnp.full((1, PEERS), -1.0, F32)
    ray_ref[3:4, 0:RAYS] = owner_ref[...].astype(F32)
    owners = ray_ref[3:4, :].astype(jnp.int32)
    camera, camera_rank = expert_rank(owners, PEERS)
    camera_ref[...] = camera.astype(BF16)
    ray_ref[3:4, :] = camera_rank
    slots = slot_ref[...]
    ray_ref[4:5, 0:RAYS] = (slots // LOW).astype(F32)
    ray_ref[5:6, 0:RAYS] = (slots & (LOW - 1)).astype(F32)


def forward_kernel(points_ref, wave_ref, first_ref, second_ref, head_ref, out_ref):
    points = points_ref[...]
    freq = wave_ref[0:3, :]
    phase = wave_ref[3:4, :]
    first = first_ref[...]
    second = second_ref[...]
    head_all = head_ref[...]
    lane_row = iota((PEERS, HID), 0)
    total = None
    for slot in range(CAP):
        sine, cosine = sin_cos(angles_of(points, slot, freq, phase))
        stack = [sine.astype(BF16)] + [(cosine * freq[c : c + 1]).astype(BF16) for c in range(3)]
        one = [dot_nn(part, first) for part in stack]
        value, slope = silu_pair(one[0])
        hidden = [value.astype(BF16)] + [(one[k] * slope).astype(BF16) for k in range(1, 4)]
        two = [dot_nn(part, second) for part in hidden]
        value, slope = silu_pair(two[0])
        hidden = [value.astype(BF16)] + [(two[k] * slope).astype(BF16) for k in range(1, 4)]
        for k in range(4):
            keep = (lane_row // 16 == slot) & (lane_row % 4 == k)
            head = jnp.where(keep, head_all, jnp.zeros_like(head_all))
            term = dot_nt(hidden[k], head)
            total = term if total is None else total + term
    out_ref[...] = total


def device_kernel(
    fields_ref,
    wide_ref,
    ray_ref,
    hot_ref,
    member_ref,
    camera_ref,
    after_hbm,
    out_ref,
    token_ref,
    stack_ref,
    block_ref,
    samp_ref,
):
    token_ref[...] = jnp.zeros_like(token_ref)
    px = wide_ref[0:1, :]
    py = wide_ref[1:2, :]
    pz = wide_ref[2:3, :]
    spacing = wide_ref[3:4, :]
    rank = wide_ref[4:5, :]
    near_one = wide_ref[5:6, :]
    near_two = wide_ref[6:7, :]
    near_three = wide_ref[7:8, :]
    hot = hot_ref[...]
    member = member_ref[...]
    turned = jnp.transpose(fields_ref[...])[0 : 16 * CAP]
    high, middle, low = split_three(turned)
    gathered = dot_nn(high, hot) + (dot_nn(middle, hot) + dot_nn(low, hot))
    fields = jnp.where(rank == 0.0, gathered[0:16], 0.0)
    for slot in range(1, CAP):
        fields = jnp.where(rank == float(slot), gathered[16 * slot : 16 * slot + 16], fields)

    def preceding(value):
        return (
            pltpu.roll(value, 1, 1) * near_one
            + pltpu.roll(value, 2, 1) * near_two
            + pltpu.roll(value, 3, 1) * near_three
        )

    def following(value):
        return (
            pltpu.roll(value * near_one, LANES - 1, 1)
            + pltpu.roll(value * near_two, LANES - 2, 1)
            + pltpu.roll(value * near_three, LANES - 3, 1)
        )

    raw = [fields[4 * o : 4 * o + 1] for o in range(4)]
    moved = [[fields[4 * o + 1 + c : 4 * o + 2 + c] for c in range(3)] for o in range(4)]
    density = jnp.maximum(raw[0], 0.0) + jnp.log1p(jnp.exp(-jnp.abs(raw[0])))
    depth = density * spacing
    through = jnp.exp(-preceding(depth))
    fade = jnp.exp(-depth)
    weight = through * (1.0 - fade)
    depth_slope = spacing * jax.nn.sigmoid(raw[0])
    along = []
    for o in range(4):
        m0, m1, m2 = moved[o]
        along.append([m2 * py - m1 * pz, m0 * pz - m2 * px, m1 * px - m0 * py, m0, m1, m2])
    stack_ref[...] = jnp.zeros_like(stack_ref)
    samp_ref[...] = jnp.zeros_like(samp_ref)
    scale = 1.0 / float(RAYS * REPS)
    slope_zero = None
    slope_rest = []
    for c in range(3):
        tint = jax.nn.sigmoid(raw[1 + c])
        share = weight * tint
        later = following(share)
        sense_zero = (through * fade * tint - later) * depth_slope
        sense_own = share * (1.0 - tint)
        miss = share + preceding(share) + later - wide_ref[8 + c : 9 + c, :]
        part = miss * sense_zero
        slope_zero = part if slope_zero is None else slope_zero + part
        slope_rest.append(scale * miss * sense_own)
        for k in range(6):
            stack_ref[8 * c + k : 8 * c + k + 1, :] = (
                sense_zero * along[0][k] + sense_own * along[1 + c][k]
            )
        stack_ref[8 * c + 6 : 8 * c + 7, :] = share
    slopes = [scale * slope_zero] + slope_rest
    for slot in range(CAP):
        for o in range(4):
            samp_ref[SLOPE_LANE + 8 * slot + o : SLOPE_LANE + 8 * slot + o + 1, :] = jnp.where(
                rank == float(slot), slopes[o], 0.0
            )

    high, middle, low = split_three(stack_ref[...])
    rays = dot_nt(high, member) + (dot_nt(middle, member) + dot_nt(low, member))
    camera_rank = ray_ref[3:4, 0:RAYS]
    blocks = []
    row = iota((8, RAYS), 0)
    for c in range(3):
        block = rays[8 * c : 8 * c + 8]
        blocks.append(jnp.where(row == 6, block - ray_ref[c : c + 1, 0:RAYS], block))
    block_ref[...] = jnp.zeros_like(block_ref)
    for a in range(6):
        outer = blocks[0][a : a + 1] * blocks[0]
        outer = outer + blocks[1][a : a + 1] * blocks[1]
        outer = outer + blocks[2][a : a + 1] * blocks[2]
        for slot in range(CAPC):
            kept = jnp.where(camera_rank == float(slot), outer, 0.0)
            base = 48 * slot
            block_ref[base + 6 * a : base + 6 * a + 6, 0:RAYS] = kept[0:6]
            block_ref[base + FORCE_ROW + a : base + FORCE_ROW + a + 1, 0:RAYS] = kept[6:7]
    for slot in range(CAPC):
        base = 48 * slot + LABEL_ROW
        block_ref[base : base + 2, 0:RAYS] = jnp.where(
            camera_rank == float(slot), ray_ref[4:6, 0:RAYS], 0.0
        )
    message = dot_nt(camera_ref[...], block_ref[...].astype(BF16))
    out_ref[...] = message + dot_nt(hot, samp_ref[...].astype(BF16))


def relay_kernel(got_ref, after_hbm, out_ref):
    half = PEERS // 2
    for core in range(2):
        part = got_ref[pl.ds(core, half, stride=2), :].astype(BF16)
        for rep in range(REPS):
            row = (2 * rep + core) * half
            out_ref[row : row + half, :] = part


def hidden_kernel(
    points_ref,
    wave_ref,
    first_ref,
    second_ref,
    after_hbm,
    feature_ref,
    one_ref,
    two_ref,
    slope_one_ref,
    slope_two_ref,
):
    freq = wave_ref[0:3, :]
    phase = wave_ref[3:4, :]
    first = first_ref[...]
    second = second_ref[...]
    half = PEERS // 2
    for rep in range(REPS):
        points = jnp.concatenate(
            [points_ref[rep, pl.ds(core, half, stride=2), :] for core in range(2)], axis=0
        )
        for slot in range(CAP):
            row = (rep * CAP + slot) * PEERS
            sine, _ = sin_cos(angles_of(points, slot, freq, phase))
            feature = sine.astype(BF16)
            value_one, slope_one = silu_pair(dot_nn(feature, first))
            hidden_one = value_one.astype(BF16)
            value_two, slope_two = silu_pair(dot_nn(hidden_one, second))
            two_ref[row : row + PEERS, :] = value_two.astype(BF16)
            slope_one_ref[row : row + PEERS, :] = slope_one
            slope_two_ref[row : row + PEERS, :] = slope_two
            feature_ref[:, row : row + PEERS] = jnp.transpose(sine).astype(BF16)
            one_ref[:, row : row + PEERS] = jnp.transpose(value_one).astype(BF16)


def final_kernel(
    got_ref,
    feature_ref,
    one_ref,
    two_ref,
    slope_one_ref,
    slope_two_ref,
    flipped_ref,
    head_ref,
    grad_first_ref,
    grad_second_ref,
    grad_head_ref,
    normal_ref,
    force_ref,
    back_one_ref,
    back_two_ref,
    left_ref,
):
    wide_row = iota((PEERS, HID), 0)
    head_all = head_ref[...]
    heads = []
    for slot in range(CAP):
        keep = (wide_row >= SLOPE_LANE + 8 * slot) & (wide_row < SLOPE_LANE + 8 * slot + 8)
        heads.append(jnp.where(keep, head_all, jnp.zeros_like(head_all)))
    turned = []
    head_parts = [None] * CAP
    for rep in range(REPS):
        got = got_ref[rep * PEERS : (rep + 1) * PEERS, :]
        flipped = jnp.transpose(got.astype(F32))
        turned.append(flipped)
        slopes_flipped = flipped[SLOPE_LANE:PEERS].astype(BF16)
        for slot in range(CAP):
            row = (rep * CAP + slot) * PEERS
            back_two = dot_nn(got, heads[slot]) * slope_two_ref[row : row + PEERS, :]
            back_two_ref[row : row + PEERS, :] = back_two.astype(BF16)
            term = dot_nn(slopes_flipped, two_ref[row : row + PEERS, :])
            head_parts[slot] = term if head_parts[slot] is None else head_parts[slot] + term
    head_sum = jnp.zeros((4, HID), F32)
    for slot in range(CAP):
        head_sum = head_sum + head_parts[slot][8 * slot : 8 * slot + 4]
    grad_head_ref[0] = head_sum
    grad_second_ref[0] = dot_nn(one_ref[...], back_two_ref[...])
    back_one = dot_nn(back_two_ref[...], flipped_ref[...]) * slope_one_ref[...]
    back_one_ref[...] = back_one.astype(BF16)
    grad_first_ref[0] = dot_nn(feature_ref[...], back_one_ref[...])

    values = []
    group = []
    low_hot = []
    low_lane = iota((PEERS, LOW), 1).astype(F32)
    for rep in range(REPS):
        got = got_ref[rep * PEERS : (rep + 1) * PEERS, :].astype(F32)
        for slot in range(CAPC):
            base = 48 * slot
            label = base + LABEL_ROW
            values.append(turned[rep][base : base + 48])
            group.append(turned[rep][label : label + 1])
            low_hot.append((got[:, label + 1 : label + 2] == low_lane).astype(BF16))
    values = jnp.concatenate(values, axis=1)
    group = jnp.concatenate(group, axis=1)
    low_hot = jnp.concatenate(low_hot, axis=0)
    for block in range(CAM_DEV // LOW):
        left_ref[48 * block : 48 * block + 48, :] = jnp.where(
            group == float(block), values, 0.0
        ).astype(BF16)
    table = dot_nn(left_ref[...], low_hot)
    for block in range(CAM_DEV // LOW):
        base = 48 * block
        place = slice(block * LOW, (block + 1) * LOW)
        normal_ref[:, place] = table[base : base + 36]
        force_ref[:, place] = table[base + FORCE_ROW : base + FORCE_ROW + 6]


def call(kernel, out_shape, *args, hbm=(), scratch=(), cost=None, room=8):
    specs = [
        pl.BlockSpec(memory_space=pltpu.HBM if number in hbm else pltpu.VMEM)
        for number in range(len(args))
    ]
    estimate = cost and pl.CostEstimate(flops=cost, transcendentals=0, bytes_accessed=1 << 20)
    return pl.pallas_call(
        kernel,
        out_shape=out_shape,
        in_specs=specs,
        scratch_shapes=list(scratch),
        cost_estimate=estimate,
        compiler_params=pltpu.CompilerParams(vmem_limit_bytes=room * 1024 * 1024),
    )(*args)


def shape(*dims, dtype=F32):
    return jax.ShapeDtypeStruct(dims, dtype)


def exchange(value, axes="expert", groups=None):
    return lax.all_to_all(
        value, axes, split_axis=0, concat_axis=0, tiled=True, axis_index_groups=groups
    )


def per_device(
    positions,
    frequencies,
    phases,
    w_first,
    w_second,
    w_head,
    spacing,
    expert_ids,
    ray_lengths,
    target,
    cam_owner,
    cam_slot,
):
    ids_row = expert_ids.reshape(1, SAMP)
    square = shape(PEERS, PEERS)
    half = PEERS // 2
    outgoing = call(
        prep_kernel,
        square,
        ids_row,
        positions,
        hbm=(0, 1),
        scratch=[
            pltpu.VMEM((1, SAMP), jnp.int32),
            pltpu.VMEM((3, SAMP), F32),
            pltpu.VMEM((PEERS, SAMP), F32),
            pltpu.SemaphoreType.DMA((2,)),
        ],
    )
    points = exchange(outgoing)
    wide, ray, wave, hot, member, camera, first, second, second_t, head_out, head_back = call(
        setup_kernel,
        (
            shape(16, LANES),
            shape(8, PEERS),
            shape(8, HID),
            shape(PEERS, LANES, dtype=BF16),
            shape(RAYS, LANES, dtype=BF16),
            shape(PEERS, PEERS, dtype=BF16),
            shape(HID, HID, dtype=BF16),
            shape(HID, HID, dtype=BF16),
            shape(HID, HID, dtype=BF16),
            shape(PEERS, HID, dtype=BF16),
            shape(PEERS, HID, dtype=BF16),
        ),
        ids_row,
        positions,
        spacing.reshape(1, SAMP),
        ray_lengths,
        target,
        cam_owner.reshape(1, RAYS),
        cam_slot.reshape(1, RAYS),
        frequencies,
        phases.reshape(1, HID),
        w_first,
        w_second,
        w_head,
        outgoing,
        hbm=range(13),
        scratch=[
            pltpu.VMEM((1, SAMP), jnp.int32),
            pltpu.VMEM((3, SAMP), F32),
            pltpu.VMEM((1, SAMP), F32),
            pltpu.VMEM((1, RAYS), jnp.int32),
            pltpu.VMEM((3, RAYS), F32),
            pltpu.VMEM((1, RAYS), jnp.int32),
            pltpu.VMEM((1, RAYS), jnp.int32),
            pltpu.VMEM((3, HID), F32),
            pltpu.VMEM((1, HID), F32),
            pltpu.VMEM((1, HID, HID), BF16),
            pltpu.VMEM((1, HID, HID), BF16),
            pltpu.VMEM((1, 4, HID), BF16),
            pltpu.SemaphoreType.DMA((12,)),
        ],
        cost=1 << 31,
    )
    fields = call(forward_kernel, square, points, wave, first, second, head_out)
    all_points = lax.all_gather(points, "rep", axis=0, tiled=False)
    returned = exchange(fields)
    message, token = call(
        device_kernel,
        (square, shape(8, PEERS)),
        returned,
        wide,
        ray,
        hot,
        member,
        camera,
        all_points,
        hbm=(6,),
        scratch=[
            pltpu.VMEM((24, LANES), F32),
            pltpu.VMEM((PEERS, PEERS), F32),
            pltpu.VMEM((PEERS, LANES), F32),
        ],
    )
    rows = REPS * CAP * PEERS
    hidden = call(
        hidden_kernel,
        (
            shape(HID, rows, dtype=BF16),
            shape(HID, rows, dtype=BF16),
            shape(rows, HID, dtype=BF16),
            shape(rows, HID),
            shape(rows, HID),
        ),
        all_points,
        wave,
        first,
        second,
        token,
        hbm=(4,),
        cost=1 << 33,
        room=16,
    )
    same_core = [[2 * pair + core for pair in range(half)] for core in range(2)]
    arrived = exchange(message, groups=same_core)
    relayed = call(relay_kernel, shape(REPS * PEERS, PEERS, dtype=BF16), arrived, hidden[4], hbm=(1,))
    around = [
        [rep * PEERS + 2 * pair + core for rep in range(REPS) for core in range(2)]
        for pair in range(half)
    ]
    everything = exchange(relayed, ("rep", "expert"), around)
    return call(
        final_kernel,
        (
            shape(1, HID, HID),
            shape(1, HID, HID),
            shape(1, 4, HID),
            shape(36, CAM_DEV),
            shape(6, CAM_DEV),
        ),
        everything,
        *hidden,
        second_t,
        head_back,
        room=24,
        scratch=[
            pltpu.VMEM((rows, HID), BF16),
            pltpu.VMEM((rows, HID), BF16),
            pltpu.VMEM((48 * (CAM_DEV // LOW), REPS * CAPC * PEERS), BF16),
        ],
    )


def solution(mesh):
    in_specs = (
        P(None, ("rep", "expert")),
        P(),
        P(),
        P("expert", None, None),
        P("expert", None, None),
        P("expert", None, None),
        P(("rep", "expert")),
        P(("rep", "expert"), None),
        P(("rep", "expert"), None),
        P(None, ("rep", "expert")),
        P(("rep", "expert"), None),
        P(("rep", "expert")),
    )
    out_specs = (
        P("expert", None, None),
        P("expert", None, None),
        P("expert", None, None),
        P(None, "expert"),
        P(None, "expert"),
    )
    return jax.shard_map(
        per_device, mesh=mesh, in_specs=in_specs, out_specs=out_specs, check_vma=False
    )
```

```python
import jax
import jax.numpy as jnp
from jax import lax
from jax.experimental import pallas as pl
from jax.experimental.pallas import tpu as pltpu
from jax.sharding import PartitionSpec as P

HID = 256
PEERS = 128
REPS = 4
SAMP = 192
RAYS = 96
LANES = 256
CAP = 3
CAPC = 2
CAM_DEV = 8192
LOW = 256
SLOPE_LANE = 96
LABEL_ROW = 36
FORCE_ROW = 40

F32 = jnp.float32
BF16 = jnp.bfloat16


def iota(shape, axis):
    return lax.broadcasted_iota(jnp.int32, shape, axis)


def dot_nn(left, right):
    return jnp.dot(left, right, preferred_element_type=F32)


def dot_nt(left, right):
    return lax.dot_general(left, right, (((1,), (1,)), ((), ())), preferred_element_type=F32)


def dot_tn(left, right):
    return lax.dot_general(left, right, (((0,), (0,)), ((), ())), preferred_element_type=F32)


def split_three(value):
    high = value.astype(BF16)
    rest = value - high.astype(F32)
    middle = rest.astype(BF16)
    low = (rest - middle.astype(F32)).astype(BF16)
    return high, middle, low


def sin_cos(angle):
    turns = jnp.round(angle * 0.6366197723675814)
    rest = angle - turns * 1.5703125
    rest = rest - turns * 4.8375129699707031e-4
    rest = rest - turns * 7.549789954891882e-8
    square = rest * rest
    sine = rest + rest * square * (
        -1.6666654611e-1 + square * (8.3321608736e-3 - square * 1.9515295891e-4)
    )
    cosine = (
        1.0
        - 0.5 * square
        + square
        * square
        * (4.166664568298827e-2 + square * (-1.388731625493765e-3 + square * 2.443315711809948e-5))
    )
    quarter = turns.astype(jnp.int32)
    odd = (quarter & 1) == 1
    sin_value = jnp.where(odd, cosine, sine)
    cos_value = jnp.where(odd, sine, cosine)
    sin_value = jnp.where((quarter & 2) == 2, -sin_value, sin_value)
    cos_value = jnp.where(((quarter + 1) & 2) == 2, -cos_value, cos_value)
    return sin_value, cos_value


def angles_of(points, slot, freq, phase):
    base = 4 * slot
    angle = freq[0:1] * points[:, base : base + 1] + freq[1:2] * points[:, base + 1 : base + 2]
    return angle + freq[2:3] * points[:, base + 2 : base + 3] + phase


def silu_pair(value):
    sig = jax.nn.sigmoid(value)
    return value * sig, sig * (1.0 + value * (1.0 - sig))


def expert_rank(ids_row, width):
    hot = (iota((PEERS, width), 0) == ids_row).astype(F32)
    earlier = (iota((width, width), 0) < iota((width, width), 1)).astype(BF16)
    counts = dot_nn(hot.astype(BF16), earlier)
    rank = jnp.sum(counts * hot, axis=0, keepdims=True)
    return hot, rank


def fetch(pairs, sems):
    copies = [
        pltpu.make_async_copy(source, place, sems.at[number])
        for number, (source, place) in enumerate(pairs)
    ]
    for copy in copies:
        copy.start()
    for copy in copies:
        copy.wait()


def setup_kernel(
    ids_hbm,
    pos_hbm,
    space_hbm,
    length_hbm,
    target_hbm,
    owner_hbm,
    slot_hbm,
    freq_hbm,
    phase_hbm,
    first_hbm,
    second_hbm,
    head_hbm,
    outgoing_ref,
    wide_ref,
    ray_ref,
    wave_ref,
    hot_ref,
    member_ref,
    camera_ref,
    first_ref,
    second_ref,
    head_out_ref,
    ids_ref,
    pos_ref,
    space_ref,
    length_ref,
    target_ref,
    owner_ref,
    slot_ref,
    freq_ref,
    phase_ref,
    one_ref,
    two_ref,
    head_ref,
    rows_ref,
    sems,
):
    fetch(
        [
            (ids_hbm, ids_ref),
            (pos_hbm, pos_ref),
            (space_hbm, space_ref),
            (length_hbm, length_ref),
            (target_hbm, target_ref),
            (owner_hbm, owner_ref),
            (slot_hbm, slot_ref),
            (freq_hbm, freq_ref),
            (phase_hbm, phase_ref),
            (first_hbm, one_ref),
            (second_hbm, two_ref),
            (head_hbm, head_ref),
        ],
        sems,
    )
    first_ref[...] = one_ref[0]
    second_ref[...] = two_ref[0]
    wave_ref[...] = jnp.zeros_like(wave_ref)
    wave_ref[0:3, :] = freq_ref[...]
    wave_ref[3:4, :] = phase_ref[...]
    row = iota((PEERS, 4), 0)
    column = iota((PEERS, 4), 1)
    head = head_ref[0]
    head_out_ref[...] = dot_nn(((row // 4) % 4 == column).astype(BF16), head).astype(BF16)

    wide_ref[...] = jnp.zeros_like(wide_ref)
    wide_ref[0:3, 0:SAMP] = pos_ref[...]
    wide_ref[3:4, 0:SAMP] = space_ref[...]
    wide_ref[4:5, :] = jnp.full((1, LANES), -1.0, F32)
    wide_ref[4:5, 0:SAMP] = ids_ref[...].astype(F32)
    ids = wide_ref[4:5, :].astype(jnp.int32)
    hot, rank = expert_rank(ids, LANES)
    hot = hot.astype(BF16)
    hot_ref[...] = hot
    wide_ref[4:5, :] = rank
    rows_ref[...] = jnp.zeros_like(rows_ref)
    points = wide_ref[0:3, :]
    for slot in range(CAP):
        rows_ref[4 * slot : 4 * slot + 3, :] = jnp.where(rank == float(slot), points, 0.0)
    high, middle, low = split_three(rows_ref[...])
    outgoing_ref[...] = dot_nt(hot, high) + (dot_nt(hot, middle) + dot_nt(hot, low))

    lengths = length_ref[...].astype(F32)
    ray_a = iota((RAYS, RAYS), 0)
    ray_b = iota((RAYS, RAYS), 1)
    starts = jnp.sum(jnp.where(ray_b < ray_a, lengths, 0.0), axis=1, keepdims=True)
    ends = jnp.sum(jnp.where(ray_b <= ray_a, lengths, 0.0), axis=1, keepdims=True)
    index = iota((RAYS, LANES), 1).astype(F32)
    member = ((index >= starts) & (index < ends)).astype(BF16)
    member_ref[...] = member
    begin = jnp.sum((index == starts).astype(F32), axis=0, keepdims=True)
    near_one = 1.0 - begin
    near_two = near_one * pltpu.roll(near_one, 1, 1)
    near_three = near_two * pltpu.roll(near_one, 2, 1)
    wide_ref[5:6, :] = near_one
    wide_ref[6:7, :] = near_two
    wide_ref[7:8, :] = near_three
    targets = target_ref[...]
    high, middle, low = split_three(targets)
    wide_ref[8:11, :] = dot_nn(high, member) + (dot_nn(middle, member) + dot_nn(low, member))

    ray_ref[...] = jnp.zeros_like(ray_ref)
    ray_ref[0:3, 0:RAYS] = targets
    ray_ref[3:4, :] = jnp.full((1, PEERS), -1.0, F32)
    ray_ref[3:4, 0:RAYS] = owner_ref[...].astype(F32)
    owners = ray_ref[3:4, :].astype(jnp.int32)
    camera, camera_rank = expert_rank(owners, PEERS)
    camera_ref[...] = camera.astype(BF16)
    ray_ref[3:4, :] = camera_rank
    slots = slot_ref[...]
    ray_ref[4:5, 0:RAYS] = (slots // LOW).astype(F32)
    ray_ref[5:6, 0:RAYS] = (slots & (LOW - 1)).astype(F32)


def forward_kernel(points_ref, wave_ref, first_ref, second_ref, head_ref, out_ref):
    points = points_ref[...]
    freq = wave_ref[0:3, :]
    phase = wave_ref[3:4, :]
    first = first_ref[...]
    second = second_ref[...]
    head_all = head_ref[...]
    lane_row = iota((PEERS, HID), 0)
    total = None
    for slot in range(CAP):
        sine, cosine = sin_cos(angles_of(points, slot, freq, phase))
        stack = [sine.astype(BF16)] + [(cosine * freq[c : c + 1]).astype(BF16) for c in range(3)]
        one = [dot_nn(part, first) for part in stack]
        value, slope = silu_pair(one[0])
        hidden = [value.astype(BF16)] + [(one[k] * slope).astype(BF16) for k in range(1, 4)]
        two = [dot_nn(part, second) for part in hidden]
        value, slope = silu_pair(two[0])
        hidden = [value.astype(BF16)] + [(two[k] * slope).astype(BF16) for k in range(1, 4)]
        for k in range(4):
            keep = (lane_row // 16 == slot) & (lane_row % 4 == k)
            head = jnp.where(keep, head_all, jnp.zeros_like(head_all))
            term = dot_nt(hidden[k], head)
            total = term if total is None else total + term
    out_ref[...] = total


def device_kernel(
    fields_ref,
    wide_ref,
    ray_ref,
    hot_ref,
    member_ref,
    camera_ref,
    after_hbm,
    out_ref,
    stack_ref,
    block_ref,
    samp_ref,
):
    px = wide_ref[0:1, :]
    py = wide_ref[1:2, :]
    pz = wide_ref[2:3, :]
    spacing = wide_ref[3:4, :]
    rank = wide_ref[4:5, :]
    near_one = wide_ref[5:6, :]
    near_two = wide_ref[6:7, :]
    near_three = wide_ref[7:8, :]
    hot = hot_ref[...]
    member = member_ref[...]
    turned = jnp.transpose(fields_ref[...])[0 : 16 * CAP]
    high, middle, low = split_three(turned)
    gathered = dot_nn(high, hot) + (dot_nn(middle, hot) + dot_nn(low, hot))
    fields = jnp.where(rank == 0.0, gathered[0:16], 0.0)
    for slot in range(1, CAP):
        fields = jnp.where(rank == float(slot), gathered[16 * slot : 16 * slot + 16], fields)

    def preceding(value):
        return (
            pltpu.roll(value, 1, 1) * near_one
            + pltpu.roll(value, 2, 1) * near_two
            + pltpu.roll(value, 3, 1) * near_three
        )

    def following(value):
        return (
            pltpu.roll(value * near_one, LANES - 1, 1)
            + pltpu.roll(value * near_two, LANES - 2, 1)
            + pltpu.roll(value * near_three, LANES - 3, 1)
        )

    raw = [fields[4 * o : 4 * o + 1] for o in range(4)]
    moved = [[fields[4 * o + 1 + c : 4 * o + 2 + c] for c in range(3)] for o in range(4)]
    density = jnp.maximum(raw[0], 0.0) + jnp.log1p(jnp.exp(-jnp.abs(raw[0])))
    depth = density * spacing
    through = jnp.exp(-preceding(depth))
    fade = jnp.exp(-depth)
    weight = through * (1.0 - fade)
    depth_slope = spacing * jax.nn.sigmoid(raw[0])
    along = []
    for o in range(4):
        m0, m1, m2 = moved[o]
        along.append([m2 * py - m1 * pz, m0 * pz - m2 * px, m1 * px - m0 * py, m0, m1, m2])
    stack_ref[...] = jnp.zeros_like(stack_ref)
    samp_ref[...] = jnp.zeros_like(samp_ref)
    scale = 1.0 / float(RAYS * REPS)
    slope_zero = None
    slope_rest = []
    for c in range(3):
        tint = jax.nn.sigmoid(raw[1 + c])
        share = weight * tint
        later = following(share)
        sense_zero = (through * fade * tint - later) * depth_slope
        sense_own = share * (1.0 - tint)
        miss = share + preceding(share) + later - wide_ref[8 + c : 9 + c, :]
        part = miss * sense_zero
        slope_zero = part if slope_zero is None else slope_zero + part
        slope_rest.append(scale * miss * sense_own)
        for k in range(6):
            stack_ref[8 * c + k : 8 * c + k + 1, :] = (
                sense_zero * along[0][k] + sense_own * along[1 + c][k]
            )
        stack_ref[8 * c + 6 : 8 * c + 7, :] = share
    slopes = [scale * slope_zero] + slope_rest
    for slot in range(CAP):
        for o in range(4):
            samp_ref[SLOPE_LANE + 8 * slot + o : SLOPE_LANE + 8 * slot + o + 1, :] = jnp.where(
                rank == float(slot), slopes[o], 0.0
            )

    high, middle, low = split_three(stack_ref[...])
    rays = dot_nt(high, member) + (dot_nt(middle, member) + dot_nt(low, member))
    camera_rank = ray_ref[3:4, 0:RAYS]
    blocks = []
    row = iota((8, RAYS), 0)
    for c in range(3):
        block = rays[8 * c : 8 * c + 8]
        blocks.append(jnp.where(row == 6, block - ray_ref[c : c + 1, 0:RAYS], block))
    block_ref[...] = jnp.zeros_like(block_ref)
    for a in range(6):
        outer = blocks[0][a : a + 1] * blocks[0]
        outer = outer + blocks[1][a : a + 1] * blocks[1]
        outer = outer + blocks[2][a : a + 1] * blocks[2]
        for slot in range(CAPC):
            kept = jnp.where(camera_rank == float(slot), outer, 0.0)
            base = 48 * slot
            block_ref[base + 6 * a : base + 6 * a + 6, 0:RAYS] = kept[0:6]
            block_ref[base + FORCE_ROW + a : base + FORCE_ROW + a + 1, 0:RAYS] = kept[6:7]
    for slot in range(CAPC):
        base = 48 * slot + LABEL_ROW
        block_ref[base : base + 2, 0:RAYS] = jnp.where(
            camera_rank == float(slot), ray_ref[4:6, 0:RAYS], 0.0
        )
    message = dot_nt(camera_ref[...], block_ref[...].astype(BF16))
    out_ref[...] = message + dot_nt(hot, samp_ref[...].astype(BF16))


def relay_kernel(got_ref, out_ref, token_ref):
    token_ref[...] = jnp.zeros_like(token_ref)
    half = PEERS // 2
    for core in range(2):
        part = got_ref[pl.ds(core, half, stride=2), :].astype(BF16)
        for rep in range(REPS):
            row = (2 * rep + core) * half
            out_ref[row : row + half, :] = part


def hidden_kernel(
    points_ref,
    wave_ref,
    first_ref,
    second_ref,
    after_ref,
    feature_hbm,
    one_hbm,
    two_hbm,
    slope_one_hbm,
    slope_two_hbm,
    feature_ref,
    one_ref,
    two_ref,
    slope_one_ref,
    slope_two_ref,
    sems,
):
    freq = wave_ref[0:3, :]
    phase = wave_ref[3:4, :]
    first = first_ref[...]
    second = second_ref[...]
    half = PEERS // 2
    copies = []
    for rep in range(REPS):
        points = jnp.concatenate(
            [points_ref[rep, pl.ds(core, half, stride=2), :] for core in range(2)], axis=0
        )
        for slot in range(CAP):
            row = (rep * CAP + slot) * PEERS
            sine, _ = sin_cos(angles_of(points, slot, freq, phase))
            feature = sine.astype(BF16)
            value_one, slope_one = silu_pair(dot_nn(feature, first))
            hidden_one = value_one.astype(BF16)
            value_two, slope_two = silu_pair(dot_nn(hidden_one, second))
            two_ref[row : row + PEERS, :] = value_two.astype(BF16)
            slope_one_ref[row : row + PEERS, :] = slope_one
            slope_two_ref[row : row + PEERS, :] = slope_two
            feature_ref[:, row : row + PEERS] = jnp.transpose(sine).astype(BF16)
            one_ref[:, row : row + PEERS] = jnp.transpose(value_one).astype(BF16)
        part = pl.ds(rep * CAP * PEERS, CAP * PEERS)
        for number, (source, place) in enumerate(
            [
                (feature_ref.at[:, part], feature_hbm.at[:, part]),
                (one_ref.at[:, part], one_hbm.at[:, part]),
                (two_ref.at[part, :], two_hbm.at[part, :]),
                (slope_one_ref.at[part, :], slope_one_hbm.at[part, :]),
                (slope_two_ref.at[part, :], slope_two_hbm.at[part, :]),
            ]
        ):
            copy = pltpu.make_async_copy(source, place, sems.at[5 * rep + number])
            copy.start()
            copies.append(copy)
    for copy in copies:
        copy.wait()


def final_kernel(
    got_ref,
    feature_hbm,
    one_hbm,
    two_hbm,
    slope_one_hbm,
    slope_two_hbm,
    second_hbm,
    head_hbm,
    grad_first_hbm,
    grad_second_hbm,
    grad_head_hbm,
    normal_hbm,
    force_hbm,
    feature_ref,
    one_ref,
    two_ref,
    slope_one_ref,
    slope_two_ref,
    second_ref,
    head_ref,
    grad_first_ref,
    grad_second_ref,
    grad_head_ref,
    normal_ref,
    force_ref,
    back_one_ref,
    back_two_ref,
    left_ref,
    sems,
):
    head_in, two_in, slope_two_in, one_in, second_in, slope_one_in, feature_in = [
        pltpu.make_async_copy(source, place, sems.at[number])
        for number, (source, place) in enumerate(
            [
                (head_hbm, head_ref),
                (two_hbm, two_ref),
                (slope_two_hbm, slope_two_ref),
                (one_hbm, one_ref),
                (second_hbm, second_ref),
                (slope_one_hbm, slope_one_ref),
                (feature_hbm, feature_ref),
            ]
        )
    ]
    for copy in (head_in, two_in, slope_two_in, one_in, second_in, slope_one_in, feature_in):
        copy.start()
    first_out, second_out, head_out, normal_out, force_out = [
        pltpu.make_async_copy(source, place, sems.at[7 + number])
        for number, (source, place) in enumerate(
            [
                (grad_first_ref, grad_first_hbm),
                (grad_second_ref, grad_second_hbm),
                (grad_head_ref, grad_head_hbm),
                (normal_ref, normal_hbm),
                (force_ref, force_hbm),
            ]
        )
    ]

    values = []
    group = []
    low_hot = []
    turned = []
    low_lane = iota((PEERS, LOW), 1).astype(F32)
    for rep in range(REPS):
        got = got_ref[rep * PEERS : (rep + 1) * PEERS, :].astype(F32)
        flipped = jnp.transpose(got)
        turned.append(flipped)
        for slot in range(CAPC):
            base = 48 * slot
            label = base + LABEL_ROW
            values.append(flipped[base : base + 48])
            group.append(flipped[label : label + 1])
            low_hot.append((got[:, label + 1 : label + 2] == low_lane).astype(BF16))
    values = jnp.concatenate(values, axis=1)
    group = jnp.concatenate(group, axis=1)
    low_hot = jnp.concatenate(low_hot, axis=0)
    for block in range(CAM_DEV // LOW):
        left_ref[48 * block : 48 * block + 48, :] = jnp.where(
            group == float(block), values, 0.0
        ).astype(BF16)
    table = dot_nn(left_ref[...], low_hot)
    for block in range(CAM_DEV // LOW):
        base = 48 * block
        place = slice(block * LOW, (block + 1) * LOW)
        normal_ref[:, place] = table[base : base + 36]
        force_ref[:, place] = table[base + FORCE_ROW : base + FORCE_ROW + 6]
    normal_out.start()
    force_out.start()

    head_in.wait()
    two_in.wait()
    slope_two_in.wait()
    wide_row = iota((PEERS, HID), 0)
    row = iota((PEERS, 4), 0)
    column = iota((PEERS, 4), 1)
    head_all = dot_nn((row % 8 == column).astype(BF16), head_ref[0]).astype(BF16)
    heads = []
    for slot in range(CAP):
        keep = (wide_row >= SLOPE_LANE + 8 * slot) & (wide_row < SLOPE_LANE + 8 * slot + 8)
        heads.append(jnp.where(keep, head_all, jnp.zeros_like(head_all)))
    head_parts = [None] * CAP
    for rep in range(REPS):
        got = got_ref[rep * PEERS : (rep + 1) * PEERS, :]
        slopes_flipped = turned[rep][SLOPE_LANE:PEERS].astype(BF16)
        for slot in range(CAP):
            row = (rep * CAP + slot) * PEERS
            back_two = dot_nn(got, heads[slot]) * slope_two_ref[row : row + PEERS, :]
            back_two_ref[row : row + PEERS, :] = back_two.astype(BF16)
            term = dot_nn(slopes_flipped, two_ref[row : row + PEERS, :])
            head_parts[slot] = term if head_parts[slot] is None else head_parts[slot] + term
    head_sum = jnp.zeros((4, HID), F32)
    for slot in range(CAP):
        head_sum = head_sum + head_parts[slot][8 * slot : 8 * slot + 4]
    grad_head_ref[0] = head_sum
    head_out.start()
    one_in.wait()
    grad_second_ref[0] = dot_nn(one_ref[...], back_two_ref[...])
    second_out.start()
    second_in.wait()
    slope_one_in.wait()
    back_one = dot_nt(back_two_ref[...], second_ref[0]) * slope_one_ref[...]
    back_one_ref[...] = back_one.astype(BF16)
    feature_in.wait()
    grad_first_ref[0] = dot_nn(feature_ref[...], back_one_ref[...])
    first_out.start()
    for copy in (normal_out, force_out, head_out, second_out, first_out):
        copy.wait()


def call(kernel, out_shape, *args, hbm=(), unread=(), hbm_out=False, scratch=(), cost=None, room=8):
    def spec(number):
        if number in unread:
            return pl.BlockSpec(memory_space=pl.ANY)
        return pl.BlockSpec(memory_space=pltpu.HBM if number in hbm else pltpu.VMEM)

    place = pltpu.HBM if hbm_out else pltpu.VMEM
    estimate = cost and pl.CostEstimate(flops=cost, transcendentals=0, bytes_accessed=1 << 20)
    args = [
        pltpu.with_memory_space_constraint(arg, pltpu.HBM) if number in hbm else arg
        for number, arg in enumerate(args)
    ]
    return pl.pallas_call(
        kernel,
        out_shape=out_shape,
        in_specs=[spec(number) for number in range(len(args))],
        out_specs=jax.tree.map(lambda _: pl.BlockSpec(memory_space=place), out_shape),
        scratch_shapes=list(scratch),
        cost_estimate=estimate,
        compiler_params=pltpu.CompilerParams(vmem_limit_bytes=room * 1024 * 1024),
    )(*args)


def shape(*dims, dtype=F32):
    return jax.ShapeDtypeStruct(dims, dtype)


def exchange(value, axes="expert", groups=None):
    return lax.all_to_all(
        value, axes, split_axis=0, concat_axis=0, tiled=True, axis_index_groups=groups
    )


def per_device(
    positions,
    frequencies,
    phases,
    w_first,
    w_second,
    w_head,
    spacing,
    expert_ids,
    ray_lengths,
    target,
    cam_owner,
    cam_slot,
):
    ids_row = expert_ids.reshape(1, SAMP)
    square = shape(PEERS, PEERS)
    half = PEERS // 2
    outgoing, wide, ray, wave, hot, member, camera, *rest = call(
        setup_kernel,
        (
            square,
            pltpu.VMEM((16, LANES), F32),
            pltpu.VMEM((8, PEERS), F32),
            pltpu.VMEM((8, HID), F32),
            pltpu.VMEM((PEERS, LANES), BF16),
            pltpu.VMEM((RAYS, LANES), BF16),
            pltpu.VMEM((PEERS, PEERS), BF16),
            pltpu.VMEM((HID, HID), BF16),
            pltpu.VMEM((HID, HID), BF16),
            pltpu.VMEM((PEERS, HID), BF16),
        ),
        ids_row,
        positions,
        spacing.reshape(1, SAMP),
        ray_lengths,
        target,
        cam_owner.reshape(1, RAYS),
        cam_slot.reshape(1, RAYS),
        frequencies,
        phases.reshape(1, HID),
        w_first,
        w_second,
        w_head,
        hbm=range(12),
        scratch=[
            pltpu.VMEM((1, SAMP), jnp.int32),
            pltpu.VMEM((3, SAMP), F32),
            pltpu.VMEM((1, SAMP), F32),
            pltpu.VMEM((1, RAYS), jnp.int32),
            pltpu.VMEM((3, RAYS), F32),
            pltpu.VMEM((1, RAYS), jnp.int32),
            pltpu.VMEM((1, RAYS), jnp.int32),
            pltpu.VMEM((3, HID), F32),
            pltpu.VMEM((1, HID), F32),
            pltpu.VMEM((1, HID, HID), BF16),
            pltpu.VMEM((1, HID, HID), BF16),
            pltpu.VMEM((1, 4, HID), BF16),
            pltpu.VMEM((PEERS, LANES), F32),
            pltpu.SemaphoreType.DMA((12,)),
        ],
    )
    first, second, head_out = rest
    points = exchange(outgoing)
    fields = call(forward_kernel, square, points, wave, first, second, head_out)
    all_points = lax.all_gather(points, "rep", axis=0, tiled=False)
    returned = exchange(fields)
    message = call(
        device_kernel,
        square,
        returned,
        wide,
        ray,
        hot,
        member,
        camera,
        all_points,
        unread=(6,),
        scratch=[
            pltpu.VMEM((24, LANES), F32),
            pltpu.VMEM((PEERS, PEERS), F32),
            pltpu.VMEM((PEERS, LANES), F32),
        ],
    )
    same_core = [[2 * pair + core for pair in range(half)] for core in range(2)]
    arrived = exchange(message, groups=same_core)
    relayed, token = call(
        relay_kernel, (shape(REPS * PEERS, PEERS, dtype=BF16), shape(8, PEERS)), arrived
    )
    around = [
        [rep * PEERS + 2 * pair + core for rep in range(REPS) for core in range(2)]
        for pair in range(half)
    ]
    rows = REPS * CAP * PEERS
    kept = [((HID, rows), BF16)] * 2 + [((rows, HID), BF16)] + [((rows, HID), F32)] * 2
    kept_shapes = tuple(pltpu.HBM(dims, kind) for dims, kind in kept)
    kept_room = [pltpu.VMEM(dims, kind) for dims, kind in kept]
    hidden = call(
        hidden_kernel,
        kept_shapes,
        all_points,
        wave,
        first,
        second,
        token,
        unread=(4,),
        hbm_out=True,
        scratch=[*kept_room, pltpu.SemaphoreType.DMA((5 * REPS,))],
        cost=1 << 33,
        room=16,
    )
    everything = exchange(relayed, ("rep", "expert"), around)
    return call(
        final_kernel,
        (
            shape(1, HID, HID),
            shape(1, HID, HID),
            shape(1, 4, HID),
            shape(36, CAM_DEV),
            shape(6, CAM_DEV),
        ),
        everything,
        *hidden,
        w_second,
        w_head,
        hbm=range(1, 8),
        hbm_out=True,
        room=32,
        scratch=[
            *kept_room,
            pltpu.VMEM((1, HID, HID), BF16),
            pltpu.VMEM((1, 4, HID), BF16),
            pltpu.VMEM((1, HID, HID), F32),
            pltpu.VMEM((1, HID, HID), F32),
            pltpu.VMEM((1, 4, HID), F32),
            pltpu.VMEM((36, CAM_DEV), F32),
            pltpu.VMEM((6, CAM_DEV), F32),
            pltpu.VMEM((rows, HID), BF16),
            pltpu.VMEM((rows, HID), BF16),
            pltpu.VMEM((48 * (CAM_DEV // LOW), REPS * CAPC * PEERS), BF16),
            pltpu.SemaphoreType.DMA((12,)),
        ],
    )


def solution(mesh):
    in_specs = (
        P(None, ("rep", "expert")),
        P(),
        P(),
        P("expert", None, None),
        P("expert", None, None),
        P("expert", None, None),
        P(("rep", "expert")),
        P(("rep", "expert"), None),
        P(("rep", "expert"), None),
        P(None, ("rep", "expert")),
        P(("rep", "expert"), None),
        P(("rep", "expert")),
    )
    out_specs = (
        P("expert", None, None),
        P("expert", None, None),
        P("expert", None, None),
        P(None, "expert"),
        P(None, "expert"),
    )
    return jax.shard_map(
        per_device, mesh=mesh, in_specs=in_specs, out_specs=out_specs, check_vma=False
    )
```

```python
import jax
import jax.numpy as jnp
from jax import lax
from jax.experimental import pallas as pl
from jax.experimental.pallas import tpu as pltpu
from jax.sharding import PartitionSpec as P

HID = 256
PEERS = 128
REPS = 4
HALF = PEERS // 2
SAMP = 192
RAYS = 96
LANES = 256
CAP = 3
CAPC = 2
CAM_DEV = 8192
LOW = 256
SLOPE_LANE = 96
LABEL_ROW = 36
FORCE_ROW = 40
CORE_LANE = 15

F32 = jnp.float32
BF16 = jnp.bfloat16


def iota(shape, axis):
    return lax.broadcasted_iota(jnp.int32, shape, axis)


def dot_nn(left, right):
    return jnp.dot(left, right, preferred_element_type=F32)


def dot_nt(left, right):
    return lax.dot_general(left, right, (((1,), (1,)), ((), ())), preferred_element_type=F32)


def dot_tn(left, right):
    return lax.dot_general(left, right, (((0,), (0,)), ((), ())), preferred_element_type=F32)


def split_three(value):
    high = value.astype(BF16)
    rest = value - high.astype(F32)
    middle = rest.astype(BF16)
    low = (rest - middle.astype(F32)).astype(BF16)
    return high, middle, low


def sin_cos(angle):
    turns = jnp.round(angle * 0.6366197723675814)
    rest = angle - turns * 1.5703125
    rest = rest - turns * 4.8375129699707031e-4
    rest = rest - turns * 7.549789954891882e-8
    square = rest * rest
    sine = rest + rest * square * (
        -1.6666654611e-1 + square * (8.3321608736e-3 - square * 1.9515295891e-4)
    )
    cosine = (
        1.0
        - 0.5 * square
        + square
        * square
        * (4.166664568298827e-2 + square * (-1.388731625493765e-3 + square * 2.443315711809948e-5))
    )
    quarter = turns.astype(jnp.int32)
    odd = (quarter & 1) == 1
    sin_value = jnp.where(odd, cosine, sine)
    cos_value = jnp.where(odd, sine, cosine)
    sin_value = jnp.where((quarter & 2) == 2, -sin_value, sin_value)
    cos_value = jnp.where(((quarter + 1) & 2) == 2, -cos_value, cos_value)
    return sin_value, cos_value


def angles_of(points, slot, freq, phase):
    base = 4 * slot
    angle = freq[0:1] * points[:, base : base + 1] + freq[1:2] * points[:, base + 1 : base + 2]
    return angle + freq[2:3] * points[:, base + 2 : base + 3] + phase


def silu_pair(value):
    sig = jax.nn.sigmoid(value)
    return value * sig, sig * (1.0 + value * (1.0 - sig))


def expert_rank(ids_row, width):
    hot = (iota((PEERS, width), 0) == ids_row).astype(F32)
    earlier = (iota((width, width), 0) < iota((width, width), 1)).astype(BF16)
    counts = dot_nn(hot.astype(BF16), earlier)
    rank = jnp.sum(counts * hot, axis=0, keepdims=True)
    return hot, rank


def fetch(pairs, sems):
    copies = [
        pltpu.make_async_copy(source, place, sems.at[number])
        for number, (source, place) in enumerate(pairs)
    ]
    for copy in copies:
        copy.start()
    for copy in copies:
        copy.wait()


def setup_kernel(
    ids_hbm,
    pos_hbm,
    space_hbm,
    length_hbm,
    target_hbm,
    owner_hbm,
    slot_hbm,
    freq_hbm,
    phase_hbm,
    first_hbm,
    second_hbm,
    head_hbm,
    outgoing_ref,
    wide_ref,
    ray_ref,
    wave_ref,
    hot_ref,
    member_ref,
    camera_ref,
    first_ref,
    second_ref,
    head_out_ref,
    head_back_ref,
    ids_ref,
    pos_ref,
    space_ref,
    length_ref,
    target_ref,
    owner_ref,
    slot_ref,
    freq_ref,
    phase_ref,
    one_ref,
    two_ref,
    head_ref,
    rows_ref,
    sems,
):
    fetch(
        [
            (ids_hbm, ids_ref),
            (pos_hbm, pos_ref),
            (space_hbm, space_ref),
            (length_hbm, length_ref),
            (target_hbm, target_ref),
            (owner_hbm, owner_ref),
            (slot_hbm, slot_ref),
            (freq_hbm, freq_ref),
            (phase_hbm, phase_ref),
            (first_hbm, one_ref),
            (second_hbm, two_ref),
            (head_hbm, head_ref),
        ],
        sems,
    )
    first_ref[...] = one_ref[0]
    second_ref[...] = two_ref[0]
    wave_ref[...] = jnp.zeros_like(wave_ref)
    wave_ref[0:3, :] = freq_ref[...]
    wave_ref[3:4, :] = phase_ref[...]
    row = iota((PEERS, 4), 0)
    column = iota((PEERS, 4), 1)
    head = head_ref[0]
    head_out_ref[...] = dot_nn(((row // 4) % 4 == column).astype(BF16), head).astype(BF16)
    head_back_ref[...] = dot_nn((row % 8 == column).astype(BF16), head).astype(BF16)

    wide_ref[...] = jnp.zeros_like(wide_ref)
    wide_ref[0:3, 0:SAMP] = pos_ref[...]
    wide_ref[3:4, 0:SAMP] = space_ref[...]
    wide_ref[4:5, :] = jnp.full((1, LANES), -1.0, F32)
    wide_ref[4:5, 0:SAMP] = ids_ref[...].astype(F32)
    ids = wide_ref[4:5, :].astype(jnp.int32)
    hot, rank = expert_rank(ids, LANES)
    hot = hot.astype(BF16)
    hot_ref[...] = hot
    wide_ref[4:5, :] = rank
    rows_ref[...] = jnp.zeros_like(rows_ref)
    points = wide_ref[0:3, :]
    for slot in range(CAP):
        rows_ref[4 * slot : 4 * slot + 3, :] = jnp.where(rank == float(slot), points, 0.0)
    high, middle, low = split_three(rows_ref[...])
    place = iota((PEERS, PEERS), 1)
    core = (iota((PEERS, PEERS), 0) & 1).astype(F32)
    message = dot_nt(hot, high) + (dot_nt(hot, middle) + dot_nt(hot, low))
    outgoing_ref[...] = jnp.where(place == CORE_LANE, core, message)

    lengths = length_ref[...].astype(F32)
    ray_a = iota((RAYS, RAYS), 0)
    ray_b = iota((RAYS, RAYS), 1)
    starts = jnp.sum(jnp.where(ray_b < ray_a, lengths, 0.0), axis=1, keepdims=True)
    ends = jnp.sum(jnp.where(ray_b <= ray_a, lengths, 0.0), axis=1, keepdims=True)
    index = iota((RAYS, LANES), 1).astype(F32)
    member = ((index >= starts) & (index < ends)).astype(BF16)
    member_ref[...] = member
    begin = jnp.sum((index == starts).astype(F32), axis=0, keepdims=True)
    near_one = 1.0 - begin
    near_two = near_one * pltpu.roll(near_one, 1, 1)
    near_three = near_two * pltpu.roll(near_one, 2, 1)
    wide_ref[5:6, :] = near_one
    wide_ref[6:7, :] = near_two
    wide_ref[7:8, :] = near_three
    targets = target_ref[...]
    high, middle, low = split_three(targets)
    wide_ref[8:11, :] = dot_nn(high, member) + (dot_nn(middle, member) + dot_nn(low, member))

    ray_ref[...] = jnp.zeros_like(ray_ref)
    ray_ref[0:3, 0:RAYS] = targets
    ray_ref[3:4, :] = jnp.full((1, PEERS), -1.0, F32)
    ray_ref[3:4, 0:RAYS] = owner_ref[...].astype(F32)
    owners = ray_ref[3:4, :].astype(jnp.int32)
    camera, camera_rank = expert_rank(owners, PEERS)
    camera_ref[...] = camera.astype(BF16)
    ray_ref[3:4, :] = camera_rank
    slots = slot_ref[...]
    ray_ref[4:5, 0:RAYS] = (slots // LOW).astype(F32)
    ray_ref[5:6, 0:RAYS] = (slots & (LOW - 1)).astype(F32)


def forward_kernel(points_ref, wave_ref, first_ref, second_ref, head_ref, out_ref):
    points = points_ref[...]
    freq = wave_ref[0:3, :]
    phase = wave_ref[3:4, :]
    first = first_ref[...]
    second = second_ref[...]
    head_all = head_ref[...]
    lane_row = iota((PEERS, HID), 0)
    total = None
    for slot in range(CAP):
        sine, cosine = sin_cos(angles_of(points, slot, freq, phase))
        stack = [sine.astype(BF16)] + [(cosine * freq[c : c + 1]).astype(BF16) for c in range(3)]
        one = [dot_nn(part, first) for part in stack]
        value, slope = silu_pair(one[0])
        hidden = [value.astype(BF16)] + [(one[k] * slope).astype(BF16) for k in range(1, 4)]
        two = [dot_nn(part, second) for part in hidden]
        value, slope = silu_pair(two[0])
        hidden = [value.astype(BF16)] + [(two[k] * slope).astype(BF16) for k in range(1, 4)]
        for k in range(4):
            keep = (lane_row // 16 == slot) & (lane_row % 4 == k)
            head = jnp.where(keep, head_all, jnp.zeros_like(head_all))
            term = dot_nt(hidden[k], head)
            total = term if total is None else total + term
    out_ref[...] = total


def device_kernel(
    fields_ref,
    wide_ref,
    ray_ref,
    hot_ref,
    member_ref,
    camera_ref,
    out_ref,
    stack_ref,
    block_ref,
    samp_ref,
):
    px = wide_ref[0:1, :]
    py = wide_ref[1:2, :]
    pz = wide_ref[2:3, :]
    spacing = wide_ref[3:4, :]
    rank = wide_ref[4:5, :]
    near_one = wide_ref[5:6, :]
    near_two = wide_ref[6:7, :]
    near_three = wide_ref[7:8, :]
    hot = hot_ref[...]
    member = member_ref[...]
    turned = jnp.transpose(fields_ref[...])[0 : 16 * CAP]
    high, middle, low = split_three(turned)
    gathered = dot_nn(high, hot) + (dot_nn(middle, hot) + dot_nn(low, hot))
    fields = jnp.where(rank == 0.0, gathered[0:16], 0.0)
    for slot in range(1, CAP):
        fields = jnp.where(rank == float(slot), gathered[16 * slot : 16 * slot + 16], fields)

    def preceding(value):
        return (
            pltpu.roll(value, 1, 1) * near_one
            + pltpu.roll(value, 2, 1) * near_two
            + pltpu.roll(value, 3, 1) * near_three
        )

    def following(value):
        return (
            pltpu.roll(value * near_one, LANES - 1, 1)
            + pltpu.roll(value * near_two, LANES - 2, 1)
            + pltpu.roll(value * near_three, LANES - 3, 1)
        )

    raw = [fields[4 * o : 4 * o + 1] for o in range(4)]
    moved = [[fields[4 * o + 1 + c : 4 * o + 2 + c] for c in range(3)] for o in range(4)]
    density = jnp.maximum(raw[0], 0.0) + jnp.log1p(jnp.exp(-jnp.abs(raw[0])))
    depth = density * spacing
    through = jnp.exp(-preceding(depth))
    fade = jnp.exp(-depth)
    weight = through * (1.0 - fade)
    depth_slope = spacing * jax.nn.sigmoid(raw[0])
    along = []
    for o in range(4):
        m0, m1, m2 = moved[o]
        along.append([m2 * py - m1 * pz, m0 * pz - m2 * px, m1 * px - m0 * py, m0, m1, m2])
    stack_ref[...] = jnp.zeros_like(stack_ref)
    samp_ref[...] = jnp.zeros_like(samp_ref)
    scale = 1.0 / float(RAYS * REPS)
    slope_zero = None
    slope_rest = []
    for c in range(3):
        tint = jax.nn.sigmoid(raw[1 + c])
        share = weight * tint
        later = following(share)
        sense_zero = (through * fade * tint - later) * depth_slope
        sense_own = share * (1.0 - tint)
        miss = share + preceding(share) + later - wide_ref[8 + c : 9 + c, :]
        part = miss * sense_zero
        slope_zero = part if slope_zero is None else slope_zero + part
        slope_rest.append(scale * miss * sense_own)
        for k in range(6):
            stack_ref[8 * c + k : 8 * c + k + 1, :] = (
                sense_zero * along[0][k] + sense_own * along[1 + c][k]
            )
        stack_ref[8 * c + 6 : 8 * c + 7, :] = share
    slopes = [scale * slope_zero] + slope_rest
    for slot in range(CAP):
        for o in range(4):
            samp_ref[SLOPE_LANE + 8 * slot + o : SLOPE_LANE + 8 * slot + o + 1, :] = jnp.where(
                rank == float(slot), slopes[o], 0.0
            )

    high, middle, low = split_three(stack_ref[...])
    rays = dot_nt(high, member) + (dot_nt(middle, member) + dot_nt(low, member))
    camera_rank = ray_ref[3:4, 0:RAYS]
    blocks = []
    row = iota((8, RAYS), 0)
    for c in range(3):
        block = rays[8 * c : 8 * c + 8]
        blocks.append(jnp.where(row == 6, block - ray_ref[c : c + 1, 0:RAYS], block))
    block_ref[...] = jnp.zeros_like(block_ref)
    for a in range(6):
        outer = blocks[0][a : a + 1] * blocks[0]
        outer = outer + blocks[1][a : a + 1] * blocks[1]
        outer = outer + blocks[2][a : a + 1] * blocks[2]
        for slot in range(CAPC):
            kept = jnp.where(camera_rank == float(slot), outer, 0.0)
            base = 48 * slot
            block_ref[base + 6 * a : base + 6 * a + 6, 0:RAYS] = kept[0:6]
            block_ref[base + FORCE_ROW + a : base + FORCE_ROW + a + 1, 0:RAYS] = kept[6:7]
    for slot in range(CAPC):
        base = 48 * slot + LABEL_ROW
        block_ref[base : base + 2, 0:RAYS] = jnp.where(
            camera_rank == float(slot), ray_ref[4:6, 0:RAYS], 0.0
        )
    message = dot_nt(camera_ref[...], block_ref[...].astype(BF16))
    out_ref[...] = message + dot_nt(hot, samp_ref[...].astype(BF16))


def relay_kernel(got_ref, points_ref, out_ref):
    mine = points_ref[0:HALF, CORE_LANE : CORE_LANE + 1]
    packed = None
    for core in range(2):
        parts = split_three(points_ref[pl.ds(core, HALF, stride=2), :])
        for number, part in enumerate(parts):
            moved = part.astype(F32)
            shift = HALF * core + 16 * number
            if shift:
                moved = pltpu.roll(moved, shift, 1)
            packed = moved if packed is None else packed + moved
    for core in range(2):
        part = got_ref[pl.ds(core, HALF, stride=2), :].astype(BF16)
        kept = jnp.where(mine == float(core), packed, 0.0).astype(BF16)
        for rep in range(REPS):
            row = (2 * rep + core) * PEERS
            out_ref[row : row + HALF, :] = part
            out_ref[row + HALF : row + PEERS, :] = kept


def unpack_points(packed):
    rows = []
    for core in range(2):
        total = None
        for number in range(3):
            shift = HALF * core + 16 * number
            part = pltpu.roll(packed, PEERS - shift, 1) if shift else packed
            total = part if total is None else total + part
        rows.append(total)
    return jnp.concatenate(rows, axis=0)


def final_kernel(
    got_ref,
    wave_ref,
    first_ref,
    second_ref,
    head_ref,
    grad_first_hbm,
    grad_second_hbm,
    grad_head_hbm,
    normal_hbm,
    force_hbm,
    grad_first_ref,
    grad_second_ref,
    grad_head_ref,
    normal_ref,
    force_ref,
    feature_ref,
    one_ref,
    back_one_ref,
    back_two_ref,
    left_ref,
    sems,
):
    first_out, second_out, head_out, normal_out, force_out = [
        pltpu.make_async_copy(source, place, sems.at[number])
        for number, (source, place) in enumerate(
            [
                (grad_first_ref, grad_first_hbm),
                (grad_second_ref, grad_second_hbm),
                (grad_head_ref, grad_head_hbm),
                (normal_ref, normal_hbm),
                (force_ref, force_hbm),
            ]
        )
    ]

    values = []
    group = []
    low_hot = []
    arrived = []
    turned = []
    low_lane = iota((PEERS, LOW), 1).astype(F32)
    for rep in range(REPS):
        base = 2 * rep * PEERS
        got = jnp.concatenate(
            [got_ref[base : base + HALF, :], got_ref[base + PEERS : base + PEERS + HALF, :]], axis=0
        )
        arrived.append(got)
        got = got.astype(F32)
        flipped = jnp.transpose(got)
        turned.append(flipped)
        for slot in range(CAPC):
            base = 48 * slot
            label = base + LABEL_ROW
            values.append(flipped[base : base + 48])
            group.append(flipped[label : label + 1])
            low_hot.append((got[:, label + 1 : label + 2] == low_lane).astype(BF16))
    values = jnp.concatenate(values, axis=1)
    group = jnp.concatenate(group, axis=1)
    low_hot = jnp.concatenate(low_hot, axis=0)
    for block in range(CAM_DEV // LOW):
        left_ref[48 * block : 48 * block + 48, :] = jnp.where(
            group == float(block), values, 0.0
        ).astype(BF16)
    table = dot_nn(left_ref[...], low_hot)
    for block in range(CAM_DEV // LOW):
        base = 48 * block
        place = slice(block * LOW, (block + 1) * LOW)
        normal_ref[:, place] = table[base : base + 36]
        force_ref[:, place] = table[base + FORCE_ROW : base + FORCE_ROW + 6]
    normal_out.start()
    force_out.start()

    freq = wave_ref[0:3, :]
    phase = wave_ref[3:4, :]
    first = first_ref[...]
    second = second_ref[...]
    wide_row = iota((PEERS, HID), 0)
    head_all = head_ref[...]
    heads = []
    for slot in range(CAP):
        keep = (wide_row >= SLOPE_LANE + 8 * slot) & (wide_row < SLOPE_LANE + 8 * slot + 8)
        heads.append(jnp.where(keep, head_all, jnp.zeros_like(head_all)))
    head_parts = [None] * CAP
    for rep in range(REPS):
        base = 2 * rep * PEERS + HALF
        packed = got_ref[base : base + HALF, :].astype(F32)
        packed = packed + got_ref[base + PEERS : base + PEERS + HALF, :].astype(F32)
        points = unpack_points(packed)
        slopes_flipped = turned[rep][SLOPE_LANE:PEERS].astype(BF16)
        for slot in range(CAP):
            row = (rep * CAP + slot) * PEERS
            sine, _ = sin_cos(angles_of(points, slot, freq, phase))
            feature = sine.astype(BF16)
            value_one, slope_one = silu_pair(dot_nn(feature, first))
            hidden_one = value_one.astype(BF16)
            value_two, slope_two = silu_pair(dot_nn(hidden_one, second))
            hidden_two = value_two.astype(BF16)
            back_two = (dot_nn(arrived[rep], heads[slot]) * slope_two).astype(BF16)
            back_one = (dot_nt(back_two, second) * slope_one).astype(BF16)
            term = dot_nn(slopes_flipped, hidden_two)
            head_parts[slot] = term if head_parts[slot] is None else head_parts[slot] + term
            feature_ref[:, row : row + PEERS] = jnp.transpose(sine).astype(BF16)
            one_ref[:, row : row + PEERS] = jnp.transpose(value_one).astype(BF16)
            back_one_ref[row : row + PEERS, :] = back_one
            back_two_ref[row : row + PEERS, :] = back_two
    head_sum = jnp.zeros((4, HID), F32)
    for slot in range(CAP):
        head_sum = head_sum + head_parts[slot][8 * slot : 8 * slot + 4]
    grad_head_ref[0] = head_sum
    head_out.start()
    grad_second_ref[0] = dot_nn(one_ref[...], back_two_ref[...])
    second_out.start()
    grad_first_ref[0] = dot_nn(feature_ref[...], back_one_ref[...])
    first_out.start()
    for copy in (normal_out, force_out, head_out, second_out, first_out):
        copy.wait()


def call(kernel, out_shape, *args, hbm=(), hbm_out=False, scratch=(), room=8):
    def spec(number):
        return pl.BlockSpec(memory_space=pltpu.HBM if number in hbm else pltpu.VMEM)

    place = pltpu.HBM if hbm_out else pltpu.VMEM
    args = [
        pltpu.with_memory_space_constraint(arg, pltpu.HBM) if number in hbm else arg
        for number, arg in enumerate(args)
    ]
    return pl.pallas_call(
        kernel,
        out_shape=out_shape,
        in_specs=[spec(number) for number in range(len(args))],
        out_specs=jax.tree.map(lambda _: pl.BlockSpec(memory_space=place), out_shape),
        scratch_shapes=list(scratch),
        compiler_params=pltpu.CompilerParams(vmem_limit_bytes=room * 1024 * 1024),
    )(*args)


def shape(*dims, dtype=F32):
    return jax.ShapeDtypeStruct(dims, dtype)


def exchange(value, axes="expert", groups=None):
    return lax.all_to_all(
        value, axes, split_axis=0, concat_axis=0, tiled=True, axis_index_groups=groups
    )


def per_device(
    positions,
    frequencies,
    phases,
    w_first,
    w_second,
    w_head,
    spacing,
    expert_ids,
    ray_lengths,
    target,
    cam_owner,
    cam_slot,
):
    ids_row = expert_ids.reshape(1, SAMP)
    square = shape(PEERS, PEERS)
    outgoing, wide, ray, wave, hot, member, camera, *rest = call(
        setup_kernel,
        (
            square,
            pltpu.VMEM((16, LANES), F32),
            pltpu.VMEM((8, PEERS), F32),
            pltpu.VMEM((8, HID), F32),
            pltpu.VMEM((PEERS, LANES), BF16),
            pltpu.VMEM((RAYS, LANES), BF16),
            pltpu.VMEM((PEERS, PEERS), BF16),
            pltpu.VMEM((HID, HID), BF16),
            pltpu.VMEM((HID, HID), BF16),
            pltpu.VMEM((PEERS, HID), BF16),
            pltpu.VMEM((PEERS, HID), BF16),
        ),
        ids_row,
        positions,
        spacing.reshape(1, SAMP),
        ray_lengths,
        target,
        cam_owner.reshape(1, RAYS),
        cam_slot.reshape(1, RAYS),
        frequencies,
        phases.reshape(1, HID),
        w_first,
        w_second,
        w_head,
        hbm=range(12),
        scratch=[
            pltpu.VMEM((1, SAMP), jnp.int32),
            pltpu.VMEM((3, SAMP), F32),
            pltpu.VMEM((1, SAMP), F32),
            pltpu.VMEM((1, RAYS), jnp.int32),
            pltpu.VMEM((3, RAYS), F32),
            pltpu.VMEM((1, RAYS), jnp.int32),
            pltpu.VMEM((1, RAYS), jnp.int32),
            pltpu.VMEM((3, HID), F32),
            pltpu.VMEM((1, HID), F32),
            pltpu.VMEM((1, HID, HID), BF16),
            pltpu.VMEM((1, HID, HID), BF16),
            pltpu.VMEM((1, 4, HID), BF16),
            pltpu.VMEM((PEERS, LANES), F32),
            pltpu.SemaphoreType.DMA((12,)),
        ],
    )
    first, second, head_out, head_back = rest
    points = exchange(outgoing)
    fields = call(forward_kernel, square, points, wave, first, second, head_out)
    returned = exchange(fields)
    message = call(
        device_kernel,
        square,
        returned,
        wide,
        ray,
        hot,
        member,
        camera,
        scratch=[
            pltpu.VMEM((24, LANES), F32),
            pltpu.VMEM((PEERS, PEERS), F32),
            pltpu.VMEM((PEERS, LANES), F32),
        ],
    )
    same_core = [[2 * pair + core for pair in range(HALF)] for core in range(2)]
    arrived = exchange(message, groups=same_core)
    relayed = call(
        relay_kernel,
        shape(2 * REPS * PEERS, PEERS, dtype=BF16),
        arrived,
        points,
    )
    around = [
        [rep * PEERS + 2 * pair + core for rep in range(REPS) for core in range(2)]
        for pair in range(HALF)
    ]
    rows = REPS * CAP * PEERS
    everything = exchange(relayed, ("rep", "expert"), around)
    rows = REPS * CAP * PEERS
    return call(
        final_kernel,
        (
            shape(1, HID, HID),
            shape(1, HID, HID),
            shape(1, 4, HID),
            shape(36, CAM_DEV),
            shape(6, CAM_DEV),
        ),
        everything,
        wave,
        first,
        second,
        head_back,
        hbm_out=True,
        room=32,
        scratch=[
            pltpu.VMEM((1, HID, HID), F32),
            pltpu.VMEM((1, HID, HID), F32),
            pltpu.VMEM((1, 4, HID), F32),
            pltpu.VMEM((36, CAM_DEV), F32),
            pltpu.VMEM((6, CAM_DEV), F32),
            pltpu.VMEM((HID, rows), BF16),
            pltpu.VMEM((HID, rows), BF16),
            pltpu.VMEM((rows, HID), BF16),
            pltpu.VMEM((rows, HID), BF16),
            pltpu.VMEM((48 * (CAM_DEV // LOW), REPS * CAPC * PEERS), BF16),
            pltpu.SemaphoreType.DMA((5,)),
        ],
    )


def solution(mesh):
    in_specs = (
        P(None, ("rep", "expert")),
        P(),
        P(),
        P("expert", None, None),
        P("expert", None, None),
        P("expert", None, None),
        P(("rep", "expert")),
        P(("rep", "expert"), None),
        P(("rep", "expert"), None),
        P(None, ("rep", "expert")),
        P(("rep", "expert"), None),
        P(("rep", "expert")),
    )
    out_specs = (
        P("expert", None, None),
        P("expert", None, None),
        P("expert", None, None),
        P(None, "expert"),
        P(None, "expert"),
    )
    return jax.shard_map(
        per_device, mesh=mesh, in_specs=in_specs, out_specs=out_specs, check_vma=False
    )
```

```python
import jax
import jax.numpy as jnp
from jax import lax
from jax.experimental import pallas as pl
from jax.experimental.pallas import tpu as pltpu
from jax.sharding import PartitionSpec as P

HID = 256
PEERS = 128
REPS = 4
HALF = PEERS // 2
SAMP = 192
RAYS = 96
LANES = 256
CAP = 3
CAPC = 2
CAM_DEV = 8192
LOW = 256
SLOPE_LANE = 96
LABEL_ROW = 36
FORCE_ROW = 40
POINT_LANES = (
    *range(100, 104),
    *range(108, 112),
    *range(116, 128),
    *(38, 39, 46, 47, 86, 87, 94, 95),
)

F32 = jnp.float32
BF16 = jnp.bfloat16


def iota(shape, axis):
    return lax.broadcasted_iota(jnp.int32, shape, axis)


def dot_nn(left, right):
    return jnp.dot(left, right, preferred_element_type=F32)


def dot_nt(left, right):
    return lax.dot_general(left, right, (((1,), (1,)), ((), ())), preferred_element_type=F32)


def dot_tn(left, right):
    return lax.dot_general(left, right, (((0,), (0,)), ((), ())), preferred_element_type=F32)


def split_three(value):
    high = value.astype(BF16)
    rest = value - high.astype(F32)
    middle = rest.astype(BF16)
    low = (rest - middle.astype(F32)).astype(BF16)
    return high, middle, low


def sin_cos(angle):
    turns = jnp.round(angle * 0.6366197723675814)
    rest = angle - turns * 1.5703125
    rest = rest - turns * 4.8375129699707031e-4
    rest = rest - turns * 7.549789954891882e-8
    square = rest * rest
    sine = rest + rest * square * (
        -1.6666654611e-1 + square * (8.3321608736e-3 - square * 1.9515295891e-4)
    )
    cosine = (
        1.0
        - 0.5 * square
        + square
        * square
        * (4.166664568298827e-2 + square * (-1.388731625493765e-3 + square * 2.443315711809948e-5))
    )
    quarter = turns.astype(jnp.int32)
    odd = (quarter & 1) == 1
    sin_value = jnp.where(odd, cosine, sine)
    cos_value = jnp.where(odd, sine, cosine)
    sin_value = jnp.where((quarter & 2) == 2, -sin_value, sin_value)
    cos_value = jnp.where(((quarter + 1) & 2) == 2, -cos_value, cos_value)
    return sin_value, cos_value


def sine_of(angle):
    turns = jnp.round(angle * 0.3183098861837907)
    rest = (angle - turns * 3.140625) - turns * 9.676535897932385e-4
    square = rest * rest
    value = rest + rest * square * (
        -1.6666666666e-1
        + square
        * (
            8.3333333e-3
            + square * (-1.98412698e-4 + square * (2.7557319e-6 - square * 2.5052108e-8))
        )
    )
    half = 0.5 * turns
    return value * (1.0 - 4.0 * (half - jnp.floor(half)))


def angles_of(points, slot, freq, phase):
    base = 4 * slot
    angle = freq[0:1] * points[:, base : base + 1] + freq[1:2] * points[:, base + 1 : base + 2]
    return angle + freq[2:3] * points[:, base + 2 : base + 3] + phase


def silu_pair(value):
    sig = jax.nn.sigmoid(value)
    result = value * sig
    return result, sig + result * (1.0 - sig)


def expert_rank(ids_row, width):
    hot = (iota((PEERS, width), 0) == ids_row).astype(F32)
    earlier = (iota((width, width), 0) < iota((width, width), 1)).astype(BF16)
    counts = dot_nn(hot.astype(BF16), earlier)
    rank = jnp.sum(counts * hot, axis=0, keepdims=True)
    return hot, rank


def fetch(pairs, sems):
    copies = [
        pltpu.make_async_copy(source, place, sems.at[number])
        for number, (source, place) in enumerate(pairs)
    ]
    for copy in copies:
        copy.start()
    for copy in copies:
        copy.wait()


def setup_kernel(
    ids_hbm,
    pos_hbm,
    space_hbm,
    length_hbm,
    target_hbm,
    owner_hbm,
    slot_hbm,
    freq_hbm,
    phase_hbm,
    first_hbm,
    second_hbm,
    head_hbm,
    outgoing_ref,
    base_ref,
    wide_ref,
    ray_ref,
    wave_ref,
    hot_ref,
    member_ref,
    camera_ref,
    first_ref,
    second_ref,
    head_out_ref,
    head_back_ref,
    ids_ref,
    pos_ref,
    space_ref,
    length_ref,
    target_ref,
    owner_ref,
    slot_ref,
    freq_ref,
    phase_ref,
    one_ref,
    two_ref,
    head_ref,
    rows_ref,
    sems,
):
    fetch(
        [
            (ids_hbm, ids_ref),
            (pos_hbm, pos_ref),
            (space_hbm, space_ref),
            (length_hbm, length_ref),
            (target_hbm, target_ref),
            (owner_hbm, owner_ref),
            (slot_hbm, slot_ref),
            (freq_hbm, freq_ref),
            (phase_hbm, phase_ref),
            (first_hbm, one_ref),
            (second_hbm, two_ref),
            (head_hbm, head_ref),
        ],
        sems,
    )
    first_ref[...] = one_ref[0]
    second_ref[...] = two_ref[0]
    wave_ref[...] = jnp.zeros_like(wave_ref)
    wave_ref[0:3, :] = freq_ref[...]
    wave_ref[3:4, :] = phase_ref[...]
    row = iota((PEERS, 4), 0)
    column = iota((PEERS, 4), 1)
    head = head_ref[0]
    head_out_ref[...] = dot_nn(((row // 4) % 4 == column).astype(BF16), head).astype(BF16)
    row = iota((16, 4), 0)
    head_back_ref[...] = dot_nn((row == iota((16, 4), 1)).astype(BF16), head).astype(BF16)

    wide_ref[...] = jnp.zeros_like(wide_ref)
    wide_ref[0:3, 0:SAMP] = pos_ref[...]
    wide_ref[3:4, 0:SAMP] = space_ref[...]
    wide_ref[4:5, :] = jnp.full((1, LANES), -1.0, F32)
    wide_ref[4:5, 0:SAMP] = ids_ref[...].astype(F32)
    ids = wide_ref[4:5, :].astype(jnp.int32)
    hot, rank = expert_rank(ids, LANES)
    hot = hot.astype(BF16)
    hot_ref[...] = hot
    wide_ref[4:5, :] = rank
    rows_ref[...] = jnp.zeros_like(rows_ref)
    points = wide_ref[0:3, :]
    for slot in range(CAP):
        rows_ref[4 * slot : 4 * slot + 3, :] = jnp.where(rank == float(slot), points, 0.0)
    high, middle, low = split_three(rows_ref[...])
    outgoing_ref[...] = dot_nt(hot, high) + (dot_nt(hot, middle) + dot_nt(hot, low))
    rows_ref[0:16, :] = jnp.zeros((16, LANES), F32)
    parts = [part.astype(F32) for part in split_three(points)]
    for slot in range(CAP):
        for number, part in enumerate(parts):
            kept = jnp.where(rank == float(slot), part, 0.0)
            for c in range(3):
                lane = POINT_LANES[9 * slot + 3 * number + c]
                rows_ref[lane : lane + 1, :] = kept[c : c + 1]
    base_ref[...] = dot_nt(hot, rows_ref[...].astype(BF16))

    lengths = length_ref[...].astype(F32)
    ray_a = iota((RAYS, RAYS), 0)
    ray_b = iota((RAYS, RAYS), 1)
    starts = jnp.sum(jnp.where(ray_b < ray_a, lengths, 0.0), axis=1, keepdims=True)
    ends = jnp.sum(jnp.where(ray_b <= ray_a, lengths, 0.0), axis=1, keepdims=True)
    index = iota((RAYS, LANES), 1).astype(F32)
    member = ((index >= starts) & (index < ends)).astype(BF16)
    member_ref[...] = member
    begin = jnp.sum((index == starts).astype(F32), axis=0, keepdims=True)
    near_one = 1.0 - begin
    near_two = near_one * pltpu.roll(near_one, 1, 1)
    near_three = near_two * pltpu.roll(near_one, 2, 1)
    wide_ref[5:6, :] = near_one
    wide_ref[6:7, :] = near_two
    wide_ref[7:8, :] = near_three
    targets = target_ref[...]
    high, middle, low = split_three(targets)
    wide_ref[8:11, :] = dot_nn(high, member) + (dot_nn(middle, member) + dot_nn(low, member))

    ray_ref[...] = jnp.zeros_like(ray_ref)
    ray_ref[0:3, 0:RAYS] = targets
    ray_ref[3:4, :] = jnp.full((1, PEERS), -1.0, F32)
    ray_ref[3:4, 0:RAYS] = owner_ref[...].astype(F32)
    owners = ray_ref[3:4, :].astype(jnp.int32)
    camera, camera_rank = expert_rank(owners, PEERS)
    camera_ref[...] = camera.astype(BF16)
    ray_ref[3:4, :] = camera_rank
    slots = slot_ref[...]
    ray_ref[4:5, 0:RAYS] = (slots // LOW).astype(F32)
    ray_ref[5:6, 0:RAYS] = (slots & (LOW - 1)).astype(F32)


def forward_kernel(points_ref, wave_ref, first_ref, second_ref, head_ref, out_ref):
    points = points_ref[...]
    freq = wave_ref[0:3, :]
    phase = wave_ref[3:4, :]
    first = first_ref[...]
    second = second_ref[...]
    head_all = head_ref[...]
    lane_row = iota((PEERS, HID), 0)
    total = None
    for slot in range(CAP):
        sine, cosine = sin_cos(angles_of(points, slot, freq, phase))
        stack = [sine.astype(BF16)] + [(cosine * freq[c : c + 1]).astype(BF16) for c in range(3)]
        one = [dot_nn(part, first) for part in stack]
        value, slope = silu_pair(one[0])
        hidden = [value.astype(BF16)] + [(one[k] * slope).astype(BF16) for k in range(1, 4)]
        two = [dot_nn(part, second) for part in hidden]
        value, slope = silu_pair(two[0])
        hidden = [value.astype(BF16)] + [(two[k] * slope).astype(BF16) for k in range(1, 4)]
        for k in range(4):
            keep = (lane_row // 16 == slot) & (lane_row % 4 == k)
            head = jnp.where(keep, head_all, jnp.zeros_like(head_all))
            term = dot_nt(hidden[k], head)
            total = term if total is None else total + term
    out_ref[...] = total


def device_kernel(
    fields_ref,
    wide_ref,
    ray_ref,
    hot_ref,
    member_ref,
    camera_ref,
    base_ref,
    out_ref,
    stack_ref,
    block_ref,
    samp_ref,
):
    px = wide_ref[0:1, :]
    py = wide_ref[1:2, :]
    pz = wide_ref[2:3, :]
    spacing = wide_ref[3:4, :]
    rank = wide_ref[4:5, :]
    near_one = wide_ref[5:6, :]
    near_two = wide_ref[6:7, :]
    near_three = wide_ref[7:8, :]
    hot = hot_ref[...]
    member = member_ref[...]
    turned = jnp.transpose(fields_ref[...])[0 : 16 * CAP]
    high, middle, low = split_three(turned)
    gathered = dot_nn(high, hot) + (dot_nn(middle, hot) + dot_nn(low, hot))
    fields = jnp.where(rank == 0.0, gathered[0:16], 0.0)
    for slot in range(1, CAP):
        fields = jnp.where(rank == float(slot), gathered[16 * slot : 16 * slot + 16], fields)

    def preceding(value):
        return (
            pltpu.roll(value, 1, 1) * near_one
            + pltpu.roll(value, 2, 1) * near_two
            + pltpu.roll(value, 3, 1) * near_three
        )

    def following(value):
        return (
            pltpu.roll(value * near_one, LANES - 1, 1)
            + pltpu.roll(value * near_two, LANES - 2, 1)
            + pltpu.roll(value * near_three, LANES - 3, 1)
        )

    raw = [fields[4 * o : 4 * o + 1] for o in range(4)]
    moved = [[fields[4 * o + 1 + c : 4 * o + 2 + c] for c in range(3)] for o in range(4)]
    density = jnp.maximum(raw[0], 0.0) + jnp.log1p(jnp.exp(-jnp.abs(raw[0])))
    depth = density * spacing
    through = jnp.exp(-preceding(depth))
    fade = jnp.exp(-depth)
    weight = through * (1.0 - fade)
    depth_slope = spacing * jax.nn.sigmoid(raw[0])
    along = []
    for o in range(4):
        m0, m1, m2 = moved[o]
        along.append([m2 * py - m1 * pz, m0 * pz - m2 * px, m1 * px - m0 * py, m0, m1, m2])
    stack_ref[...] = jnp.zeros_like(stack_ref)
    samp_ref[...] = jnp.zeros_like(samp_ref)
    scale = 1.0 / float(RAYS * REPS)
    slope_zero = None
    slope_rest = []
    for c in range(3):
        tint = jax.nn.sigmoid(raw[1 + c])
        share = weight * tint
        later = following(share)
        sense_zero = (through * fade * tint - later) * depth_slope
        sense_own = share * (1.0 - tint)
        miss = share + preceding(share) + later - wide_ref[8 + c : 9 + c, :]
        part = miss * sense_zero
        slope_zero = part if slope_zero is None else slope_zero + part
        slope_rest.append(scale * miss * sense_own)
        for k in range(6):
            stack_ref[8 * c + k : 8 * c + k + 1, :] = (
                sense_zero * along[0][k] + sense_own * along[1 + c][k]
            )
        stack_ref[8 * c + 6 : 8 * c + 7, :] = share
    slopes = [scale * slope_zero] + slope_rest
    for slot in range(CAP):
        for o in range(4):
            samp_ref[SLOPE_LANE + 8 * slot + o : SLOPE_LANE + 8 * slot + o + 1, :] = jnp.where(
                rank == float(slot), slopes[o], 0.0
            )

    high, middle, low = split_three(stack_ref[...])
    rays = dot_nt(high, member) + (dot_nt(middle, member) + dot_nt(low, member))
    camera_rank = ray_ref[3:4, 0:RAYS]
    blocks = []
    row = iota((8, RAYS), 0)
    for c in range(3):
        block = rays[8 * c : 8 * c + 8]
        blocks.append(jnp.where(row == 6, block - ray_ref[c : c + 1, 0:RAYS], block))
    block_ref[...] = jnp.zeros_like(block_ref)
    for a in range(6):
        outer = blocks[0][a : a + 1] * blocks[0]
        outer = outer + blocks[1][a : a + 1] * blocks[1]
        outer = outer + blocks[2][a : a + 1] * blocks[2]
        for slot in range(CAPC):
            kept = jnp.where(camera_rank == float(slot), outer, 0.0)
            base = 48 * slot
            block_ref[base + 6 * a : base + 6 * a + 6, 0:RAYS] = kept[0:6]
            block_ref[base + FORCE_ROW + a : base + FORCE_ROW + a + 1, 0:RAYS] = kept[6:7]
    for slot in range(CAPC):
        base = 48 * slot + LABEL_ROW
        block_ref[base : base + 2, 0:RAYS] = jnp.where(
            camera_rank == float(slot), ray_ref[4:6, 0:RAYS], 0.0
        )
    message = dot_nt(camera_ref[...], block_ref[...].astype(BF16))
    out_ref[...] = (message + base_ref[...]) + dot_nt(hot, samp_ref[...].astype(BF16))


def relay_kernel(got_ref, out_ref):
    for core in range(2):
        part = got_ref[pl.ds(core, HALF, stride=2), :].astype(BF16)
        for rep in range(REPS):
            row = (2 * rep + core) * HALF
            out_ref[row : row + HALF, :] = part


def final_kernel(
    got_ref,
    wave_ref,
    first_ref,
    second_ref,
    head_ref,
    grad_first_hbm,
    grad_second_hbm,
    grad_head_hbm,
    normal_hbm,
    force_hbm,
    grad_first_ref,
    grad_second_ref,
    grad_head_ref,
    normal_ref,
    force_ref,
    spread_ref,
    left_ref,
    sems,
):
    first_out, second_out, head_out, normal_out, force_out = [
        pltpu.make_async_copy(source, place, sems.at[number])
        for number, (source, place) in enumerate(
            [
                (grad_first_ref, grad_first_hbm),
                (grad_second_ref, grad_second_hbm),
                (grad_head_ref, grad_head_hbm),
                (normal_ref, normal_hbm),
                (force_ref, force_hbm),
            ]
        )
    ]

    values = []
    group = []
    low_hot = []
    turned = []
    low_lane = iota((PEERS, LOW), 1).astype(F32)
    for rep in range(REPS):
        got = got_ref[rep * PEERS : (rep + 1) * PEERS, :].astype(F32)
        flipped = jnp.transpose(got)
        turned.append(flipped)
        for slot in range(CAPC):
            base = 48 * slot
            label = base + LABEL_ROW
            values.append(flipped[base : base + 48])
            group.append(flipped[label : label + 1])
            low_hot.append((got[:, label + 1 : label + 2] == low_lane).astype(BF16))
    values = jnp.concatenate(values, axis=1)
    group = jnp.concatenate(group, axis=1)
    low_hot = jnp.concatenate(low_hot, axis=0)
    for block in range(CAM_DEV // LOW):
        left_ref[48 * block : 48 * block + 48, :] = jnp.where(
            group == float(block), values, 0.0
        ).astype(BF16)
    table = dot_nn(left_ref[...], low_hot)
    for block in range(CAM_DEV // LOW):
        base = 48 * block
        place = slice(block * LOW, (block + 1) * LOW)
        normal_ref[:, place] = table[base : base + 36]
        force_ref[:, place] = table[base + FORCE_ROW : base + FORCE_ROW + 6]
    normal_out.start()
    force_out.start()

    columns = jnp.transpose(wave_ref[...])
    for number in range(4):
        spread_ref[number] = jnp.broadcast_to(columns[:, number : number + 1], (HID, PEERS))
    first = first_ref[...]
    second = second_ref[...]
    head = head_ref[...]
    grad_first = grad_second = grad_head = None
    for part in range(2):
        features = []
        slopes = []
        for rep in range(2 * part, 2 * part + 2):
            flipped = turned[rep]
            for slot in range(CAP):
                angle = None
                for c in range(3):
                    lanes = [POINT_LANES[9 * slot + 3 * number + c] for number in range(3)]
                    high, middle, low = [flipped[lane : lane + 1] for lane in lanes]
                    term = spread_ref[c] * (high + middle + low)
                    angle = term if angle is None else angle + term
                features.append(sine_of(angle + spread_ref[3]).astype(BF16))
                base = SLOPE_LANE + 8 * slot
                slopes.append(flipped[base : base + 8])
        feature = jnp.concatenate(features, axis=1)
        slopes = jnp.concatenate(slopes, axis=1)
        slopes = jnp.concatenate([slopes, jnp.zeros_like(slopes)], axis=0).astype(BF16)
        value_one, slope_one = silu_pair(dot_tn(first, feature))
        hidden_one = value_one.astype(BF16)
        value_two, slope_two = silu_pair(dot_tn(second, hidden_one))
        hidden_two = value_two.astype(BF16)
        back_two = (dot_tn(head, slopes) * slope_two).astype(BF16)
        back_one = (dot_nn(second, back_two) * slope_one).astype(BF16)
        terms = (
            dot_nt(feature, back_one),
            dot_nt(hidden_one, back_two),
            dot_nt(slopes, hidden_two),
        )
        if part == 0:
            grad_first, grad_second, grad_head = terms
        else:
            grad_head_ref[0] = (grad_head + terms[2])[0:4]
            head_out.start()
            grad_second_ref[0] = grad_second + terms[1]
            second_out.start()
            grad_first_ref[0] = grad_first + terms[0]
            first_out.start()
    for copy in (normal_out, force_out, head_out, second_out, first_out):
        copy.wait()


def call(kernel, out_shape, *args, hbm=(), hbm_out=False, scratch=(), room=8):
    def spec(number):
        return pl.BlockSpec(memory_space=pltpu.HBM if number in hbm else pltpu.VMEM)

    place = pltpu.HBM if hbm_out else pltpu.VMEM
    args = [
        pltpu.with_memory_space_constraint(arg, pltpu.HBM) if number in hbm else arg
        for number, arg in enumerate(args)
    ]
    return pl.pallas_call(
        kernel,
        out_shape=out_shape,
        in_specs=[spec(number) for number in range(len(args))],
        out_specs=jax.tree.map(lambda _: pl.BlockSpec(memory_space=place), out_shape),
        scratch_shapes=list(scratch),
        compiler_params=pltpu.CompilerParams(vmem_limit_bytes=room * 1024 * 1024),
    )(*args)


def shape(*dims, dtype=F32):
    return jax.ShapeDtypeStruct(dims, dtype)


def exchange(value, axes="expert", groups=None):
    return lax.all_to_all(
        value, axes, split_axis=0, concat_axis=0, tiled=True, axis_index_groups=groups
    )


def per_device(
    positions,
    frequencies,
    phases,
    w_first,
    w_second,
    w_head,
    spacing,
    expert_ids,
    ray_lengths,
    target,
    cam_owner,
    cam_slot,
):
    ids_row = expert_ids.reshape(1, SAMP)
    square = shape(PEERS, PEERS)
    outgoing, base, wide, ray, wave, hot, member, camera, *rest = call(
        setup_kernel,
        (
            square,
            pltpu.VMEM((PEERS, PEERS), F32),
            pltpu.VMEM((16, LANES), F32),
            pltpu.VMEM((8, PEERS), F32),
            pltpu.VMEM((8, HID), F32),
            pltpu.VMEM((PEERS, LANES), BF16),
            pltpu.VMEM((RAYS, LANES), BF16),
            pltpu.VMEM((PEERS, PEERS), BF16),
            pltpu.VMEM((HID, HID), BF16),
            pltpu.VMEM((HID, HID), BF16),
            pltpu.VMEM((PEERS, HID), BF16),
            pltpu.VMEM((16, HID), BF16),
        ),
        ids_row,
        positions,
        spacing.reshape(1, SAMP),
        ray_lengths,
        target,
        cam_owner.reshape(1, RAYS),
        cam_slot.reshape(1, RAYS),
        frequencies,
        phases.reshape(1, HID),
        w_first,
        w_second,
        w_head,
        hbm=range(12),
        scratch=[
            pltpu.VMEM((1, SAMP), jnp.int32),
            pltpu.VMEM((3, SAMP), F32),
            pltpu.VMEM((1, SAMP), F32),
            pltpu.VMEM((1, RAYS), jnp.int32),
            pltpu.VMEM((3, RAYS), F32),
            pltpu.VMEM((1, RAYS), jnp.int32),
            pltpu.VMEM((1, RAYS), jnp.int32),
            pltpu.VMEM((3, HID), F32),
            pltpu.VMEM((1, HID), F32),
            pltpu.VMEM((1, HID, HID), BF16),
            pltpu.VMEM((1, HID, HID), BF16),
            pltpu.VMEM((1, 4, HID), BF16),
            pltpu.VMEM((PEERS, LANES), F32),
            pltpu.SemaphoreType.DMA((12,)),
        ],
    )
    first, second, head_out, head_back = rest
    points = exchange(outgoing)
    fields = call(forward_kernel, square, points, wave, first, second, head_out)
    returned = exchange(fields)
    message = call(
        device_kernel,
        square,
        returned,
        wide,
        ray,
        hot,
        member,
        camera,
        base,
        scratch=[
            pltpu.VMEM((24, LANES), F32),
            pltpu.VMEM((PEERS, PEERS), F32),
            pltpu.VMEM((PEERS, LANES), F32),
        ],
    )
    same_core = [[2 * pair + core for pair in range(HALF)] for core in range(2)]
    arrived = exchange(message, groups=same_core)
    relayed = call(
        relay_kernel,
        shape(REPS * PEERS, PEERS, dtype=BF16),
        arrived,
    )
    around = [
        [rep * PEERS + 2 * pair + core for rep in range(REPS) for core in range(2)]
        for pair in range(HALF)
    ]
    rows = REPS * CAP * PEERS
    everything = exchange(relayed, ("rep", "expert"), around)
    return call(
        final_kernel,
        (
            shape(1, HID, HID),
            shape(1, HID, HID),
            shape(1, 4, HID),
            shape(36, CAM_DEV),
            shape(6, CAM_DEV),
        ),
        everything,
        wave,
        first,
        second,
        head_back,
        hbm_out=True,
        room=32,
        scratch=[
            pltpu.VMEM((1, HID, HID), F32),
            pltpu.VMEM((1, HID, HID), F32),
            pltpu.VMEM((1, 4, HID), F32),
            pltpu.VMEM((36, CAM_DEV), F32),
            pltpu.VMEM((6, CAM_DEV), F32),
            pltpu.VMEM((4, HID, PEERS), F32),
            pltpu.VMEM((48 * (CAM_DEV // LOW), REPS * CAPC * PEERS), BF16),
            pltpu.SemaphoreType.DMA((5,)),
        ],
    )


def solution(mesh):
    in_specs = (
        P(None, ("rep", "expert")),
        P(),
        P(),
        P("expert", None, None),
        P("expert", None, None),
        P("expert", None, None),
        P(("rep", "expert")),
        P(("rep", "expert"), None),
        P(("rep", "expert"), None),
        P(None, ("rep", "expert")),
        P(("rep", "expert"), None),
        P(("rep", "expert")),
    )
    out_specs = (
        P("expert", None, None),
        P("expert", None, None),
        P("expert", None, None),
        P(None, "expert"),
        P(None, "expert"),
    )
    return jax.shard_map(
        per_device, mesh=mesh, in_specs=in_specs, out_specs=out_specs, check_vma=False
    )
```

```python
import jax
import jax.numpy as jnp
from jax import lax
from jax.experimental import pallas as pl
from jax.experimental.pallas import tpu as pltpu
from jax.sharding import PartitionSpec as P

HID = 256
PEERS = 128
REPS = 4
HALF = PEERS // 2
SAMP = 192
RAYS = 96
LANES = 256
CAP = 3
CAPC = 2
CAM_DEV = 8192
LOW = 256
SLOPE_LANE = 96
BUNDLE = 2 * HID + 16
LABEL_ROW = 36
FORCE_ROW = 40
POINT_LANES = (
    *range(100, 104),
    *range(108, 112),
    *range(116, 128),
    *(38, 39, 46, 47, 86, 87, 94, 95),
)

F32 = jnp.float32
BF16 = jnp.bfloat16


def iota(shape, axis):
    return lax.broadcasted_iota(jnp.int32, shape, axis)


def dot_nn(left, right):
    return jnp.dot(left, right, preferred_element_type=F32)


def dot_nt(left, right):
    return lax.dot_general(left, right, (((1,), (1,)), ((), ())), preferred_element_type=F32)


def dot_tn(left, right):
    return lax.dot_general(left, right, (((0,), (0,)), ((), ())), preferred_element_type=F32)


def split_three(value):
    high = value.astype(BF16)
    rest = value - high.astype(F32)
    middle = rest.astype(BF16)
    low = (rest - middle.astype(F32)).astype(BF16)
    return high, middle, low


def sin_cos(angle):
    turns = jnp.round(angle * 0.6366197723675814)
    rest = angle - turns * 1.5703125
    rest = rest - turns * 4.8375129699707031e-4
    rest = rest - turns * 7.549789954891882e-8
    square = rest * rest
    sine = rest + rest * square * (
        -1.6666654611e-1 + square * (8.3321608736e-3 - square * 1.9515295891e-4)
    )
    cosine = (
        1.0
        - 0.5 * square
        + square
        * square
        * (4.166664568298827e-2 + square * (-1.388731625493765e-3 + square * 2.443315711809948e-5))
    )
    quarter = turns.astype(jnp.int32)
    odd = (quarter & 1) == 1
    sin_value = jnp.where(odd, cosine, sine)
    cos_value = jnp.where(odd, sine, cosine)
    sin_value = jnp.where((quarter & 2) == 2, -sin_value, sin_value)
    cos_value = jnp.where(((quarter + 1) & 2) == 2, -cos_value, cos_value)
    return sin_value, cos_value


def sine_of(angle):
    turns = jnp.round(angle * 0.3183098861837907)
    rest = (angle - turns * 3.140625) - turns * 9.676535897932385e-4
    square = rest * rest
    value = rest + rest * square * (
        -1.6666666666e-1
        + square
        * (
            8.3333333e-3
            + square * (-1.98412698e-4 + square * (2.7557319e-6 - square * 2.5052108e-8))
        )
    )
    half = 0.5 * turns
    return value * (1.0 - 4.0 * (half - jnp.floor(half)))


def angles_of(points, slot, freq, phase):
    base = 4 * slot
    angle = freq[0:1] * points[:, base : base + 1] + freq[1:2] * points[:, base + 1 : base + 2]
    return angle + freq[2:3] * points[:, base + 2 : base + 3] + phase


def silu_pair(value):
    sig = jax.nn.sigmoid(value)
    result = value * sig
    return result, sig + result * (1.0 - sig)


def expert_rank(ids_row, width):
    hot = (iota((PEERS, width), 0) == ids_row).astype(F32)
    earlier = (iota((width, width), 0) < iota((width, width), 1)).astype(BF16)
    counts = dot_nn(hot.astype(BF16), earlier)
    rank = jnp.sum(counts * hot, axis=0, keepdims=True)
    return hot, rank


def fetch(pairs, sems):
    copies = [
        pltpu.make_async_copy(source, place, sems.at[number])
        for number, (source, place) in enumerate(pairs)
    ]
    for copy in copies:
        copy.start()
    for copy in copies:
        copy.wait()


def setup_kernel(
    ids_hbm,
    pos_hbm,
    space_hbm,
    length_hbm,
    target_hbm,
    owner_hbm,
    slot_hbm,
    freq_hbm,
    phase_hbm,
    first_hbm,
    second_hbm,
    head_hbm,
    core_ref,
    outgoing_ref,
    base_ref,
    wide_ref,
    ray_ref,
    wave_ref,
    hot_ref,
    member_ref,
    camera_ref,
    bundle_ref,
    ids_ref,
    pos_ref,
    space_ref,
    length_ref,
    target_ref,
    owner_ref,
    slot_ref,
    freq_ref,
    phase_ref,
    one_ref,
    two_ref,
    head_ref,
    rows_ref,
    sems,
):
    fetch(
        [
            (ids_hbm, ids_ref),
            (pos_hbm, pos_ref),
            (space_hbm, space_ref),
            (length_hbm, length_ref),
            (target_hbm, target_ref),
            (owner_hbm, owner_ref),
            (slot_hbm, slot_ref),
            (freq_hbm, freq_ref),
            (phase_hbm, phase_ref),
            (first_hbm, one_ref),
            (second_hbm, two_ref),
            (head_hbm, head_ref),
        ],
        sems,
    )
    bundle_ref[0:HID, :] = one_ref[0]
    bundle_ref[HID : 2 * HID, :] = two_ref[0]
    wave_ref[...] = jnp.zeros_like(wave_ref)
    wave_ref[0:3, :] = freq_ref[...]
    wave_ref[3:4, :] = phase_ref[...]
    pick = (iota((16, 4), 0) == iota((16, 4), 1)).astype(BF16)
    bundle_ref[2 * HID : BUNDLE, :] = dot_nn(pick, head_ref[0]).astype(BF16)

    wide_ref[...] = jnp.zeros_like(wide_ref)
    wide_ref[0:3, 0:SAMP] = pos_ref[...]
    wide_ref[3:4, 0:SAMP] = space_ref[...]
    wide_ref[11:12, 0:PEERS] = core_ref[0:1, :]
    wide_ref[4:5, :] = jnp.full((1, LANES), -1.0, F32)
    wide_ref[4:5, 0:SAMP] = ids_ref[...].astype(F32)
    ids = wide_ref[4:5, :].astype(jnp.int32)
    hot, rank = expert_rank(ids, LANES)
    hot = hot.astype(BF16)
    hot_ref[...] = hot
    wide_ref[4:5, :] = rank
    rows_ref[...] = jnp.zeros_like(rows_ref)
    points = wide_ref[0:3, :]
    for slot in range(CAP):
        rows_ref[4 * slot : 4 * slot + 3, :] = jnp.where(rank == float(slot), points, 0.0)
    high, middle, low = split_three(rows_ref[...])
    outgoing_ref[...] = dot_nt(hot, high) + (dot_nt(hot, middle) + dot_nt(hot, low))
    rows_ref[0:16, :] = jnp.zeros((16, LANES), F32)
    parts = [part.astype(F32) for part in split_three(points)]
    for slot in range(CAP):
        for number, part in enumerate(parts):
            kept = jnp.where(rank == float(slot), part, 0.0)
            for c in range(3):
                lane = POINT_LANES[9 * slot + 3 * number + c]
                rows_ref[lane : lane + 1, :] = kept[c : c + 1]
    base_ref[...] = dot_nt(hot, rows_ref[...].astype(BF16))

    lengths = length_ref[...].astype(F32)
    ray_a = iota((RAYS, RAYS), 0)
    ray_b = iota((RAYS, RAYS), 1)
    starts = jnp.sum(jnp.where(ray_b < ray_a, lengths, 0.0), axis=1, keepdims=True)
    ends = jnp.sum(jnp.where(ray_b <= ray_a, lengths, 0.0), axis=1, keepdims=True)
    index = iota((RAYS, LANES), 1).astype(F32)
    member = ((index >= starts) & (index < ends)).astype(BF16)
    member_ref[...] = member
    begin = jnp.sum((index == starts).astype(F32), axis=0, keepdims=True)
    near_one = 1.0 - begin
    near_two = near_one * pltpu.roll(near_one, 1, 1)
    near_three = near_two * pltpu.roll(near_one, 2, 1)
    wide_ref[5:6, :] = near_one
    wide_ref[6:7, :] = near_two
    wide_ref[7:8, :] = near_three
    targets = target_ref[...]
    high, middle, low = split_three(targets)
    wide_ref[8:11, :] = dot_nn(high, member) + (dot_nn(middle, member) + dot_nn(low, member))

    ray_ref[...] = jnp.zeros_like(ray_ref)
    ray_ref[0:3, 0:RAYS] = targets
    ray_ref[3:4, :] = jnp.full((1, PEERS), -1.0, F32)
    ray_ref[3:4, 0:RAYS] = owner_ref[...].astype(F32)
    owners = ray_ref[3:4, :].astype(jnp.int32)
    camera, camera_rank = expert_rank(owners, PEERS)
    camera_ref[...] = camera.astype(BF16)
    ray_ref[3:4, :] = camera_rank
    slots = slot_ref[...]
    ray_ref[4:5, 0:RAYS] = (slots // LOW).astype(F32)
    ray_ref[5:6, 0:RAYS] = (slots & (LOW - 1)).astype(F32)


def forward_kernel(points_ref, wave_ref, bundle_ref, partner_ref, wide_ref, out_ref):
    freq = wave_ref[0:3, :]
    phase = wave_ref[3:4, :]
    mine = wide_ref[11:12, 0:1]
    row = iota((PEERS, 16), 0)
    head_pick = ((row // 4) % 4 == iota((PEERS, 16), 1)).astype(BF16)
    lane_row = iota((PEERS, HID), 0)
    for core in range(2):
        own = jnp.broadcast_to(mine, (BUNDLE, HID)) == float(core)
        bundle = jnp.where(own, bundle_ref[...].astype(F32), partner_ref[...].astype(F32))
        bundle = bundle.astype(BF16)
        first = bundle[0:HID]
        second = bundle[HID : 2 * HID]
        head_all = dot_nn(head_pick, bundle[2 * HID : BUNDLE]).astype(BF16)
        points = points_ref[pl.ds(core, HALF, stride=2), :]
        angle = jnp.concatenate(
            [angles_of(points, slot, freq, phase) for slot in range(CAP)], axis=0
        )
        sine, cosine = sin_cos(angle)
        stack = [sine.astype(BF16)] + [(cosine * freq[c : c + 1]).astype(BF16) for c in range(3)]
        one = [dot_nn(part, first) for part in stack]
        value, slope = silu_pair(one[0])
        hidden = [value.astype(BF16)] + [(one[k] * slope).astype(BF16) for k in range(1, 4)]
        two = [dot_nn(part, second) for part in hidden]
        value, slope = silu_pair(two[0])
        hidden = [value.astype(BF16)] + [(two[k] * slope).astype(BF16) for k in range(1, 4)]
        total = None
        for slot in range(CAP):
            for k in range(4):
                keep = (lane_row // 16 == slot) & (lane_row % 4 == k)
                head = jnp.where(keep, head_all, jnp.zeros_like(head_all))
                term = dot_nt(hidden[k][HALF * slot : HALF * slot + HALF], head)
                total = term if total is None else total + term
        out_ref[pl.ds(core, HALF, stride=2), :] = total


def device_kernel(
    fields_ref,
    wide_ref,
    ray_ref,
    hot_ref,
    member_ref,
    camera_ref,
    base_ref,
    out_ref,
    stack_ref,
    block_ref,
    samp_ref,
):
    px = wide_ref[0:1, :]
    py = wide_ref[1:2, :]
    pz = wide_ref[2:3, :]
    spacing = wide_ref[3:4, :]
    rank = wide_ref[4:5, :]
    near_one = wide_ref[5:6, :]
    near_two = wide_ref[6:7, :]
    near_three = wide_ref[7:8, :]
    hot = hot_ref[...]
    member = member_ref[...]
    turned = jnp.transpose(fields_ref[...])[0 : 16 * CAP]
    high, middle, low = split_three(turned)
    gathered = dot_nn(high, hot) + (dot_nn(middle, hot) + dot_nn(low, hot))
    fields = jnp.where(rank == 0.0, gathered[0:16], 0.0)
    for slot in range(1, CAP):
        fields = jnp.where(rank == float(slot), gathered[16 * slot : 16 * slot + 16], fields)

    def preceding(value):
        return (
            pltpu.roll(value, 1, 1) * near_one
            + pltpu.roll(value, 2, 1) * near_two
            + pltpu.roll(value, 3, 1) * near_three
        )

    def following(value):
        return (
            pltpu.roll(value * near_one, LANES - 1, 1)
            + pltpu.roll(value * near_two, LANES - 2, 1)
            + pltpu.roll(value * near_three, LANES - 3, 1)
        )

    raw = [fields[4 * o : 4 * o + 1] for o in range(4)]
    moved = [[fields[4 * o + 1 + c : 4 * o + 2 + c] for c in range(3)] for o in range(4)]
    density = jnp.maximum(raw[0], 0.0) + jnp.log1p(jnp.exp(-jnp.abs(raw[0])))
    depth = density * spacing
    through = jnp.exp(-preceding(depth))
    fade = jnp.exp(-depth)
    weight = through * (1.0 - fade)
    depth_slope = spacing * jax.nn.sigmoid(raw[0])
    along = []
    for o in range(4):
        m0, m1, m2 = moved[o]
        along.append([m2 * py - m1 * pz, m0 * pz - m2 * px, m1 * px - m0 * py, m0, m1, m2])
    stack_ref[...] = jnp.zeros_like(stack_ref)
    samp_ref[...] = jnp.zeros_like(samp_ref)
    scale = 1.0 / float(RAYS * REPS)
    slope_zero = None
    slope_rest = []
    for c in range(3):
        tint = jax.nn.sigmoid(raw[1 + c])
        share = weight * tint
        later = following(share)
        sense_zero = (through * fade * tint - later) * depth_slope
        sense_own = share * (1.0 - tint)
        miss = share + preceding(share) + later - wide_ref[8 + c : 9 + c, :]
        part = miss * sense_zero
        slope_zero = part if slope_zero is None else slope_zero + part
        slope_rest.append(scale * miss * sense_own)
        for k in range(6):
            stack_ref[8 * c + k : 8 * c + k + 1, :] = (
                sense_zero * along[0][k] + sense_own * along[1 + c][k]
            )
        stack_ref[8 * c + 6 : 8 * c + 7, :] = share
    slopes = [scale * slope_zero] + slope_rest
    for slot in range(CAP):
        for o in range(4):
            samp_ref[SLOPE_LANE + 8 * slot + o : SLOPE_LANE + 8 * slot + o + 1, :] = jnp.where(
                rank == float(slot), slopes[o], 0.0
            )

    high, middle, low = split_three(stack_ref[...])
    rays = dot_nt(high, member) + (dot_nt(middle, member) + dot_nt(low, member))
    camera_rank = ray_ref[3:4, 0:RAYS]
    blocks = []
    row = iota((8, RAYS), 0)
    for c in range(3):
        block = rays[8 * c : 8 * c + 8]
        blocks.append(jnp.where(row == 6, block - ray_ref[c : c + 1, 0:RAYS], block))
    block_ref[...] = jnp.zeros_like(block_ref)
    for a in range(6):
        outer = blocks[0][a : a + 1] * blocks[0]
        outer = outer + blocks[1][a : a + 1] * blocks[1]
        outer = outer + blocks[2][a : a + 1] * blocks[2]
        for slot in range(CAPC):
            kept = jnp.where(camera_rank == float(slot), outer, 0.0)
            base = 48 * slot
            block_ref[base + 6 * a : base + 6 * a + 6, 0:RAYS] = kept[0:6]
            block_ref[base + FORCE_ROW + a : base + FORCE_ROW + a + 1, 0:RAYS] = kept[6:7]
    for slot in range(CAPC):
        base = 48 * slot + LABEL_ROW
        block_ref[base : base + 2, 0:RAYS] = jnp.where(
            camera_rank == float(slot), ray_ref[4:6, 0:RAYS], 0.0
        )
    message = dot_nt(camera_ref[...], block_ref[...].astype(BF16))
    out_ref[...] = (message + base_ref[...]) + dot_nt(hot, samp_ref[...].astype(BF16))


def relay_kernel(got_ref, out_ref):
    for core in range(2):
        part = got_ref[pl.ds(core, HALF, stride=2), :].astype(BF16)
        for rep in range(REPS):
            row = (2 * rep + core) * HALF
            out_ref[row : row + HALF, :] = part


def final_kernel(
    got_ref,
    wave_ref,
    bundle_ref,
    grad_first_hbm,
    grad_second_hbm,
    grad_head_hbm,
    normal_hbm,
    force_hbm,
    grad_first_ref,
    grad_second_ref,
    grad_head_ref,
    normal_ref,
    force_ref,
    spread_ref,
    left_ref,
    sems,
):
    first_out, second_out, head_out, normal_out, force_out = [
        pltpu.make_async_copy(source, place, sems.at[number])
        for number, (source, place) in enumerate(
            [
                (grad_first_ref, grad_first_hbm),
                (grad_second_ref, grad_second_hbm),
                (grad_head_ref, grad_head_hbm),
                (normal_ref, normal_hbm),
                (force_ref, force_hbm),
            ]
        )
    ]

    values = []
    group = []
    low_hot = []
    turned = []
    low_lane = iota((PEERS, LOW), 1).astype(F32)
    for rep in range(REPS):
        got = got_ref[rep * PEERS : (rep + 1) * PEERS, :].astype(F32)
        flipped = jnp.transpose(got)
        turned.append(flipped)
        for slot in range(CAPC):
            base = 48 * slot
            label = base + LABEL_ROW
            values.append(flipped[base : base + 48])
            group.append(flipped[label : label + 1])
            low_hot.append((got[:, label + 1 : label + 2] == low_lane).astype(BF16))
    values = jnp.concatenate(values, axis=1)
    group = jnp.concatenate(group, axis=1)
    low_hot = jnp.concatenate(low_hot, axis=0)
    for block in range(CAM_DEV // LOW):
        left_ref[48 * block : 48 * block + 48, :] = jnp.where(
            group == float(block), values, 0.0
        ).astype(BF16)
    table = dot_nn(left_ref[...], low_hot)
    for block in range(CAM_DEV // LOW):
        base = 48 * block
        place = slice(block * LOW, (block + 1) * LOW)
        normal_ref[:, place] = table[base : base + 36]
        force_ref[:, place] = table[base + FORCE_ROW : base + FORCE_ROW + 6]
    normal_out.start()
    force_out.start()

    columns = jnp.transpose(wave_ref[...])
    for number in range(4):
        spread_ref[number] = jnp.broadcast_to(columns[:, number : number + 1], (HID, PEERS))
    first = bundle_ref[0:HID, :]
    second = bundle_ref[HID : 2 * HID, :]
    head = bundle_ref[2 * HID : BUNDLE, :]
    grad_first = grad_second = grad_head = None
    for part in range(2):
        features = []
        slopes = []
        for rep in range(2 * part, 2 * part + 2):
            flipped = turned[rep]
            for slot in range(CAP):
                angle = None
                for c in range(3):
                    lanes = [POINT_LANES[9 * slot + 3 * number + c] for number in range(3)]
                    high, middle, low = [flipped[lane : lane + 1] for lane in lanes]
                    term = spread_ref[c] * (high + middle + low)
                    angle = term if angle is None else angle + term
                features.append(sine_of(angle + spread_ref[3]).astype(BF16))
                base = SLOPE_LANE + 8 * slot
                slopes.append(flipped[base : base + 8])
        feature = jnp.concatenate(features, axis=1)
        slopes = jnp.concatenate(slopes, axis=1)
        slopes = jnp.concatenate([slopes, jnp.zeros_like(slopes)], axis=0).astype(BF16)
        value_one, slope_one = silu_pair(dot_tn(first, feature))
        hidden_one = value_one.astype(BF16)
        value_two, slope_two = silu_pair(dot_tn(second, hidden_one))
        hidden_two = value_two.astype(BF16)
        back_two = (dot_tn(head, slopes) * slope_two).astype(BF16)
        back_one = (dot_nn(second, back_two) * slope_one).astype(BF16)
        terms = (
            dot_nt(feature, back_one),
            dot_nt(hidden_one, back_two),
            dot_nt(slopes, hidden_two),
        )
        if part == 0:
            grad_first, grad_second, grad_head = terms
        else:
            grad_head_ref[0] = (grad_head + terms[2])[0:4]
            head_out.start()
            grad_second_ref[0] = grad_second + terms[1]
            second_out.start()
            grad_first_ref[0] = grad_first + terms[0]
            first_out.start()
    for copy in (normal_out, force_out, head_out, second_out, first_out):
        copy.wait()


def call(kernel, out_shape, *args, hbm=(), hbm_out=False, scratch=(), room=8):
    def spec(number):
        return pl.BlockSpec(memory_space=pltpu.HBM if number in hbm else pltpu.VMEM)

    place = pltpu.HBM if hbm_out else pltpu.VMEM
    args = [
        pltpu.with_memory_space_constraint(arg, pltpu.HBM) if number in hbm else arg
        for number, arg in enumerate(args)
    ]
    return pl.pallas_call(
        kernel,
        out_shape=out_shape,
        in_specs=[spec(number) for number in range(len(args))],
        out_specs=jax.tree.map(lambda _: pl.BlockSpec(memory_space=place), out_shape),
        scratch_shapes=list(scratch),
        compiler_params=pltpu.CompilerParams(vmem_limit_bytes=room * 1024 * 1024),
    )(*args)


def shape(*dims, dtype=F32):
    return jax.ShapeDtypeStruct(dims, dtype)


def exchange(value, axes="expert", groups=None):
    return lax.all_to_all(
        value, axes, split_axis=0, concat_axis=0, tiled=True, axis_index_groups=groups
    )


def per_device(
    positions,
    frequencies,
    phases,
    w_first,
    w_second,
    w_head,
    spacing,
    expert_ids,
    ray_lengths,
    target,
    cam_owner,
    cam_slot,
):
    ids_row = expert_ids.reshape(1, SAMP)
    square = shape(PEERS, PEERS)
    core = lax.axis_index("expert") & 1
    outgoing, base, wide, ray, wave, hot, member, camera, bundle = call(
        setup_kernel,
        (
            square,
            pltpu.VMEM((PEERS, PEERS), F32),
            pltpu.VMEM((16, LANES), F32),
            pltpu.VMEM((8, PEERS), F32),
            pltpu.VMEM((8, HID), F32),
            pltpu.VMEM((PEERS, LANES), BF16),
            pltpu.VMEM((RAYS, LANES), BF16),
            pltpu.VMEM((PEERS, PEERS), BF16),
            shape(BUNDLE, HID, dtype=BF16),
        ),
        ids_row,
        positions,
        spacing.reshape(1, SAMP),
        ray_lengths,
        target,
        cam_owner.reshape(1, RAYS),
        cam_slot.reshape(1, RAYS),
        frequencies,
        phases.reshape(1, HID),
        w_first,
        w_second,
        w_head,
        jnp.broadcast_to(core.astype(F32), (8, PEERS)),
        hbm=range(12),
        scratch=[
            pltpu.VMEM((1, SAMP), jnp.int32),
            pltpu.VMEM((3, SAMP), F32),
            pltpu.VMEM((1, SAMP), F32),
            pltpu.VMEM((1, RAYS), jnp.int32),
            pltpu.VMEM((3, RAYS), F32),
            pltpu.VMEM((1, RAYS), jnp.int32),
            pltpu.VMEM((1, RAYS), jnp.int32),
            pltpu.VMEM((3, HID), F32),
            pltpu.VMEM((1, HID), F32),
            pltpu.VMEM((1, HID, HID), BF16),
            pltpu.VMEM((1, HID, HID), BF16),
            pltpu.VMEM((1, 4, HID), BF16),
            pltpu.VMEM((PEERS, LANES), F32),
            pltpu.SemaphoreType.DMA((12,)),
        ],
    )
    same_core = [[2 * pair + core for pair in range(HALF)] for core in range(2)]
    swap = [(index, index ^ 1) for index in range(PEERS)]
    partner = lax.ppermute(bundle, "expert", swap)
    points = exchange(outgoing, groups=same_core)
    fields = call(forward_kernel, square, points, wave, bundle, partner, wide)
    returned = exchange(fields, groups=same_core)
    message = call(
        device_kernel,
        square,
        returned,
        wide,
        ray,
        hot,
        member,
        camera,
        base,
        scratch=[
            pltpu.VMEM((24, LANES), F32),
            pltpu.VMEM((PEERS, PEERS), F32),
            pltpu.VMEM((PEERS, LANES), F32),
        ],
    )
    arrived = exchange(message, groups=same_core)
    relayed = call(
        relay_kernel,
        shape(REPS * PEERS, PEERS, dtype=BF16),
        arrived,
    )
    around = [
        [rep * PEERS + 2 * pair + core for rep in range(REPS) for core in range(2)]
        for pair in range(HALF)
    ]
    rows = REPS * CAP * PEERS
    everything = exchange(relayed, ("rep", "expert"), around)
    return call(
        final_kernel,
        (
            shape(1, HID, HID),
            shape(1, HID, HID),
            shape(1, 4, HID),
            shape(36, CAM_DEV),
            shape(6, CAM_DEV),
        ),
        everything,
        wave,
        bundle,
        hbm_out=True,
        room=32,
        scratch=[
            pltpu.VMEM((1, HID, HID), F32),
            pltpu.VMEM((1, HID, HID), F32),
            pltpu.VMEM((1, 4, HID), F32),
            pltpu.VMEM((36, CAM_DEV), F32),
            pltpu.VMEM((6, CAM_DEV), F32),
            pltpu.VMEM((4, HID, PEERS), F32),
            pltpu.VMEM((48 * (CAM_DEV // LOW), REPS * CAPC * PEERS), BF16),
            pltpu.SemaphoreType.DMA((5,)),
        ],
    )


def solution(mesh):
    in_specs = (
        P(None, ("rep", "expert")),
        P(),
        P(),
        P("expert", None, None),
        P("expert", None, None),
        P("expert", None, None),
        P(("rep", "expert")),
        P(("rep", "expert"), None),
        P(("rep", "expert"), None),
        P(None, ("rep", "expert")),
        P(("rep", "expert"), None),
        P(("rep", "expert")),
    )
    out_specs = (
        P("expert", None, None),
        P("expert", None, None),
        P("expert", None, None),
        P(None, "expert"),
        P(None, "expert"),
    )
    return jax.shard_map(
        per_device, mesh=mesh, in_specs=in_specs, out_specs=out_specs, check_vma=False
    )
```

```python
import jax
import jax.numpy as jnp
from jax import lax
from jax.experimental import pallas as pl
from jax.experimental.pallas import tpu as pltpu
from jax.sharding import PartitionSpec as P

HID = 256
PEERS = 128
REPS = 4
HALF = PEERS // 2
SAMP = 192
RAYS = 96
LANES = 256
CAP = 3
CAPC = 2
CAM_DEV = 8192
LOW = 256
SLOPE_LANE = 96
BUNDLE = 2 * HID + 16
LABEL_ROW = 36
FORCE_ROW = 40
POINT_LANES = (
    *range(100, 104),
    *range(108, 112),
    *range(116, 128),
    *(38, 39, 46, 47, 86, 87, 94, 95),
)

F32 = jnp.float32
BF16 = jnp.bfloat16


def iota(shape, axis):
    return lax.broadcasted_iota(jnp.int32, shape, axis)


def dot_nn(left, right):
    return jnp.dot(left, right, preferred_element_type=F32)


def dot_nt(left, right):
    return lax.dot_general(left, right, (((1,), (1,)), ((), ())), preferred_element_type=F32)


def dot_tn(left, right):
    return lax.dot_general(left, right, (((0,), (0,)), ((), ())), preferred_element_type=F32)


def split_three(value):
    high = value.astype(BF16)
    rest = value - high.astype(F32)
    middle = rest.astype(BF16)
    low = (rest - middle.astype(F32)).astype(BF16)
    return high, middle, low


TURN = 0.15915494309189535
SINE = (
    6.283182621002197,
    -41.34142303466797,
    81.59618377685547,
    -76.5801010131836,
    41.20540237426758,
    -12.271273612976074,
)
COSINE = (
    1.0,
    -19.73920440673828,
    64.93911743164062,
    -85.45016479492188,
    60.1678466796875,
    -25.96836280822754,
    6.529670715332031,
)


def polynomial(square, terms):
    value = terms[-1]
    for term in terms[-2::-1]:
        value = value * square + term
    return value


def sine_of(turns):
    rest = turns - jnp.round(turns)
    return rest * polynomial(rest * rest, SINE)


def sin_cos(turns):
    rest = turns - jnp.round(turns)
    square = rest * rest
    return rest * polynomial(square, SINE), polynomial(square, COSINE)


def angles_of(points, slot, freq, phase):
    base = 4 * slot
    angle = freq[0:1] * points[:, base : base + 1] + freq[1:2] * points[:, base + 1 : base + 2]
    return angle + freq[2:3] * points[:, base + 2 : base + 3] + phase


def silu_pair(value):
    sig = 0.5 * jnp.tanh(0.5 * value) + 0.5
    result = value * sig
    return result, sig + result * (1.0 - sig)


def expert_rank(ids_row, width):
    hot = (iota((PEERS, width), 0) == ids_row).astype(F32)
    earlier = (iota((width, width), 0) < iota((width, width), 1)).astype(BF16)
    counts = dot_nn(hot.astype(BF16), earlier)
    rank = jnp.sum(counts * hot, axis=0, keepdims=True)
    return hot, rank


def fetch(pairs, sems):
    copies = [
        pltpu.make_async_copy(source, place, sems.at[number])
        for number, (source, place) in enumerate(pairs)
    ]
    for copy in copies:
        copy.start()
    for copy in copies:
        copy.wait()


def setup_kernel(
    ids_hbm,
    pos_hbm,
    space_hbm,
    length_hbm,
    target_hbm,
    owner_hbm,
    slot_hbm,
    freq_hbm,
    phase_hbm,
    first_hbm,
    second_hbm,
    head_hbm,
    core_ref,
    outgoing_ref,
    base_ref,
    wide_ref,
    ray_ref,
    wave_ref,
    hot_ref,
    member_ref,
    camera_ref,
    bundle_ref,
    ids_ref,
    pos_ref,
    space_ref,
    length_ref,
    target_ref,
    owner_ref,
    slot_ref,
    freq_ref,
    phase_ref,
    one_ref,
    two_ref,
    head_ref,
    rows_ref,
    sems,
):
    fetch(
        [
            (ids_hbm, ids_ref),
            (pos_hbm, pos_ref),
            (space_hbm, space_ref),
            (length_hbm, length_ref),
            (target_hbm, target_ref),
            (owner_hbm, owner_ref),
            (slot_hbm, slot_ref),
            (freq_hbm, freq_ref),
            (phase_hbm, phase_ref),
            (first_hbm, one_ref),
            (second_hbm, two_ref),
            (head_hbm, head_ref),
        ],
        sems,
    )
    bundle_ref[0:HID, :] = one_ref[0]
    bundle_ref[HID : 2 * HID, :] = two_ref[0]
    wave_ref[...] = jnp.zeros_like(wave_ref)
    wave_ref[0:3, :] = freq_ref[...]
    wave_ref[3:4, :] = phase_ref[...]
    pick = (iota((16, 4), 0) == iota((16, 4), 1)).astype(BF16)
    bundle_ref[2 * HID : BUNDLE, :] = dot_nn(pick, head_ref[0]).astype(BF16)

    wide_ref[...] = jnp.zeros_like(wide_ref)
    wide_ref[0:3, 0:SAMP] = pos_ref[...]
    wide_ref[3:4, 0:SAMP] = space_ref[...]
    wide_ref[11:12, 0:PEERS] = core_ref[0:1, :]
    wide_ref[4:5, :] = jnp.full((1, LANES), -1.0, F32)
    wide_ref[4:5, 0:SAMP] = ids_ref[...].astype(F32)
    ids = wide_ref[4:5, :].astype(jnp.int32)
    hot, rank = expert_rank(ids, LANES)
    hot = hot.astype(BF16)
    hot_ref[...] = hot
    wide_ref[4:5, :] = rank
    rows_ref[...] = jnp.zeros_like(rows_ref)
    points = wide_ref[0:3, :]
    for slot in range(CAP):
        rows_ref[4 * slot : 4 * slot + 3, :] = jnp.where(rank == float(slot), points, 0.0)
    high, middle, low = split_three(rows_ref[...])
    outgoing_ref[...] = dot_nt(hot, high) + (dot_nt(hot, middle) + dot_nt(hot, low))
    rows_ref[0:16, :] = jnp.zeros((16, LANES), F32)
    parts = [part.astype(F32) for part in split_three(points)]
    for slot in range(CAP):
        for number, part in enumerate(parts):
            kept = jnp.where(rank == float(slot), part, 0.0)
            for c in range(3):
                lane = POINT_LANES[9 * slot + 3 * number + c]
                rows_ref[lane : lane + 1, :] = kept[c : c + 1]
    base_ref[...] = dot_nt(hot, rows_ref[...].astype(BF16))

    lengths = length_ref[...].astype(F32)
    ray_a = iota((RAYS, RAYS), 0)
    ray_b = iota((RAYS, RAYS), 1)
    starts = jnp.sum(jnp.where(ray_b < ray_a, lengths, 0.0), axis=1, keepdims=True)
    ends = jnp.sum(jnp.where(ray_b <= ray_a, lengths, 0.0), axis=1, keepdims=True)
    index = iota((RAYS, LANES), 1).astype(F32)
    member = ((index >= starts) & (index < ends)).astype(BF16)
    member_ref[...] = member
    begin = jnp.sum((index == starts).astype(F32), axis=0, keepdims=True)
    near_one = 1.0 - begin
    near_two = near_one * pltpu.roll(near_one, 1, 1)
    near_three = near_two * pltpu.roll(near_one, 2, 1)
    wide_ref[5:6, :] = near_one
    wide_ref[6:7, :] = near_two
    wide_ref[7:8, :] = near_three
    targets = target_ref[...]
    high, middle, low = split_three(targets)
    wide_ref[8:11, :] = dot_nn(high, member) + (dot_nn(middle, member) + dot_nn(low, member))

    ray_ref[...] = jnp.zeros_like(ray_ref)
    ray_ref[0:3, 0:RAYS] = targets
    ray_ref[3:4, :] = jnp.full((1, PEERS), -1.0, F32)
    ray_ref[3:4, 0:RAYS] = owner_ref[...].astype(F32)
    owners = ray_ref[3:4, :].astype(jnp.int32)
    camera, camera_rank = expert_rank(owners, PEERS)
    camera_ref[...] = camera.astype(BF16)
    ray_ref[3:4, :] = camera_rank
    slots = slot_ref[...]
    ray_ref[4:5, 0:RAYS] = (slots // LOW).astype(F32)
    ray_ref[5:6, 0:RAYS] = (slots & (LOW - 1)).astype(F32)


def forward_kernel(points_ref, wave_ref, bundle_ref, partner_ref, wide_ref, out_ref):
    slopes = wave_ref[0:3, :]
    freq = slopes * TURN
    phase = wave_ref[3:4, :] * TURN
    even = wide_ref[11:12, 0:PEERS] == 0.0
    row = iota((PEERS, 16), 0)
    head_pick = ((row // 4 == iota((PEERS, 16), 1)) & (row < 16)).astype(BF16)
    head_row = iota((PEERS, HID), 0) % 4
    first_rows = points_ref[pl.ds(0, HALF, stride=2), :]
    second_rows = points_ref[pl.ds(1, HALF, stride=2), :]
    results = []
    for weights, points in (
        (bundle_ref, jnp.where(even, first_rows, second_rows)),
        (partner_ref, jnp.where(even, second_rows, first_rows)),
    ):
        first = weights[0:HID, :]
        second = weights[HID : 2 * HID, :]
        head_all = dot_nn(head_pick, weights[2 * HID : BUNDLE, :]).astype(BF16)
        angle = jnp.concatenate(
            [angles_of(points, slot, freq, phase) for slot in range(CAP)], axis=0
        )
        sine, cosine = sin_cos(angle)
        stack = [sine.astype(BF16)] + [(cosine * slopes[c : c + 1]).astype(BF16) for c in range(3)]
        one = [dot_nn(part, first) for part in stack]
        value, slope = silu_pair(one[0])
        hidden = [value.astype(BF16)] + [(one[k] * slope).astype(BF16) for k in range(1, 4)]
        two = [dot_nn(part, second) for part in hidden]
        value, slope = silu_pair(two[0])
        hidden = [value.astype(BF16)] + [(two[k] * slope).astype(BF16) for k in range(1, 4)]
        total = None
        for k in range(4):
            head = jnp.where(head_row == k, head_all, jnp.zeros_like(head_all))
            term = dot_nt(hidden[k], head)
            total = term if total is None else total + term
        packed = total[0:HALF]
        for slot in range(1, CAP):
            packed = packed + pltpu.roll(total[HALF * slot : HALF * slot + HALF], 16 * slot, 1)
        results.append(packed)
    out_ref[pl.ds(0, HALF, stride=2), :] = jnp.where(even, results[0], results[1])
    out_ref[pl.ds(1, HALF, stride=2), :] = jnp.where(even, results[1], results[0])


def device_kernel(
    fields_ref,
    wide_ref,
    ray_ref,
    hot_ref,
    member_ref,
    camera_ref,
    base_ref,
    out_ref,
    stack_ref,
    block_ref,
    samp_ref,
):
    px = wide_ref[0:1, :]
    py = wide_ref[1:2, :]
    pz = wide_ref[2:3, :]
    spacing = wide_ref[3:4, :]
    rank = wide_ref[4:5, :]
    near_one = wide_ref[5:6, :]
    near_two = wide_ref[6:7, :]
    near_three = wide_ref[7:8, :]
    hot = hot_ref[...]
    member = member_ref[...]
    turned = jnp.transpose(fields_ref[...])[0 : 16 * CAP]
    high, middle, low = split_three(turned)
    gathered = dot_nn(high, hot) + (dot_nn(middle, hot) + dot_nn(low, hot))
    fields = jnp.where(rank == 0.0, gathered[0:16], 0.0)
    for slot in range(1, CAP):
        fields = jnp.where(rank == float(slot), gathered[16 * slot : 16 * slot + 16], fields)

    def preceding(value):
        return (
            pltpu.roll(value, 1, 1) * near_one
            + pltpu.roll(value, 2, 1) * near_two
            + pltpu.roll(value, 3, 1) * near_three
        )

    def following(value):
        return (
            pltpu.roll(value * near_one, LANES - 1, 1)
            + pltpu.roll(value * near_two, LANES - 2, 1)
            + pltpu.roll(value * near_three, LANES - 3, 1)
        )

    raw = [fields[4 * o : 4 * o + 1] for o in range(4)]
    moved = [[fields[4 * o + 1 + c : 4 * o + 2 + c] for c in range(3)] for o in range(4)]
    density = jnp.maximum(raw[0], 0.0) + jnp.log1p(jnp.exp(-jnp.abs(raw[0])))
    depth = density * spacing
    through = jnp.exp(-preceding(depth))
    fade = jnp.exp(-depth)
    weight = through * (1.0 - fade)
    depth_slope = spacing * jax.nn.sigmoid(raw[0])
    along = []
    for o in range(4):
        m0, m1, m2 = moved[o]
        along.append([m2 * py - m1 * pz, m0 * pz - m2 * px, m1 * px - m0 * py, m0, m1, m2])
    stack_ref[...] = jnp.zeros_like(stack_ref)
    samp_ref[...] = jnp.zeros_like(samp_ref)
    scale = 1.0 / float(RAYS * REPS)
    slope_zero = None
    slope_rest = []
    for c in range(3):
        tint = jax.nn.sigmoid(raw[1 + c])
        share = weight * tint
        later = following(share)
        sense_zero = (through * fade * tint - later) * depth_slope
        sense_own = share * (1.0 - tint)
        miss = share + preceding(share) + later - wide_ref[8 + c : 9 + c, :]
        part = miss * sense_zero
        slope_zero = part if slope_zero is None else slope_zero + part
        slope_rest.append(scale * miss * sense_own)
        for k in range(6):
            stack_ref[8 * c + k : 8 * c + k + 1, :] = (
                sense_zero * along[0][k] + sense_own * along[1 + c][k]
            )
        stack_ref[8 * c + 6 : 8 * c + 7, :] = share
    slopes = [scale * slope_zero] + slope_rest
    for slot in range(CAP):
        for o in range(4):
            samp_ref[SLOPE_LANE + 8 * slot + o : SLOPE_LANE + 8 * slot + o + 1, :] = jnp.where(
                rank == float(slot), slopes[o], 0.0
            )

    high, middle, low = split_three(stack_ref[...])
    rays = dot_nt(high, member) + (dot_nt(middle, member) + dot_nt(low, member))
    camera_rank = ray_ref[3:4, 0:RAYS]
    blocks = []
    row = iota((8, RAYS), 0)
    for c in range(3):
        block = rays[8 * c : 8 * c + 8]
        blocks.append(jnp.where(row == 6, block - ray_ref[c : c + 1, 0:RAYS], block))
    block_ref[...] = jnp.zeros_like(block_ref)
    for a in range(6):
        outer = blocks[0][a : a + 1] * blocks[0]
        outer = outer + blocks[1][a : a + 1] * blocks[1]
        outer = outer + blocks[2][a : a + 1] * blocks[2]
        for slot in range(CAPC):
            kept = jnp.where(camera_rank == float(slot), outer, 0.0)
            base = 48 * slot
            block_ref[base + 6 * a : base + 6 * a + 6, 0:RAYS] = kept[0:6]
            block_ref[base + FORCE_ROW + a : base + FORCE_ROW + a + 1, 0:RAYS] = kept[6:7]
    for slot in range(CAPC):
        base = 48 * slot + LABEL_ROW
        block_ref[base : base + 2, 0:RAYS] = jnp.where(
            camera_rank == float(slot), ray_ref[4:6, 0:RAYS], 0.0
        )
    message = dot_nt(camera_ref[...], block_ref[...].astype(BF16))
    out_ref[...] = (message + base_ref[...]) + dot_nt(hot, samp_ref[...].astype(BF16))


def relay_kernel(got_ref, out_ref):
    for core in range(2):
        part = got_ref[pl.ds(core, HALF, stride=2), :].astype(BF16)
        for rep in range(REPS):
            row = (2 * rep + core) * HALF
            out_ref[row : row + HALF, :] = part


def final_kernel(
    got_ref,
    wave_ref,
    bundle_ref,
    grad_first_hbm,
    grad_second_hbm,
    grad_head_hbm,
    normal_hbm,
    force_hbm,
    grad_first_ref,
    grad_second_ref,
    grad_head_ref,
    normal_ref,
    force_ref,
    spread_ref,
    left_ref,
    sems,
):
    first_out, second_out, head_out, normal_out, force_out = [
        pltpu.make_async_copy(source, place, sems.at[number])
        for number, (source, place) in enumerate(
            [
                (grad_first_ref, grad_first_hbm),
                (grad_second_ref, grad_second_hbm),
                (grad_head_ref, grad_head_hbm),
                (normal_ref, normal_hbm),
                (force_ref, force_hbm),
            ]
        )
    ]

    values = []
    group = []
    low_hot = []
    turned = []
    low_lane = iota((PEERS, LOW), 1).astype(F32)
    for rep in range(REPS):
        got = got_ref[rep * PEERS : (rep + 1) * PEERS, :].astype(F32)
        flipped = jnp.transpose(got)
        turned.append(flipped)
        for slot in range(CAPC):
            base = 48 * slot
            label = base + LABEL_ROW
            values.append(flipped[base : base + 48])
            group.append(flipped[label : label + 1])
            low_hot.append((got[:, label + 1 : label + 2] == low_lane).astype(BF16))
    values = jnp.concatenate(values, axis=1)
    group = jnp.concatenate(group, axis=1)
    low_hot = jnp.concatenate(low_hot, axis=0)
    for block in range(CAM_DEV // LOW):
        left_ref[48 * block : 48 * block + 48, :] = jnp.where(
            group == float(block), values, 0.0
        ).astype(BF16)
    table = dot_nn(left_ref[...], low_hot)
    for block in range(CAM_DEV // LOW):
        base = 48 * block
        place = slice(block * LOW, (block + 1) * LOW)
        normal_ref[:, place] = table[base : base + 36]
        force_ref[:, place] = table[base + FORCE_ROW : base + FORCE_ROW + 6]
    normal_out.start()
    force_out.start()

    columns = jnp.transpose(wave_ref[...]) * TURN
    for number in range(4):
        spread_ref[number] = jnp.broadcast_to(columns[:, number : number + 1], (HID, PEERS))
    first = bundle_ref[0:HID, :]
    second = bundle_ref[HID : 2 * HID, :]
    head = bundle_ref[2 * HID : BUNDLE, :]
    grad_first = grad_second = grad_head = None
    for part in range(2):
        features = []
        slopes = []
        for rep in range(2 * part, 2 * part + 2):
            flipped = turned[rep]
            for slot in range(CAP):
                angle = None
                for c in range(3):
                    lanes = [POINT_LANES[9 * slot + 3 * number + c] for number in range(3)]
                    high, middle, low = [flipped[lane : lane + 1] for lane in lanes]
                    term = spread_ref[c] * (high + middle + low)
                    angle = term if angle is None else angle + term
                features.append(sine_of(angle + spread_ref[3]).astype(BF16))
                base = SLOPE_LANE + 8 * slot
                slopes.append(flipped[base : base + 8])
        feature = jnp.concatenate(features, axis=1)
        slopes = jnp.concatenate(slopes, axis=1)
        slopes = jnp.concatenate([slopes, jnp.zeros_like(slopes)], axis=0).astype(BF16)
        value_one, slope_one = silu_pair(dot_tn(first, feature))
        hidden_one = value_one.astype(BF16)
        value_two, slope_two = silu_pair(dot_tn(second, hidden_one))
        hidden_two = value_two.astype(BF16)
        back_two = (dot_tn(head, slopes) * slope_two).astype(BF16)
        back_one = (dot_nn(second, back_two) * slope_one).astype(BF16)
        terms = (
            dot_nt(feature, back_one),
            dot_nt(hidden_one, back_two),
            dot_nt(slopes, hidden_two),
        )
        if part == 0:
            grad_first, grad_second, grad_head = terms
        else:
            grad_head_ref[0] = (grad_head + terms[2])[0:4]
            head_out.start()
            grad_second_ref[0] = grad_second + terms[1]
            second_out.start()
            grad_first_ref[0] = grad_first + terms[0]
            first_out.start()
    for copy in (normal_out, force_out, head_out, second_out, first_out):
        copy.wait()


def call(kernel, out_shape, *args, hbm=(), hbm_out=False, scratch=(), room=8):
    def spec(number):
        return pl.BlockSpec(memory_space=pltpu.HBM if number in hbm else pltpu.VMEM)

    place = pltpu.HBM if hbm_out else pltpu.VMEM
    args = [
        pltpu.with_memory_space_constraint(arg, pltpu.HBM) if number in hbm else arg
        for number, arg in enumerate(args)
    ]
    return pl.pallas_call(
        kernel,
        out_shape=out_shape,
        in_specs=[spec(number) for number in range(len(args))],
        out_specs=jax.tree.map(lambda _: pl.BlockSpec(memory_space=place), out_shape),
        scratch_shapes=list(scratch),
        compiler_params=pltpu.CompilerParams(vmem_limit_bytes=room * 1024 * 1024),
    )(*args)


def shape(*dims, dtype=F32):
    return jax.ShapeDtypeStruct(dims, dtype)


def exchange(value, axes="expert", groups=None):
    return lax.all_to_all(
        value, axes, split_axis=0, concat_axis=0, tiled=True, axis_index_groups=groups
    )


def per_device(
    positions,
    frequencies,
    phases,
    w_first,
    w_second,
    w_head,
    spacing,
    expert_ids,
    ray_lengths,
    target,
    cam_owner,
    cam_slot,
):
    ids_row = expert_ids.reshape(1, SAMP)
    square = shape(PEERS, PEERS)
    core = lax.axis_index("expert") & 1
    outgoing, base, wide, ray, wave, hot, member, camera, bundle = call(
        setup_kernel,
        (
            square,
            pltpu.VMEM((PEERS, PEERS), F32),
            pltpu.VMEM((16, LANES), F32),
            pltpu.VMEM((8, PEERS), F32),
            pltpu.VMEM((8, HID), F32),
            pltpu.VMEM((PEERS, LANES), BF16),
            pltpu.VMEM((RAYS, LANES), BF16),
            pltpu.VMEM((PEERS, PEERS), BF16),
            shape(BUNDLE, HID, dtype=BF16),
        ),
        ids_row,
        positions,
        spacing.reshape(1, SAMP),
        ray_lengths,
        target,
        cam_owner.reshape(1, RAYS),
        cam_slot.reshape(1, RAYS),
        frequencies,
        phases.reshape(1, HID),
        w_first,
        w_second,
        w_head,
        jnp.broadcast_to(core.astype(F32), (8, PEERS)),
        hbm=range(12),
        scratch=[
            pltpu.VMEM((1, SAMP), jnp.int32),
            pltpu.VMEM((3, SAMP), F32),
            pltpu.VMEM((1, SAMP), F32),
            pltpu.VMEM((1, RAYS), jnp.int32),
            pltpu.VMEM((3, RAYS), F32),
            pltpu.VMEM((1, RAYS), jnp.int32),
            pltpu.VMEM((1, RAYS), jnp.int32),
            pltpu.VMEM((3, HID), F32),
            pltpu.VMEM((1, HID), F32),
            pltpu.VMEM((1, HID, HID), BF16),
            pltpu.VMEM((1, HID, HID), BF16),
            pltpu.VMEM((1, 4, HID), BF16),
            pltpu.VMEM((PEERS, LANES), F32),
            pltpu.SemaphoreType.DMA((12,)),
        ],
    )
    same_core = [[2 * pair + core for pair in range(HALF)] for core in range(2)]
    swap = [(index, index ^ 1) for index in range(PEERS)]
    partner = lax.ppermute(bundle, "expert", swap)
    points = exchange(outgoing, groups=same_core)
    fields = call(forward_kernel, square, points, wave, bundle, partner, wide)
    returned = exchange(fields, groups=same_core)
    message = call(
        device_kernel,
        square,
        returned,
        wide,
        ray,
        hot,
        member,
        camera,
        base,
        scratch=[
            pltpu.VMEM((24, LANES), F32),
            pltpu.VMEM((PEERS, PEERS), F32),
            pltpu.VMEM((PEERS, LANES), F32),
        ],
    )
    arrived = exchange(message, groups=same_core)
    relayed = call(
        relay_kernel,
        shape(REPS * PEERS, PEERS, dtype=BF16),
        arrived,
    )
    around = [
        [rep * PEERS + 2 * pair + core for rep in range(REPS) for core in range(2)]
        for pair in range(HALF)
    ]
    rows = REPS * CAP * PEERS
    everything = exchange(relayed, ("rep", "expert"), around)
    return call(
        final_kernel,
        (
            shape(1, HID, HID),
            shape(1, HID, HID),
            shape(1, 4, HID),
            shape(36, CAM_DEV),
            shape(6, CAM_DEV),
        ),
        everything,
        wave,
        bundle,
        hbm_out=True,
        room=32,
        scratch=[
            pltpu.VMEM((1, HID, HID), F32),
            pltpu.VMEM((1, HID, HID), F32),
            pltpu.VMEM((1, 4, HID), F32),
            pltpu.VMEM((36, CAM_DEV), F32),
            pltpu.VMEM((6, CAM_DEV), F32),
            pltpu.VMEM((4, HID, PEERS), F32),
            pltpu.VMEM((48 * (CAM_DEV // LOW), REPS * CAPC * PEERS), BF16),
            pltpu.SemaphoreType.DMA((5,)),
        ],
    )


def solution(mesh):
    in_specs = (
        P(None, ("rep", "expert")),
        P(),
        P(),
        P("expert", None, None),
        P("expert", None, None),
        P("expert", None, None),
        P(("rep", "expert")),
        P(("rep", "expert"), None),
        P(("rep", "expert"), None),
        P(None, ("rep", "expert")),
        P(("rep", "expert"), None),
        P(("rep", "expert")),
    )
    out_specs = (
        P("expert", None, None),
        P("expert", None, None),
        P("expert", None, None),
        P(None, "expert"),
        P(None, "expert"),
    )
    return jax.shard_map(
        per_device, mesh=mesh, in_specs=in_specs, out_specs=out_specs, check_vma=False
    )
```

```python
import jax
import jax.numpy as jnp
from jax import lax
from jax.experimental import pallas as pl
from jax.experimental.pallas import tpu as pltpu
from jax.sharding import PartitionSpec as P

HID = 256
PEERS = 128
REPS = 4
HALF = PEERS // 2
SAMP = 192
RAYS = 96
LANES = 256
CAP = 3
CAPC = 2
CAM_DEV = 8192
LOW = 256
SLOPE_LANE = 96
BUNDLE = 2 * HID + 16
LABEL_ROW = 36
FORCE_ROW = 40
POINT_LANES = (
    *range(100, 104),
    *range(108, 112),
    *range(116, 128),
    *(38, 39, 46, 47, 86, 87, 94, 95),
)

F32 = jnp.float32
BF16 = jnp.bfloat16


def iota(shape, axis):
    return lax.broadcasted_iota(jnp.int32, shape, axis)


def dot_nn(left, right):
    return jnp.dot(left, right, preferred_element_type=F32)


def dot_nt(left, right):
    return lax.dot_general(left, right, (((1,), (1,)), ((), ())), preferred_element_type=F32)


def dot_tn(left, right):
    return lax.dot_general(left, right, (((0,), (0,)), ((), ())), preferred_element_type=F32)


def split_three(value):
    high = value.astype(BF16)
    rest = value - high.astype(F32)
    middle = rest.astype(BF16)
    low = (rest - middle.astype(F32)).astype(BF16)
    return high, middle, low


TURN = 0.15915494309189535
SINE = (
    6.283182621002197,
    -41.34142303466797,
    81.59618377685547,
    -76.5801010131836,
    41.20540237426758,
    -12.271273612976074,
)
COSINE = (
    1.0,
    -19.73920440673828,
    64.93911743164062,
    -85.45016479492188,
    60.1678466796875,
    -25.96836280822754,
    6.529670715332031,
)


def polynomial(square, terms):
    value = terms[-1]
    for term in terms[-2::-1]:
        value = value * square + term
    return value


def sine_of(turns):
    rest = turns - jnp.round(turns)
    return rest * polynomial(rest * rest, SINE)


def sin_cos(turns):
    rest = turns - jnp.round(turns)
    square = rest * rest
    return rest * polynomial(square, SINE), polynomial(square, COSINE)


def angles_of(points, slot, freq, phase):
    base = 4 * slot
    angle = freq[0:1] * points[:, base : base + 1] + freq[1:2] * points[:, base + 1 : base + 2]
    return angle + freq[2:3] * points[:, base + 2 : base + 3] + phase


def silu_pair(value):
    sig = 0.5 * jnp.tanh(0.5 * value) + 0.5
    result = value * sig
    return result, sig + result * (1.0 - sig)


def expert_rank(ids_row, width):
    hot = (iota((PEERS, width), 0) == ids_row).astype(F32)
    earlier = (iota((width, width), 0) < iota((width, width), 1)).astype(BF16)
    counts = dot_nn(hot.astype(BF16), earlier)
    rank = jnp.sum(counts * hot, axis=0, keepdims=True)
    return hot, rank


def fetch(pairs, sems):
    copies = [
        pltpu.make_async_copy(source, place, sems.at[number])
        for number, (source, place) in enumerate(pairs)
    ]
    for copy in copies:
        copy.start()
    for copy in copies:
        copy.wait()


def prep_kernel(ids_hbm, pos_hbm, out_ref, ids_ref, pos_ref, rows_ref, sems):
    rows_ref[...] = jnp.zeros_like(rows_ref)
    fetch([(ids_hbm, ids_ref), (pos_hbm, pos_ref)], sems)
    hot, rank = expert_rank(ids_ref[...], SAMP)
    for number, part in enumerate(split_three(pos_ref[...])):
        part = part.astype(F32)
        for slot in range(CAP):
            row = 16 * number + 4 * slot
            rows_ref[row : row + 3, :] = jnp.where(rank == float(slot), part, 0.0)
    out_ref[...] = dot_nt(hot.astype(BF16), rows_ref[...].astype(BF16))


def setup_kernel(
    ids_hbm,
    pos_hbm,
    space_hbm,
    length_hbm,
    target_hbm,
    owner_hbm,
    slot_hbm,
    freq_hbm,
    phase_hbm,
    first_hbm,
    second_hbm,
    head_hbm,
    after_hbm,
    base_ref,
    wide_ref,
    ray_ref,
    wave_ref,
    hot_ref,
    member_ref,
    camera_ref,
    bundle_ref,
    ids_ref,
    pos_ref,
    space_ref,
    length_ref,
    target_ref,
    owner_ref,
    slot_ref,
    freq_ref,
    phase_ref,
    one_ref,
    two_ref,
    head_ref,
    rows_ref,
    sems,
):
    fetch(
        [
            (ids_hbm, ids_ref),
            (pos_hbm, pos_ref),
            (space_hbm, space_ref),
            (length_hbm, length_ref),
            (target_hbm, target_ref),
            (owner_hbm, owner_ref),
            (slot_hbm, slot_ref),
            (freq_hbm, freq_ref),
            (phase_hbm, phase_ref),
            (first_hbm, one_ref),
            (second_hbm, two_ref),
            (head_hbm, head_ref),
        ],
        sems,
    )
    bundle_ref[0:HID, :] = one_ref[0]
    bundle_ref[HID : 2 * HID, :] = two_ref[0]
    wave_ref[...] = jnp.zeros_like(wave_ref)
    wave_ref[0:3, :] = freq_ref[...]
    wave_ref[3:4, :] = phase_ref[...]
    pick = (iota((16, 4), 0) == iota((16, 4), 1)).astype(BF16)
    bundle_ref[2 * HID : BUNDLE, :] = dot_nn(pick, head_ref[0]).astype(BF16)

    wide_ref[...] = jnp.zeros_like(wide_ref)
    wide_ref[0:3, 0:SAMP] = pos_ref[...]
    wide_ref[3:4, 0:SAMP] = space_ref[...]
    wide_ref[4:5, :] = jnp.full((1, LANES), -1.0, F32)
    wide_ref[4:5, 0:SAMP] = ids_ref[...].astype(F32)
    ids = wide_ref[4:5, :].astype(jnp.int32)
    hot, rank = expert_rank(ids, LANES)
    hot = hot.astype(BF16)
    hot_ref[...] = hot
    wide_ref[4:5, :] = rank
    rows_ref[...] = jnp.zeros_like(rows_ref)
    points = wide_ref[0:3, :]
    parts = [part.astype(F32) for part in split_three(points)]
    for slot in range(CAP):
        for number, part in enumerate(parts):
            kept = jnp.where(rank == float(slot), part, 0.0)
            for c in range(3):
                lane = POINT_LANES[9 * slot + 3 * number + c]
                rows_ref[lane : lane + 1, :] = kept[c : c + 1]
    base_ref[...] = dot_nt(hot, rows_ref[...].astype(BF16))

    lengths = length_ref[...].astype(F32)
    ray_a = iota((RAYS, RAYS), 0)
    ray_b = iota((RAYS, RAYS), 1)
    starts = jnp.sum(jnp.where(ray_b < ray_a, lengths, 0.0), axis=1, keepdims=True)
    ends = jnp.sum(jnp.where(ray_b <= ray_a, lengths, 0.0), axis=1, keepdims=True)
    index = iota((RAYS, LANES), 1).astype(F32)
    member = ((index >= starts) & (index < ends)).astype(BF16)
    member_ref[...] = member
    begin = jnp.sum((index == starts).astype(F32), axis=0, keepdims=True)
    near_one = 1.0 - begin
    near_two = near_one * pltpu.roll(near_one, 1, 1)
    near_three = near_two * pltpu.roll(near_one, 2, 1)
    wide_ref[5:6, :] = near_one
    wide_ref[6:7, :] = near_two
    wide_ref[7:8, :] = near_three
    targets = target_ref[...]
    high, middle, low = split_three(targets)
    wide_ref[8:11, :] = dot_nn(high, member) + (dot_nn(middle, member) + dot_nn(low, member))

    ray_ref[...] = jnp.zeros_like(ray_ref)
    ray_ref[0:3, 0:RAYS] = targets
    ray_ref[3:4, :] = jnp.full((1, PEERS), -1.0, F32)
    ray_ref[3:4, 0:RAYS] = owner_ref[...].astype(F32)
    owners = ray_ref[3:4, :].astype(jnp.int32)
    camera, camera_rank = expert_rank(owners, PEERS)
    camera_ref[...] = camera.astype(BF16)
    ray_ref[3:4, :] = camera_rank
    slots = slot_ref[...]
    ray_ref[4:5, 0:RAYS] = (slots // LOW).astype(F32)
    ray_ref[5:6, 0:RAYS] = (slots & (LOW - 1)).astype(F32)


def joined(parts):
    return parts + (pltpu.roll(parts, PEERS - 16, 1) + pltpu.roll(parts, PEERS - 32, 1))


def forward_kernel(points_ref, wave_ref, both_ref, out_ref):
    slopes = wave_ref[0:3, :]
    freq = slopes * TURN
    phase = wave_ref[3:4, :] * TURN
    row = iota((PEERS, 16), 0)
    head_pick = ((row // 4 == iota((PEERS, 16), 1)) & (row < 16)).astype(BF16)
    head_row = iota((PEERS, HID), 0) % 4
    for core in range(2):
        points = joined(points_ref[pl.ds(core, HALF, stride=2), :])
        start = BUNDLE * core
        first = both_ref[start : start + HID, :]
        second = both_ref[start + HID : start + 2 * HID, :]
        head_all = dot_nn(head_pick, both_ref[start + 2 * HID : start + BUNDLE, :]).astype(BF16)
        angle = jnp.concatenate(
            [angles_of(points, slot, freq, phase) for slot in range(CAP)], axis=0
        )
        sine, cosine = sin_cos(angle)
        stack = [sine.astype(BF16)] + [(cosine * slopes[c : c + 1]).astype(BF16) for c in range(3)]
        one = [dot_nn(part, first) for part in stack]
        value, slope = silu_pair(one[0])
        hidden = [value.astype(BF16)] + [(one[k] * slope).astype(BF16) for k in range(1, 4)]
        two = [dot_nn(part, second) for part in hidden]
        value, slope = silu_pair(two[0])
        hidden = [value.astype(BF16)] + [(two[k] * slope).astype(BF16) for k in range(1, 4)]
        total = None
        for k in range(4):
            head = jnp.where(head_row == k, head_all, jnp.zeros_like(head_all))
            term = dot_nt(hidden[k], head)
            total = term if total is None else total + term
        packed = total[0:HALF]
        for slot in range(1, CAP):
            packed = packed + pltpu.roll(total[HALF * slot : HALF * slot + HALF], 16 * slot, 1)
        out_ref[pl.ds(core, HALF, stride=2), :] = packed


def device_kernel(
    fields_ref,
    wide_ref,
    ray_ref,
    hot_ref,
    member_ref,
    camera_ref,
    base_ref,
    out_ref,
    stack_ref,
    block_ref,
    samp_ref,
):
    px = wide_ref[0:1, :]
    py = wide_ref[1:2, :]
    pz = wide_ref[2:3, :]
    spacing = wide_ref[3:4, :]
    rank = wide_ref[4:5, :]
    near_one = wide_ref[5:6, :]
    near_two = wide_ref[6:7, :]
    near_three = wide_ref[7:8, :]
    hot = hot_ref[...]
    member = member_ref[...]
    turned = jnp.transpose(fields_ref[...])[0 : 16 * CAP]
    high, middle, low = split_three(turned)
    gathered = dot_nn(high, hot) + (dot_nn(middle, hot) + dot_nn(low, hot))
    fields = jnp.where(rank == 0.0, gathered[0:16], 0.0)
    for slot in range(1, CAP):
        fields = jnp.where(rank == float(slot), gathered[16 * slot : 16 * slot + 16], fields)

    def preceding(value):
        return (
            pltpu.roll(value, 1, 1) * near_one
            + pltpu.roll(value, 2, 1) * near_two
            + pltpu.roll(value, 3, 1) * near_three
        )

    def following(value):
        return (
            pltpu.roll(value * near_one, LANES - 1, 1)
            + pltpu.roll(value * near_two, LANES - 2, 1)
            + pltpu.roll(value * near_three, LANES - 3, 1)
        )

    raw = [fields[4 * o : 4 * o + 1] for o in range(4)]
    moved = [[fields[4 * o + 1 + c : 4 * o + 2 + c] for c in range(3)] for o in range(4)]
    density = jnp.maximum(raw[0], 0.0) + jnp.log1p(jnp.exp(-jnp.abs(raw[0])))
    depth = density * spacing
    through = jnp.exp(-preceding(depth))
    fade = jnp.exp(-depth)
    weight = through * (1.0 - fade)
    depth_slope = spacing * jax.nn.sigmoid(raw[0])
    along = []
    for o in range(4):
        m0, m1, m2 = moved[o]
        along.append([m2 * py - m1 * pz, m0 * pz - m2 * px, m1 * px - m0 * py, m0, m1, m2])
    stack_ref[...] = jnp.zeros_like(stack_ref)
    samp_ref[...] = jnp.zeros_like(samp_ref)
    scale = 1.0 / float(RAYS * REPS)
    slope_zero = None
    slope_rest = []
    for c in range(3):
        tint = jax.nn.sigmoid(raw[1 + c])
        share = weight * tint
        later = following(share)
        sense_zero = (through * fade * tint - later) * depth_slope
        sense_own = share * (1.0 - tint)
        miss = share + preceding(share) + later - wide_ref[8 + c : 9 + c, :]
        part = miss * sense_zero
        slope_zero = part if slope_zero is None else slope_zero + part
        slope_rest.append(scale * miss * sense_own)
        for k in range(6):
            stack_ref[8 * c + k : 8 * c + k + 1, :] = (
                sense_zero * along[0][k] + sense_own * along[1 + c][k]
            )
        stack_ref[8 * c + 6 : 8 * c + 7, :] = share
    slopes = [scale * slope_zero] + slope_rest
    for slot in range(CAP):
        for o in range(4):
            samp_ref[SLOPE_LANE + 8 * slot + o : SLOPE_LANE + 8 * slot + o + 1, :] = jnp.where(
                rank == float(slot), slopes[o], 0.0
            )

    high, middle, low = split_three(stack_ref[...])
    rays = dot_nt(high, member) + (dot_nt(middle, member) + dot_nt(low, member))
    camera_rank = ray_ref[3:4, 0:RAYS]
    blocks = []
    row = iota((8, RAYS), 0)
    for c in range(3):
        block = rays[8 * c : 8 * c + 8]
        blocks.append(jnp.where(row == 6, block - ray_ref[c : c + 1, 0:RAYS], block))
    block_ref[...] = jnp.zeros_like(block_ref)
    for a in range(6):
        outer = blocks[0][a : a + 1] * blocks[0]
        outer = outer + blocks[1][a : a + 1] * blocks[1]
        outer = outer + blocks[2][a : a + 1] * blocks[2]
        for slot in range(CAPC):
            kept = jnp.where(camera_rank == float(slot), outer, 0.0)
            base = 48 * slot
            block_ref[base + 6 * a : base + 6 * a + 6, 0:RAYS] = kept[0:6]
            block_ref[base + FORCE_ROW + a : base + FORCE_ROW + a + 1, 0:RAYS] = kept[6:7]
    for slot in range(CAPC):
        base = 48 * slot + LABEL_ROW
        block_ref[base : base + 2, 0:RAYS] = jnp.where(
            camera_rank == float(slot), ray_ref[4:6, 0:RAYS], 0.0
        )
    message = dot_nt(camera_ref[...], block_ref[...].astype(BF16))
    out_ref[...] = (message + base_ref[...]) + dot_nt(hot, samp_ref[...].astype(BF16))


def relay_kernel(got_ref, out_ref):
    for core in range(2):
        part = got_ref[pl.ds(core, HALF, stride=2), :].astype(BF16)
        for rep in range(REPS):
            row = (2 * rep + core) * HALF
            out_ref[row : row + HALF, :] = part


def final_kernel(
    got_ref,
    wave_ref,
    bundle_ref,
    grad_first_hbm,
    grad_second_hbm,
    grad_head_hbm,
    normal_hbm,
    force_hbm,
    grad_first_ref,
    grad_second_ref,
    grad_head_ref,
    normal_ref,
    force_ref,
    spread_ref,
    left_ref,
    sems,
):
    first_out, second_out, head_out, normal_out, force_out = [
        pltpu.make_async_copy(source, place, sems.at[number])
        for number, (source, place) in enumerate(
            [
                (grad_first_ref, grad_first_hbm),
                (grad_second_ref, grad_second_hbm),
                (grad_head_ref, grad_head_hbm),
                (normal_ref, normal_hbm),
                (force_ref, force_hbm),
            ]
        )
    ]

    values = []
    group = []
    low_hot = []
    turned = []
    low_lane = iota((PEERS, LOW), 1).astype(F32)
    for rep in range(REPS):
        got = got_ref[rep * PEERS : (rep + 1) * PEERS, :].astype(F32)
        flipped = jnp.transpose(got)
        turned.append(flipped)
        for slot in range(CAPC):
            base = 48 * slot
            label = base + LABEL_ROW
            values.append(flipped[base : base + 48])
            group.append(flipped[label : label + 1])
            low_hot.append((got[:, label + 1 : label + 2] == low_lane).astype(BF16))
    values = jnp.concatenate(values, axis=1)
    group = jnp.concatenate(group, axis=1)
    low_hot = jnp.concatenate(low_hot, axis=0)
    for block in range(CAM_DEV // LOW):
        left_ref[48 * block : 48 * block + 48, :] = jnp.where(
            group == float(block), values, 0.0
        ).astype(BF16)
    table = dot_nn(left_ref[...], low_hot)
    for block in range(CAM_DEV // LOW):
        base = 48 * block
        place = slice(block * LOW, (block + 1) * LOW)
        normal_ref[:, place] = table[base : base + 36]
        force_ref[:, place] = table[base + FORCE_ROW : base + FORCE_ROW + 6]
    normal_out.start()
    force_out.start()

    columns = jnp.transpose(wave_ref[...]) * TURN
    for number in range(4):
        spread_ref[number] = jnp.broadcast_to(columns[:, number : number + 1], (HID, PEERS))
    first = bundle_ref[0:HID, :]
    second = bundle_ref[HID : 2 * HID, :]
    head = bundle_ref[2 * HID : BUNDLE, :]
    grad_first = grad_second = grad_head = None
    for part in range(2):
        features = []
        slopes = []
        for rep in range(2 * part, 2 * part + 2):
            flipped = turned[rep]
            for slot in range(CAP):
                angle = None
                for c in range(3):
                    lanes = [POINT_LANES[9 * slot + 3 * number + c] for number in range(3)]
                    high, middle, low = [flipped[lane : lane + 1] for lane in lanes]
                    term = spread_ref[c] * (high + middle + low)
                    angle = term if angle is None else angle + term
                features.append(sine_of(angle + spread_ref[3]).astype(BF16))
                base = SLOPE_LANE + 8 * slot
                slopes.append(flipped[base : base + 8])
        feature = jnp.concatenate(features, axis=1)
        slopes = jnp.concatenate(slopes, axis=1)
        slopes = jnp.concatenate([slopes, jnp.zeros_like(slopes)], axis=0).astype(BF16)
        value_one, slope_one = silu_pair(dot_tn(first, feature))
        hidden_one = value_one.astype(BF16)
        value_two, slope_two = silu_pair(dot_tn(second, hidden_one))
        hidden_two = value_two.astype(BF16)
        back_two = (dot_tn(head, slopes) * slope_two).astype(BF16)
        back_one = (dot_nn(second, back_two) * slope_one).astype(BF16)
        terms = (
            dot_nt(feature, back_one),
            dot_nt(hidden_one, back_two),
            dot_nt(slopes, hidden_two),
        )
        if part == 0:
            grad_first, grad_second, grad_head = terms
        else:
            grad_head_ref[0] = (grad_head + terms[2])[0:4]
            head_out.start()
            grad_second_ref[0] = grad_second + terms[1]
            second_out.start()
            grad_first_ref[0] = grad_first + terms[0]
            first_out.start()
    for copy in (normal_out, force_out, head_out, second_out, first_out):
        copy.wait()


def call(kernel, out_shape, *args, hbm=(), unread=(), hbm_out=False, scratch=(), cost=0, room=8):
    def spec(number):
        if number in unread:
            return pl.BlockSpec(memory_space=pl.ANY)
        return pl.BlockSpec(memory_space=pltpu.HBM if number in hbm else pltpu.VMEM)

    place = pltpu.HBM if hbm_out else pltpu.VMEM
    args = [
        pltpu.with_memory_space_constraint(arg, pltpu.HBM) if number in hbm else arg
        for number, arg in enumerate(args)
    ]
    estimate = pl.CostEstimate(flops=cost, transcendentals=0, bytes_accessed=1 << 20)
    return pl.pallas_call(
        kernel,
        out_shape=out_shape,
        cost_estimate=estimate if cost else None,
        in_specs=[spec(number) for number in range(len(args))],
        out_specs=jax.tree.map(lambda _: pl.BlockSpec(memory_space=place), out_shape),
        scratch_shapes=list(scratch),
        compiler_params=pltpu.CompilerParams(vmem_limit_bytes=room * 1024 * 1024),
    )(*args)


def shape(*dims, dtype=F32):
    return jax.ShapeDtypeStruct(dims, dtype)


def exchange(value, axes="expert", groups=None):
    return lax.all_to_all(
        value, axes, split_axis=0, concat_axis=0, tiled=True, axis_index_groups=groups
    )


def per_device(
    positions,
    frequencies,
    phases,
    w_first,
    w_second,
    w_head,
    spacing,
    expert_ids,
    ray_lengths,
    target,
    cam_owner,
    cam_slot,
):
    ids_row = expert_ids.reshape(1, SAMP)
    square = shape(PEERS, PEERS)
    outgoing = call(
        prep_kernel,
        square,
        ids_row,
        positions,
        hbm=(0, 1),
        scratch=[
            pltpu.VMEM((1, SAMP), jnp.int32),
            pltpu.VMEM((3, SAMP), F32),
            pltpu.VMEM((PEERS, SAMP), F32),
            pltpu.SemaphoreType.DMA((2,)),
        ],
    )
    base, wide, ray, wave, hot, member, camera, bundle = call(
        setup_kernel,
        (
            pltpu.VMEM((PEERS, PEERS), F32),
            pltpu.VMEM((16, LANES), F32),
            pltpu.VMEM((8, PEERS), F32),
            pltpu.VMEM((8, HID), F32),
            pltpu.VMEM((PEERS, LANES), BF16),
            pltpu.VMEM((RAYS, LANES), BF16),
            pltpu.VMEM((PEERS, PEERS), BF16),
            shape(BUNDLE, HID, dtype=BF16),
        ),
        ids_row,
        positions,
        spacing.reshape(1, SAMP),
        ray_lengths,
        target,
        cam_owner.reshape(1, RAYS),
        cam_slot.reshape(1, RAYS),
        frequencies,
        phases.reshape(1, HID),
        w_first,
        w_second,
        w_head,
        outgoing,
        hbm=range(12),
        unread=(12,),
        cost=1 << 33,
        scratch=[
            pltpu.VMEM((1, SAMP), jnp.int32),
            pltpu.VMEM((3, SAMP), F32),
            pltpu.VMEM((1, SAMP), F32),
            pltpu.VMEM((1, RAYS), jnp.int32),
            pltpu.VMEM((3, RAYS), F32),
            pltpu.VMEM((1, RAYS), jnp.int32),
            pltpu.VMEM((1, RAYS), jnp.int32),
            pltpu.VMEM((3, HID), F32),
            pltpu.VMEM((1, HID), F32),
            pltpu.VMEM((1, HID, HID), BF16),
            pltpu.VMEM((1, HID, HID), BF16),
            pltpu.VMEM((1, 4, HID), BF16),
            pltpu.VMEM((PEERS, LANES), F32),
            pltpu.SemaphoreType.DMA((12,)),
        ],
    )
    same_core = [[2 * pair + core for pair in range(HALF)] for core in range(2)]
    chips = [[2 * pair, 2 * pair + 1] for pair in range(HALF)]
    both = lax.all_gather(bundle, "expert", axis=0, tiled=True, axis_index_groups=chips)
    points = exchange(outgoing, groups=same_core)
    fields = call(forward_kernel, square, points, wave, both)
    returned = exchange(fields, groups=same_core)
    message = call(
        device_kernel,
        square,
        returned,
        wide,
        ray,
        hot,
        member,
        camera,
        base,
        scratch=[
            pltpu.VMEM((24, LANES), F32),
            pltpu.VMEM((PEERS, PEERS), F32),
            pltpu.VMEM((PEERS, LANES), F32),
        ],
    )
    arrived = exchange(message, groups=same_core)
    relayed = call(
        relay_kernel,
        shape(REPS * PEERS, PEERS, dtype=BF16),
        arrived,
    )
    around = [
        [rep * PEERS + 2 * pair + core for rep in range(REPS) for core in range(2)]
        for pair in range(HALF)
    ]
    rows = REPS * CAP * PEERS
    everything = exchange(relayed, ("rep", "expert"), around)
    return call(
        final_kernel,
        (
            shape(1, HID, HID),
            shape(1, HID, HID),
            shape(1, 4, HID),
            shape(36, CAM_DEV),
            shape(6, CAM_DEV),
        ),
        everything,
        wave,
        bundle,
        hbm_out=True,
        room=32,
        scratch=[
            pltpu.VMEM((1, HID, HID), F32),
            pltpu.VMEM((1, HID, HID), F32),
            pltpu.VMEM((1, 4, HID), F32),
            pltpu.VMEM((36, CAM_DEV), F32),
            pltpu.VMEM((6, CAM_DEV), F32),
            pltpu.VMEM((4, HID, PEERS), F32),
            pltpu.VMEM((48 * (CAM_DEV // LOW), REPS * CAPC * PEERS), BF16),
            pltpu.SemaphoreType.DMA((5,)),
        ],
    )


def solution(mesh):
    in_specs = (
        P(None, ("rep", "expert")),
        P(),
        P(),
        P("expert", None, None),
        P("expert", None, None),
        P("expert", None, None),
        P(("rep", "expert")),
        P(("rep", "expert"), None),
        P(("rep", "expert"), None),
        P(None, ("rep", "expert")),
        P(("rep", "expert"), None),
        P(("rep", "expert")),
    )
    out_specs = (
        P("expert", None, None),
        P("expert", None, None),
        P("expert", None, None),
        P(None, "expert"),
        P(None, "expert"),
    )
    return jax.shard_map(
        per_device, mesh=mesh, in_specs=in_specs, out_specs=out_specs, check_vma=False
    )
```

```python
import jax
import jax.numpy as jnp
from jax import lax
from jax.experimental import pallas as pl
from jax.experimental.pallas import tpu as pltpu
from jax.sharding import PartitionSpec as P

HID = 256
PEERS = 128
REPS = 4
HALF = PEERS // 2
SAMP = 192
RAYS = 96
LANES = 256
CAP = 3
CAPC = 2
CAM_DEV = 8192
LOW = 256
SLOPE_LANE = 96
BUNDLE = 2 * HID + 16
LABEL_ROW = 36
FORCE_ROW = 40
POINT_LANES = (
    *range(100, 104),
    *range(108, 112),
    *range(116, 128),
    *(38, 39, 46, 47, 86, 87, 94, 95),
)

F32 = jnp.float32
BF16 = jnp.bfloat16


def iota(shape, axis):
    return lax.broadcasted_iota(jnp.int32, shape, axis)


def dot_nn(left, right):
    return jnp.dot(left, right, preferred_element_type=F32)


def dot_nt(left, right):
    return lax.dot_general(left, right, (((1,), (1,)), ((), ())), preferred_element_type=F32)


def dot_tn(left, right):
    return lax.dot_general(left, right, (((0,), (0,)), ((), ())), preferred_element_type=F32)


def split_three(value):
    high = value.astype(BF16)
    rest = value - high.astype(F32)
    middle = rest.astype(BF16)
    low = (rest - middle.astype(F32)).astype(BF16)
    return high, middle, low


TURN = 0.15915494309189535
SINE = (
    6.283182621002197,
    -41.34142303466797,
    81.59618377685547,
    -76.5801010131836,
    41.20540237426758,
    -12.271273612976074,
)
COSINE = (
    1.0,
    -19.73920440673828,
    64.93911743164062,
    -85.45016479492188,
    60.1678466796875,
    -25.96836280822754,
    6.529670715332031,
)


def polynomial(square, terms):
    value = terms[-1]
    for term in terms[-2::-1]:
        value = value * square + term
    return value


def sine_of(turns):
    rest = turns - jnp.round(turns)
    return rest * polynomial(rest * rest, SINE)


def sin_cos(turns):
    rest = turns - jnp.round(turns)
    square = rest * rest
    return rest * polynomial(square, SINE), polynomial(square, COSINE)


def angles_of(points, slot, freq, phase):
    base = 4 * slot
    angle = freq[0:1] * points[:, base : base + 1] + freq[1:2] * points[:, base + 1 : base + 2]
    return angle + freq[2:3] * points[:, base + 2 : base + 3] + phase


def silu_pair(value):
    sig = 0.5 * jnp.tanh(0.5 * value) + 0.5
    result = value * sig
    return result, sig + result * (1.0 - sig)


def expert_rank(ids_row, width):
    hot = (iota((PEERS, width), 0) == ids_row).astype(F32)
    earlier = (iota((width, width), 0) < iota((width, width), 1)).astype(BF16)
    counts = dot_nn(hot.astype(BF16), earlier)
    rank = jnp.sum(counts * hot, axis=0, keepdims=True)
    return hot, rank


def fetch(pairs, sems):
    copies = [
        pltpu.make_async_copy(source, place, sems.at[number])
        for number, (source, place) in enumerate(pairs)
    ]
    for copy in copies:
        copy.start()
    for copy in copies:
        copy.wait()


def prep_kernel(ids_hbm, pos_hbm, out_ref, ids_ref, pos_ref, rows_ref, sems):
    rows_ref[...] = jnp.zeros_like(rows_ref)
    fetch([(ids_hbm, ids_ref), (pos_hbm, pos_ref)], sems)
    hot, rank = expert_rank(ids_ref[...], SAMP)
    for number, part in enumerate(split_three(pos_ref[...])):
        part = part.astype(F32)
        for slot in range(CAP):
            row = 16 * number + 4 * slot
            rows_ref[row : row + 3, :] = jnp.where(rank == float(slot), part, 0.0)
    out_ref[...] = dot_nt(hot.astype(BF16), rows_ref[...].astype(BF16)).astype(BF16)


def setup_kernel(
    ids_hbm,
    pos_hbm,
    space_hbm,
    length_hbm,
    target_hbm,
    owner_hbm,
    slot_hbm,
    freq_hbm,
    phase_hbm,
    first_hbm,
    second_hbm,
    head_hbm,
    after_hbm,
    base_ref,
    wide_ref,
    ray_ref,
    wave_ref,
    hot_ref,
    member_ref,
    camera_ref,
    bundle_ref,
    ids_ref,
    pos_ref,
    space_ref,
    length_ref,
    target_ref,
    owner_ref,
    slot_ref,
    freq_ref,
    phase_ref,
    one_ref,
    two_ref,
    head_ref,
    rows_ref,
    sems,
):
    fetch(
        [
            (ids_hbm, ids_ref),
            (pos_hbm, pos_ref),
            (space_hbm, space_ref),
            (length_hbm, length_ref),
            (target_hbm, target_ref),
            (owner_hbm, owner_ref),
            (slot_hbm, slot_ref),
            (freq_hbm, freq_ref),
            (phase_hbm, phase_ref),
            (first_hbm, one_ref),
            (second_hbm, two_ref),
            (head_hbm, head_ref),
        ],
        sems,
    )
    bundle_ref[0:HID, :] = one_ref[0]
    bundle_ref[HID : 2 * HID, :] = two_ref[0]
    wave_ref[...] = jnp.zeros_like(wave_ref)
    wave_ref[0:3, :] = freq_ref[...]
    wave_ref[3:4, :] = phase_ref[...]
    pick = (iota((16, 4), 0) == iota((16, 4), 1)).astype(BF16)
    bundle_ref[2 * HID : BUNDLE, :] = dot_nn(pick, head_ref[0]).astype(BF16)

    wide_ref[...] = jnp.zeros_like(wide_ref)
    wide_ref[0:3, 0:SAMP] = pos_ref[...]
    wide_ref[3:4, 0:SAMP] = space_ref[...]
    wide_ref[4:5, :] = jnp.full((1, LANES), -1.0, F32)
    wide_ref[4:5, 0:SAMP] = ids_ref[...].astype(F32)
    ids = wide_ref[4:5, :].astype(jnp.int32)
    hot, rank = expert_rank(ids, LANES)
    hot = hot.astype(BF16)
    hot_ref[...] = hot
    wide_ref[4:5, :] = rank
    rows_ref[...] = jnp.zeros_like(rows_ref)
    points = wide_ref[0:3, :]
    parts = [part.astype(F32) for part in split_three(points)]
    for slot in range(CAP):
        for number, part in enumerate(parts):
            kept = jnp.where(rank == float(slot), part, 0.0)
            for c in range(3):
                lane = POINT_LANES[9 * slot + 3 * number + c]
                rows_ref[lane : lane + 1, :] = kept[c : c + 1]
    base_ref[...] = dot_nt(hot, rows_ref[...].astype(BF16))

    lengths = length_ref[...].astype(F32)
    ray_a = iota((RAYS, RAYS), 0)
    ray_b = iota((RAYS, RAYS), 1)
    starts = jnp.sum(jnp.where(ray_b < ray_a, lengths, 0.0), axis=1, keepdims=True)
    ends = jnp.sum(jnp.where(ray_b <= ray_a, lengths, 0.0), axis=1, keepdims=True)
    index = iota((RAYS, LANES), 1).astype(F32)
    member = ((index >= starts) & (index < ends)).astype(BF16)
    member_ref[...] = member
    begin = jnp.sum((index == starts).astype(F32), axis=0, keepdims=True)
    near_one = 1.0 - begin
    near_two = near_one * pltpu.roll(near_one, 1, 1)
    near_three = near_two * pltpu.roll(near_one, 2, 1)
    wide_ref[5:6, :] = near_one
    wide_ref[6:7, :] = near_two
    wide_ref[7:8, :] = near_three
    targets = target_ref[...]
    high, middle, low = split_three(targets)
    wide_ref[8:11, :] = dot_nn(high, member) + (dot_nn(middle, member) + dot_nn(low, member))

    ray_ref[...] = jnp.zeros_like(ray_ref)
    ray_ref[0:3, 0:RAYS] = targets
    ray_ref[3:4, :] = jnp.full((1, PEERS), -1.0, F32)
    ray_ref[3:4, 0:RAYS] = owner_ref[...].astype(F32)
    owners = ray_ref[3:4, :].astype(jnp.int32)
    camera, camera_rank = expert_rank(owners, PEERS)
    camera_ref[...] = camera.astype(BF16)
    ray_ref[3:4, :] = camera_rank
    slots = slot_ref[...]
    ray_ref[4:5, 0:RAYS] = (slots // LOW).astype(F32)
    ray_ref[5:6, 0:RAYS] = (slots & (LOW - 1)).astype(F32)


def joined(parts):
    return parts + (pltpu.roll(parts, PEERS - 16, 1) + pltpu.roll(parts, PEERS - 32, 1))


def forward_kernel(points_ref, wave_ref, both_ref, out_ref, wide_ref, made_ref):
    wide_ref[...] = points_ref[...].astype(F32)
    slopes = wave_ref[0:3, :]
    freq = slopes * TURN
    phase = wave_ref[3:4, :] * TURN
    row = iota((PEERS, 16), 0)
    head_pick = ((row // 4 == iota((PEERS, 16), 1)) & (row < 16)).astype(BF16)
    head_row = iota((PEERS, HID), 0) % 4
    for core in range(2):
        points = joined(wide_ref[pl.ds(core, HALF, stride=2), :])
        start = BUNDLE * core
        first = both_ref[start : start + HID, :]
        second = both_ref[start + HID : start + 2 * HID, :]
        head_all = dot_nn(head_pick, both_ref[start + 2 * HID : start + BUNDLE, :]).astype(BF16)
        angle = jnp.concatenate(
            [angles_of(points, slot, freq, phase) for slot in range(CAP)], axis=0
        )
        sine, cosine = sin_cos(angle)
        stack = [sine.astype(BF16)] + [(cosine * slopes[c : c + 1]).astype(BF16) for c in range(3)]
        one = [dot_nn(part, first) for part in stack]
        value, slope = silu_pair(one[0])
        hidden = [value.astype(BF16)] + [(one[k] * slope).astype(BF16) for k in range(1, 4)]
        two = [dot_nn(part, second) for part in hidden]
        value, slope = silu_pair(two[0])
        hidden = [value.astype(BF16)] + [(two[k] * slope).astype(BF16) for k in range(1, 4)]
        total = None
        for k in range(4):
            head = jnp.where(head_row == k, head_all, jnp.zeros_like(head_all))
            term = dot_nt(hidden[k], head)
            total = term if total is None else total + term
        packed = total[0:HALF]
        for slot in range(1, CAP):
            packed = packed + pltpu.roll(total[HALF * slot : HALF * slot + HALF], 16 * slot, 1)
        high = packed.astype(BF16).astype(F32)
        low = (packed - high).astype(BF16).astype(F32)
        made_ref[pl.ds(core, HALF, stride=2), :] = high + pltpu.roll(low, HALF, 1)
    out_ref[...] = made_ref[...].astype(BF16)


def device_kernel(
    fields_ref,
    wide_ref,
    ray_ref,
    hot_ref,
    member_ref,
    camera_ref,
    base_ref,
    out_ref,
    stack_ref,
    block_ref,
    samp_ref,
):
    px = wide_ref[0:1, :]
    py = wide_ref[1:2, :]
    pz = wide_ref[2:3, :]
    spacing = wide_ref[3:4, :]
    rank = wide_ref[4:5, :]
    near_one = wide_ref[5:6, :]
    near_two = wide_ref[6:7, :]
    near_three = wide_ref[7:8, :]
    hot = hot_ref[...]
    member = member_ref[...]
    turned = jnp.transpose(fields_ref[...].astype(F32)).astype(BF16)
    gathered = dot_nn(turned[0:HALF], hot) + dot_nn(turned[HALF:PEERS], hot)
    fields = jnp.where(rank == 0.0, gathered[0:16], 0.0)
    for slot in range(1, CAP):
        fields = jnp.where(rank == float(slot), gathered[16 * slot : 16 * slot + 16], fields)

    def preceding(value):
        return (
            pltpu.roll(value, 1, 1) * near_one
            + pltpu.roll(value, 2, 1) * near_two
            + pltpu.roll(value, 3, 1) * near_three
        )

    def following(value):
        return (
            pltpu.roll(value * near_one, LANES - 1, 1)
            + pltpu.roll(value * near_two, LANES - 2, 1)
            + pltpu.roll(value * near_three, LANES - 3, 1)
        )

    raw = [fields[4 * o : 4 * o + 1] for o in range(4)]
    moved = [[fields[4 * o + 1 + c : 4 * o + 2 + c] for c in range(3)] for o in range(4)]
    density = jnp.maximum(raw[0], 0.0) + jnp.log1p(jnp.exp(-jnp.abs(raw[0])))
    depth = density * spacing
    through = jnp.exp(-preceding(depth))
    fade = jnp.exp(-depth)
    weight = through * (1.0 - fade)
    depth_slope = spacing * jax.nn.sigmoid(raw[0])
    along = []
    for o in range(4):
        m0, m1, m2 = moved[o]
        along.append([m2 * py - m1 * pz, m0 * pz - m2 * px, m1 * px - m0 * py, m0, m1, m2])
    stack_ref[...] = jnp.zeros_like(stack_ref)
    samp_ref[...] = jnp.zeros_like(samp_ref)
    scale = 1.0 / float(RAYS * REPS)
    slope_zero = None
    slope_rest = []
    for c in range(3):
        tint = jax.nn.sigmoid(raw[1 + c])
        share = weight * tint
        later = following(share)
        sense_zero = (through * fade * tint - later) * depth_slope
        sense_own = share * (1.0 - tint)
        miss = share + preceding(share) + later - wide_ref[8 + c : 9 + c, :]
        part = miss * sense_zero
        slope_zero = part if slope_zero is None else slope_zero + part
        slope_rest.append(scale * miss * sense_own)
        for k in range(6):
            stack_ref[8 * c + k : 8 * c + k + 1, :] = (
                sense_zero * along[0][k] + sense_own * along[1 + c][k]
            )
        stack_ref[8 * c + 6 : 8 * c + 7, :] = share
    slopes = [scale * slope_zero] + slope_rest
    for slot in range(CAP):
        for o in range(4):
            samp_ref[SLOPE_LANE + 8 * slot + o : SLOPE_LANE + 8 * slot + o + 1, :] = jnp.where(
                rank == float(slot), slopes[o], 0.0
            )

    high, middle, low = split_three(stack_ref[...])
    rays = dot_nt(high, member) + (dot_nt(middle, member) + dot_nt(low, member))
    camera_rank = ray_ref[3:4, 0:RAYS]
    blocks = []
    row = iota((8, RAYS), 0)
    for c in range(3):
        block = rays[8 * c : 8 * c + 8]
        blocks.append(jnp.where(row == 6, block - ray_ref[c : c + 1, 0:RAYS], block))
    block_ref[...] = jnp.zeros_like(block_ref)
    for a in range(6):
        outer = blocks[0][a : a + 1] * blocks[0]
        outer = outer + blocks[1][a : a + 1] * blocks[1]
        outer = outer + blocks[2][a : a + 1] * blocks[2]
        for slot in range(CAPC):
            kept = jnp.where(camera_rank == float(slot), outer, 0.0)
            base = 48 * slot
            block_ref[base + 6 * a : base + 6 * a + 6, 0:RAYS] = kept[0:6]
            block_ref[base + FORCE_ROW + a : base + FORCE_ROW + a + 1, 0:RAYS] = kept[6:7]
    for slot in range(CAPC):
        base = 48 * slot + LABEL_ROW
        block_ref[base : base + 2, 0:RAYS] = jnp.where(
            camera_rank == float(slot), ray_ref[4:6, 0:RAYS], 0.0
        )
    message = dot_nt(camera_ref[...], block_ref[...].astype(BF16))
    message = (message + base_ref[...]) + dot_nt(hot, samp_ref[...].astype(BF16))
    out_ref[...] = message.astype(BF16)


def relay_kernel(got_ref, out_ref, wide_ref):
    wide_ref[...] = got_ref[...].astype(F32)
    for core in range(2):
        part = wide_ref[pl.ds(core, HALF, stride=2), :].astype(BF16)
        for rep in range(REPS):
            row = (2 * rep + core) * HALF
            out_ref[row : row + HALF, :] = part


def final_kernel(
    got_ref,
    wave_ref,
    bundle_ref,
    grad_first_hbm,
    grad_second_hbm,
    grad_head_hbm,
    normal_hbm,
    force_hbm,
    grad_first_ref,
    grad_second_ref,
    grad_head_ref,
    normal_ref,
    force_ref,
    spread_ref,
    left_ref,
    sems,
):
    first_out, second_out, head_out, normal_out, force_out = [
        pltpu.make_async_copy(source, place, sems.at[number])
        for number, (source, place) in enumerate(
            [
                (grad_first_ref, grad_first_hbm),
                (grad_second_ref, grad_second_hbm),
                (grad_head_ref, grad_head_hbm),
                (normal_ref, normal_hbm),
                (force_ref, force_hbm),
            ]
        )
    ]

    values = []
    group = []
    low_hot = []
    turned = []
    low_lane = iota((PEERS, LOW), 1).astype(F32)
    for rep in range(REPS):
        got = got_ref[rep * PEERS : (rep + 1) * PEERS, :].astype(F32)
        flipped = jnp.transpose(got)
        turned.append(flipped)
        for slot in range(CAPC):
            base = 48 * slot
            label = base + LABEL_ROW
            values.append(flipped[base : base + 48])
            group.append(flipped[label : label + 1])
            low_hot.append((got[:, label + 1 : label + 2] == low_lane).astype(BF16))
    values = jnp.concatenate(values, axis=1)
    group = jnp.concatenate(group, axis=1)
    low_hot = jnp.concatenate(low_hot, axis=0)
    for block in range(CAM_DEV // LOW):
        left_ref[48 * block : 48 * block + 48, :] = jnp.where(
            group == float(block), values, 0.0
        ).astype(BF16)
    table = dot_nn(left_ref[...], low_hot)
    for block in range(CAM_DEV // LOW):
        base = 48 * block
        place = slice(block * LOW, (block + 1) * LOW)
        normal_ref[:, place] = table[base : base + 36]
        force_ref[:, place] = table[base + FORCE_ROW : base + FORCE_ROW + 6]
    normal_out.start()
    force_out.start()

    columns = jnp.transpose(wave_ref[...]) * TURN
    for number in range(4):
        spread_ref[number] = jnp.broadcast_to(columns[:, number : number + 1], (HID, PEERS))
    first = bundle_ref[0:HID, :]
    second = bundle_ref[HID : 2 * HID, :]
    head = bundle_ref[2 * HID : BUNDLE, :]
    kept = []
    grad_head = None
    for part in range(2):
        features = []
        slopes = []
        for rep in range(2 * part, 2 * part + 2):
            flipped = turned[rep]
            for slot in range(CAP):
                angle = None
                for c in range(3):
                    lanes = [POINT_LANES[9 * slot + 3 * number + c] for number in range(3)]
                    high, middle, low = [flipped[lane : lane + 1] for lane in lanes]
                    term = spread_ref[c] * (high + middle + low)
                    angle = term if angle is None else angle + term
                features.append(sine_of(angle + spread_ref[3]).astype(BF16))
                base = SLOPE_LANE + 8 * slot
                slopes.append(flipped[base : base + 8])
        feature = jnp.concatenate(features, axis=1)
        slopes = jnp.concatenate(slopes, axis=1)
        slopes = jnp.concatenate([slopes, jnp.zeros_like(slopes)], axis=0).astype(BF16)
        value_one, slope_one = silu_pair(dot_tn(first, feature))
        hidden_one = value_one.astype(BF16)
        value_two, slope_two = silu_pair(dot_tn(second, hidden_one))
        hidden_two = value_two.astype(BF16)
        back_two = (dot_tn(head, slopes) * slope_two).astype(BF16)
        back_one = (dot_nn(second, back_two) * slope_one).astype(BF16)
        kept.append((feature, back_one, hidden_one, back_two))
        term = dot_nt(slopes, hidden_two)
        grad_head = term if grad_head is None else grad_head + term
    feature, back_one, hidden_one, back_two = [
        jnp.concatenate(pair, axis=1) for pair in zip(*kept)
    ]
    grad_head_ref[0] = grad_head[0:4]
    head_out.start()
    grad_second_ref[0] = dot_nt(hidden_one, back_two)
    second_out.start()
    grad_first_ref[0] = dot_nt(feature, back_one)
    first_out.start()
    for copy in (normal_out, force_out, head_out, second_out, first_out):
        copy.wait()


def call(kernel, out_shape, *args, hbm=(), unread=(), hbm_out=False, scratch=(), cost=0, room=8):
    def spec(number):
        if number in unread:
            return pl.BlockSpec(memory_space=pl.ANY)
        return pl.BlockSpec(memory_space=pltpu.HBM if number in hbm else pltpu.VMEM)

    place = pltpu.HBM if hbm_out else pltpu.VMEM
    args = [
        pltpu.with_memory_space_constraint(arg, pltpu.HBM) if number in hbm else arg
        for number, arg in enumerate(args)
    ]
    estimate = pl.CostEstimate(flops=cost, transcendentals=0, bytes_accessed=1 << 20)
    return pl.pallas_call(
        kernel,
        out_shape=out_shape,
        cost_estimate=estimate if cost else None,
        in_specs=[spec(number) for number in range(len(args))],
        out_specs=jax.tree.map(lambda _: pl.BlockSpec(memory_space=place), out_shape),
        scratch_shapes=list(scratch),
        compiler_params=pltpu.CompilerParams(vmem_limit_bytes=room * 1024 * 1024),
    )(*args)


def shape(*dims, dtype=F32):
    return jax.ShapeDtypeStruct(dims, dtype)


def exchange(value, axes="expert", groups=None):
    return lax.all_to_all(
        value, axes, split_axis=0, concat_axis=0, tiled=True, axis_index_groups=groups
    )


def per_device(
    positions,
    frequencies,
    phases,
    w_first,
    w_second,
    w_head,
    spacing,
    expert_ids,
    ray_lengths,
    target,
    cam_owner,
    cam_slot,
):
    ids_row = expert_ids.reshape(1, SAMP)
    square = shape(PEERS, PEERS, dtype=BF16)
    room = pltpu.VMEM((PEERS, PEERS), F32)
    outgoing = call(
        prep_kernel,
        square,
        ids_row,
        positions,
        hbm=(0, 1),
        scratch=[
            pltpu.VMEM((1, SAMP), jnp.int32),
            pltpu.VMEM((3, SAMP), F32),
            pltpu.VMEM((PEERS, SAMP), F32),
            pltpu.SemaphoreType.DMA((2,)),
        ],
    )
    base, wide, ray, wave, hot, member, camera, bundle = call(
        setup_kernel,
        (
            pltpu.VMEM((PEERS, PEERS), F32),
            pltpu.VMEM((16, LANES), F32),
            pltpu.VMEM((8, PEERS), F32),
            pltpu.VMEM((8, HID), F32),
            pltpu.VMEM((PEERS, LANES), BF16),
            pltpu.VMEM((RAYS, LANES), BF16),
            pltpu.VMEM((PEERS, PEERS), BF16),
            shape(BUNDLE, HID, dtype=BF16),
        ),
        ids_row,
        positions,
        spacing.reshape(1, SAMP),
        ray_lengths,
        target,
        cam_owner.reshape(1, RAYS),
        cam_slot.reshape(1, RAYS),
        frequencies,
        phases.reshape(1, HID),
        w_first,
        w_second,
        w_head,
        outgoing,
        hbm=range(12),
        unread=(12,),
        cost=1 << 33,
        scratch=[
            pltpu.VMEM((1, SAMP), jnp.int32),
            pltpu.VMEM((3, SAMP), F32),
            pltpu.VMEM((1, SAMP), F32),
            pltpu.VMEM((1, RAYS), jnp.int32),
            pltpu.VMEM((3, RAYS), F32),
            pltpu.VMEM((1, RAYS), jnp.int32),
            pltpu.VMEM((1, RAYS), jnp.int32),
            pltpu.VMEM((3, HID), F32),
            pltpu.VMEM((1, HID), F32),
            pltpu.VMEM((1, HID, HID), BF16),
            pltpu.VMEM((1, HID, HID), BF16),
            pltpu.VMEM((1, 4, HID), BF16),
            pltpu.VMEM((PEERS, LANES), F32),
            pltpu.SemaphoreType.DMA((12,)),
        ],
    )
    same_core = [[2 * pair + core for pair in range(HALF)] for core in range(2)]
    chips = [[2 * pair, 2 * pair + 1] for pair in range(HALF)]
    both = lax.all_gather(bundle, "expert", axis=0, tiled=True, axis_index_groups=chips)
    points = exchange(outgoing, groups=same_core)
    fields = call(forward_kernel, square, points, wave, both, scratch=[room, room])
    returned = exchange(fields, groups=same_core)
    message = call(
        device_kernel,
        square,
        returned,
        wide,
        ray,
        hot,
        member,
        camera,
        base,
        scratch=[
            pltpu.VMEM((24, LANES), F32),
            pltpu.VMEM((PEERS, PEERS), F32),
            pltpu.VMEM((PEERS, LANES), F32),
        ],
    )
    arrived = exchange(message, groups=same_core)
    relayed = call(
        relay_kernel,
        shape(REPS * PEERS, PEERS, dtype=BF16),
        arrived,
        scratch=[room],
    )
    around = [
        [rep * PEERS + 2 * pair + core for rep in range(REPS) for core in range(2)]
        for pair in range(HALF)
    ]
    rows = REPS * CAP * PEERS
    everything = exchange(relayed, ("rep", "expert"), around)
    return call(
        final_kernel,
        (
            shape(1, HID, HID),
            shape(1, HID, HID),
            shape(1, 4, HID),
            shape(36, CAM_DEV),
            shape(6, CAM_DEV),
        ),
        everything,
        wave,
        bundle,
        hbm_out=True,
        room=32,
        scratch=[
            pltpu.VMEM((1, HID, HID), F32),
            pltpu.VMEM((1, HID, HID), F32),
            pltpu.VMEM((1, 4, HID), F32),
            pltpu.VMEM((36, CAM_DEV), F32),
            pltpu.VMEM((6, CAM_DEV), F32),
            pltpu.VMEM((4, HID, PEERS), F32),
            pltpu.VMEM((48 * (CAM_DEV // LOW), REPS * CAPC * PEERS), BF16),
            pltpu.SemaphoreType.DMA((5,)),
        ],
    )


def solution(mesh):
    in_specs = (
        P(None, ("rep", "expert")),
        P(),
        P(),
        P("expert", None, None),
        P("expert", None, None),
        P("expert", None, None),
        P(("rep", "expert")),
        P(("rep", "expert"), None),
        P(("rep", "expert"), None),
        P(None, ("rep", "expert")),
        P(("rep", "expert"), None),
        P(("rep", "expert")),
    )
    out_specs = (
        P("expert", None, None),
        P("expert", None, None),
        P("expert", None, None),
        P(None, "expert"),
        P(None, "expert"),
    )
    return jax.shard_map(
        per_device, mesh=mesh, in_specs=in_specs, out_specs=out_specs, check_vma=False
    )
```

```python
import jax
import jax.numpy as jnp
from jax import lax
from jax.experimental import pallas as pl
from jax.experimental.pallas import tpu as pltpu
from jax.sharding import PartitionSpec as P

HID = 256
PEERS = 128
REPS = 4
HALF = PEERS // 2
SAMP = 192
RAYS = 96
LANES = 256
CAP = 3
CAPC = 2
CAM_DEV = 8192
LOW = 256
SLOPE_LANE = 96
BUNDLE = 2 * HID + 16
LABEL_ROW = 36
FORCE_ROW = 40
POINT_LANES = (
    *range(100, 104),
    *range(108, 112),
    *range(116, 128),
    *(38, 39, 46, 47, 86, 87, 94, 95),
)

F32 = jnp.float32
BF16 = jnp.bfloat16


def iota(shape, axis):
    return lax.broadcasted_iota(jnp.int32, shape, axis)


def dot_nn(left, right):
    return jnp.dot(left, right, preferred_element_type=F32)


def dot_nt(left, right):
    return lax.dot_general(left, right, (((1,), (1,)), ((), ())), preferred_element_type=F32)


def dot_tn(left, right):
    return lax.dot_general(left, right, (((0,), (0,)), ((), ())), preferred_element_type=F32)


def split_three(value):
    high = value.astype(BF16)
    rest = value - high.astype(F32)
    middle = rest.astype(BF16)
    low = (rest - middle.astype(F32)).astype(BF16)
    return high, middle, low


TURN = 0.15915494309189535
SINE = (
    6.283182621002197,
    -41.34142303466797,
    81.59618377685547,
    -76.5801010131836,
    41.20540237426758,
    -12.271273612976074,
)
COSINE = (
    1.0,
    -19.73920440673828,
    64.93911743164062,
    -85.45016479492188,
    60.1678466796875,
    -25.96836280822754,
    6.529670715332031,
)


def polynomial(square, terms):
    value = terms[-1]
    for term in terms[-2::-1]:
        value = value * square + term
    return value


def sine_of(turns):
    rest = turns - jnp.round(turns)
    return rest * polynomial(rest * rest, SINE)


def sin_cos(turns):
    rest = turns - jnp.round(turns)
    square = rest * rest
    return rest * polynomial(square, SINE), polynomial(square, COSINE)


def angles_of(points, slot, freq, phase):
    base = 4 * slot
    angle = freq[0:1] * points[:, base : base + 1] + freq[1:2] * points[:, base + 1 : base + 2]
    return angle + freq[2:3] * points[:, base + 2 : base + 3] + phase


def silu_pair(value):
    sig = 0.5 * jnp.tanh(0.5 * value) + 0.5
    result = value * sig
    return result, sig + result * (1.0 - sig)


def expert_rank(ids_row, width):
    hot = (iota((PEERS, width), 0) == ids_row).astype(F32)
    earlier = (iota((width, width), 0) < iota((width, width), 1)).astype(BF16)
    counts = dot_nn(hot.astype(BF16), earlier)
    rank = jnp.sum(counts * hot, axis=0, keepdims=True)
    return hot, rank


def prep_kernel(*refs):
    sources, (out_ref, *places), (rows_ref, sems) = refs[:12], refs[12:25], refs[25:]
    copies = [
        pltpu.make_async_copy(source, place, sems.at[number])
        for number, (source, place) in enumerate(zip(sources, places))
    ]
    for copy in copies:
        copy.start()
    rows_ref[...] = jnp.zeros_like(rows_ref)
    copies[0].wait()
    copies[1].wait()
    ids_ref, pos_ref = places[:2]
    hot, rank = expert_rank(ids_ref[...], SAMP)
    for number, part in enumerate(split_three(pos_ref[...])):
        part = part.astype(F32)
        for slot in range(CAP):
            row = 16 * number + 4 * slot
            rows_ref[row : row + 3, :] = jnp.where(rank == float(slot), part, 0.0)
    out_ref[...] = dot_nt(hot.astype(BF16), rows_ref[...].astype(BF16)).astype(BF16)
    for copy in copies[2:]:
        copy.wait()


def setup_kernel(
    ids_ref,
    pos_ref,
    space_ref,
    length_ref,
    target_ref,
    owner_ref,
    slot_ref,
    freq_ref,
    phase_ref,
    one_ref,
    two_ref,
    head_ref,
    base_ref,
    wide_ref,
    ray_ref,
    wave_ref,
    hot_ref,
    member_ref,
    camera_ref,
    bundle_ref,
    rows_ref,
):
    bundle_ref[0:HID, :] = one_ref[0]
    bundle_ref[HID : 2 * HID, :] = two_ref[0]
    wave_ref[...] = jnp.zeros_like(wave_ref)
    wave_ref[0:3, :] = freq_ref[...]
    wave_ref[3:4, :] = phase_ref[...]
    pick = (iota((16, 4), 0) == iota((16, 4), 1)).astype(BF16)
    bundle_ref[2 * HID : BUNDLE, :] = dot_nn(pick, head_ref[0]).astype(BF16)

    wide_ref[...] = jnp.zeros_like(wide_ref)
    wide_ref[0:3, 0:SAMP] = pos_ref[...]
    wide_ref[3:4, 0:SAMP] = space_ref[...]
    wide_ref[4:5, :] = jnp.full((1, LANES), -1.0, F32)
    wide_ref[4:5, 0:SAMP] = ids_ref[...].astype(F32)
    ids = wide_ref[4:5, :].astype(jnp.int32)
    hot, rank = expert_rank(ids, LANES)
    hot = hot.astype(BF16)
    hot_ref[...] = hot
    wide_ref[4:5, :] = rank
    rows_ref[...] = jnp.zeros_like(rows_ref)
    points = wide_ref[0:3, :]
    parts = [part.astype(F32) for part in split_three(points)]
    for slot in range(CAP):
        for number, part in enumerate(parts):
            kept = jnp.where(rank == float(slot), part, 0.0)
            for c in range(3):
                lane = POINT_LANES[9 * slot + 3 * number + c]
                rows_ref[lane : lane + 1, :] = kept[c : c + 1]
    base_ref[...] = dot_nt(hot, rows_ref[...].astype(BF16))

    lengths = length_ref[...].astype(F32)
    ray_a = iota((RAYS, RAYS), 0)
    ray_b = iota((RAYS, RAYS), 1)
    starts = jnp.sum(jnp.where(ray_b < ray_a, lengths, 0.0), axis=1, keepdims=True)
    ends = jnp.sum(jnp.where(ray_b <= ray_a, lengths, 0.0), axis=1, keepdims=True)
    index = iota((RAYS, LANES), 1).astype(F32)
    member = ((index >= starts) & (index < ends)).astype(BF16)
    member_ref[...] = member
    begin = jnp.sum((index == starts).astype(F32), axis=0, keepdims=True)
    near_one = 1.0 - begin
    near_two = near_one * pltpu.roll(near_one, 1, 1)
    near_three = near_two * pltpu.roll(near_one, 2, 1)
    wide_ref[5:6, :] = near_one
    wide_ref[6:7, :] = near_two
    wide_ref[7:8, :] = near_three
    targets = target_ref[...]
    high, middle, low = split_three(targets)
    wide_ref[8:11, :] = dot_nn(high, member) + (dot_nn(middle, member) + dot_nn(low, member))

    ray_ref[...] = jnp.zeros_like(ray_ref)
    ray_ref[0:3, 0:RAYS] = targets
    ray_ref[3:4, :] = jnp.full((1, PEERS), -1.0, F32)
    ray_ref[3:4, 0:RAYS] = owner_ref[...].astype(F32)
    owners = ray_ref[3:4, :].astype(jnp.int32)
    camera, camera_rank = expert_rank(owners, PEERS)
    camera_ref[...] = camera.astype(BF16)
    ray_ref[3:4, :] = camera_rank
    slots = slot_ref[...]
    ray_ref[4:5, 0:RAYS] = (slots // LOW).astype(F32)
    ray_ref[5:6, 0:RAYS] = (slots & (LOW - 1)).astype(F32)


def joined(parts):
    return parts + (pltpu.roll(parts, PEERS - 16, 1) + pltpu.roll(parts, PEERS - 32, 1))


def forward_kernel(points_ref, wave_ref, both_ref, out_ref, wide_ref, made_ref):
    wide_ref[...] = points_ref[...].astype(F32)
    slopes = wave_ref[0:3, :]
    freq = slopes * TURN
    phase = wave_ref[3:4, :] * TURN
    row = iota((PEERS, 16), 0)
    head_pick = ((row // 4 == iota((PEERS, 16), 1)) & (row < 16)).astype(BF16)
    head_row = iota((PEERS, HID), 0) % 4
    for core in range(2):
        points = joined(wide_ref[pl.ds(core, HALF, stride=2), :])
        start = BUNDLE * core
        first = both_ref[start : start + HID, :]
        second = both_ref[start + HID : start + 2 * HID, :]
        head_all = dot_nn(head_pick, both_ref[start + 2 * HID : start + BUNDLE, :]).astype(BF16)
        angle = jnp.concatenate(
            [angles_of(points, slot, freq, phase) for slot in range(CAP)], axis=0
        )
        sine, cosine = sin_cos(angle)
        stack = [sine.astype(BF16)] + [(cosine * slopes[c : c + 1]).astype(BF16) for c in range(3)]
        count = CAP * HALF
        one = dot_nn(jnp.concatenate(stack, axis=0), first)
        one = [one[count * k : count * k + count] for k in range(4)]
        value, slope = silu_pair(one[0])
        hidden = [value.astype(BF16)] + [(one[k] * slope).astype(BF16) for k in range(1, 4)]
        two = dot_nn(jnp.concatenate(hidden, axis=0), second)
        two = [two[count * k : count * k + count] for k in range(4)]
        value, slope = silu_pair(two[0])
        hidden = [value.astype(BF16)] + [(two[k] * slope).astype(BF16) for k in range(1, 4)]
        heads = [jnp.where(head_row == k, head_all, jnp.zeros_like(head_all)) for k in range(4)]
        total = dot_nt(jnp.concatenate(hidden, axis=1), jnp.concatenate(heads, axis=1))
        packed = total[0:HALF]
        for slot in range(1, CAP):
            packed = packed + pltpu.roll(total[HALF * slot : HALF * slot + HALF], 16 * slot, 1)
        high = packed.astype(BF16).astype(F32)
        low = (packed - high).astype(BF16).astype(F32)
        made_ref[pl.ds(core, HALF, stride=2), :] = high + pltpu.roll(low, HALF, 1)
    out_ref[...] = made_ref[...].astype(BF16)


def device_kernel(
    fields_ref,
    wide_ref,
    ray_ref,
    hot_ref,
    member_ref,
    camera_ref,
    base_ref,
    out_ref,
    stack_ref,
    block_ref,
    samp_ref,
):
    px = wide_ref[0:1, :]
    py = wide_ref[1:2, :]
    pz = wide_ref[2:3, :]
    spacing = wide_ref[3:4, :]
    rank = wide_ref[4:5, :]
    near_one = wide_ref[5:6, :]
    near_two = wide_ref[6:7, :]
    near_three = wide_ref[7:8, :]
    hot = hot_ref[...]
    member = member_ref[...]
    turned = jnp.transpose(fields_ref[...].astype(F32)).astype(BF16)
    gathered = dot_nn(turned[0:HALF], hot) + dot_nn(turned[HALF:PEERS], hot)
    fields = jnp.where(rank == 0.0, gathered[0:16], 0.0)
    for slot in range(1, CAP):
        fields = jnp.where(rank == float(slot), gathered[16 * slot : 16 * slot + 16], fields)

    def preceding(value):
        return (
            pltpu.roll(value, 1, 1) * near_one
            + pltpu.roll(value, 2, 1) * near_two
            + pltpu.roll(value, 3, 1) * near_three
        )

    def following(value):
        return (
            pltpu.roll(value * near_one, LANES - 1, 1)
            + pltpu.roll(value * near_two, LANES - 2, 1)
            + pltpu.roll(value * near_three, LANES - 3, 1)
        )

    raw = [fields[4 * o : 4 * o + 1] for o in range(4)]
    moved = [[fields[4 * o + 1 + c : 4 * o + 2 + c] for c in range(3)] for o in range(4)]
    density = jnp.maximum(raw[0], 0.0) + jnp.log1p(jnp.exp(-jnp.abs(raw[0])))
    depth = density * spacing
    through = jnp.exp(-preceding(depth))
    fade = jnp.exp(-depth)
    weight = through * (1.0 - fade)
    depth_slope = spacing * jax.nn.sigmoid(raw[0])
    along = []
    for o in range(4):
        m0, m1, m2 = moved[o]
        along.append([m2 * py - m1 * pz, m0 * pz - m2 * px, m1 * px - m0 * py, m0, m1, m2])
    stack_ref[...] = jnp.zeros_like(stack_ref)
    samp_ref[...] = jnp.zeros_like(samp_ref)
    scale = 1.0 / float(RAYS * REPS)
    slope_zero = None
    slope_rest = []
    for c in range(3):
        tint = jax.nn.sigmoid(raw[1 + c])
        share = weight * tint
        later = following(share)
        sense_zero = (through * fade * tint - later) * depth_slope
        sense_own = share * (1.0 - tint)
        miss = share + preceding(share) + later - wide_ref[8 + c : 9 + c, :]
        part = miss * sense_zero
        slope_zero = part if slope_zero is None else slope_zero + part
        slope_rest.append(scale * miss * sense_own)
        for k in range(6):
            stack_ref[8 * c + k : 8 * c + k + 1, :] = (
                sense_zero * along[0][k] + sense_own * along[1 + c][k]
            )
        stack_ref[8 * c + 6 : 8 * c + 7, :] = share
    slopes = [scale * slope_zero] + slope_rest
    for slot in range(CAP):
        for o in range(4):
            samp_ref[SLOPE_LANE + 8 * slot + o : SLOPE_LANE + 8 * slot + o + 1, :] = jnp.where(
                rank == float(slot), slopes[o], 0.0
            )

    high, middle, _ = split_three(stack_ref[...])
    rays = dot_nt(jnp.concatenate([high, middle], axis=0), member)
    rays = rays[0:24] + rays[24:48]
    camera_rank = ray_ref[3:4, 0:RAYS]
    blocks = []
    row = iota((8, RAYS), 0)
    for c in range(3):
        block = rays[8 * c : 8 * c + 8]
        blocks.append(jnp.where(row == 6, block - ray_ref[c : c + 1, 0:RAYS], block))
    block_ref[...] = jnp.zeros_like(block_ref)
    for a in range(6):
        outer = blocks[0][a : a + 1] * blocks[0]
        outer = outer + blocks[1][a : a + 1] * blocks[1]
        outer = outer + blocks[2][a : a + 1] * blocks[2]
        for slot in range(CAPC):
            kept = jnp.where(camera_rank == float(slot), outer, 0.0)
            base = 48 * slot
            block_ref[base + 6 * a : base + 6 * a + 6, 0:RAYS] = kept[0:6]
            block_ref[base + FORCE_ROW + a : base + FORCE_ROW + a + 1, 0:RAYS] = kept[6:7]
    for slot in range(CAPC):
        base = 48 * slot + LABEL_ROW
        block_ref[base : base + 2, 0:RAYS] = jnp.where(
            camera_rank == float(slot), ray_ref[4:6, 0:RAYS], 0.0
        )
    message = dot_nt(camera_ref[...], block_ref[...].astype(BF16))
    message = (message + base_ref[...]) + dot_nt(hot, samp_ref[...].astype(BF16))
    out_ref[...] = message.astype(BF16)


def relay_kernel(got_ref, out_ref, wide_ref):
    wide_ref[...] = got_ref[...].astype(F32)
    for core in range(2):
        part = wide_ref[pl.ds(core, HALF, stride=2), :].astype(BF16)
        for rep in range(REPS):
            row = (2 * rep + core) * HALF
            out_ref[row : row + HALF, :] = part


def final_kernel(
    got_ref,
    wave_ref,
    bundle_ref,
    grad_first_hbm,
    grad_second_hbm,
    grad_head_hbm,
    normal_hbm,
    force_hbm,
    grad_first_ref,
    grad_second_ref,
    grad_head_ref,
    normal_ref,
    force_ref,
    spread_ref,
    left_ref,
    sems,
):
    first_out, second_out, head_out, normal_out, force_out = [
        pltpu.make_async_copy(source, place, sems.at[number])
        for number, (source, place) in enumerate(
            [
                (grad_first_ref, grad_first_hbm),
                (grad_second_ref, grad_second_hbm),
                (grad_head_ref, grad_head_hbm),
                (normal_ref, normal_hbm),
                (force_ref, force_hbm),
            ]
        )
    ]

    values = []
    group = []
    low_hot = []
    turned = []
    low_lane = iota((PEERS, LOW), 1).astype(F32)
    for rep in range(REPS):
        got = got_ref[rep * PEERS : (rep + 1) * PEERS, :].astype(F32)
        flipped = jnp.transpose(got)
        turned.append(flipped)
        for slot in range(CAPC):
            base = 48 * slot
            label = base + LABEL_ROW
            values.append(flipped[base : base + 48])
            group.append(flipped[label : label + 1])
            low_hot.append((got[:, label + 1 : label + 2] == low_lane).astype(BF16))
    values = jnp.concatenate(values, axis=1)
    group = jnp.concatenate(group, axis=1)
    low_hot = jnp.concatenate(low_hot, axis=0)
    for block in range(CAM_DEV // LOW):
        left_ref[48 * block : 48 * block + 48, :] = jnp.where(
            group == float(block), values, 0.0
        ).astype(BF16)
    table = dot_nn(left_ref[...], low_hot)
    for block in range(CAM_DEV // LOW):
        base = 48 * block
        place = slice(block * LOW, (block + 1) * LOW)
        normal_ref[:, place] = table[base : base + 36]
        force_ref[:, place] = table[base + FORCE_ROW : base + FORCE_ROW + 6]
    normal_out.start()
    force_out.start()

    columns = jnp.transpose(wave_ref[...]) * TURN
    for number in range(4):
        spread_ref[number] = jnp.broadcast_to(columns[:, number : number + 1], (HID, PEERS))
    first = bundle_ref[0:HID, :]
    second = bundle_ref[HID : 2 * HID, :]
    head = bundle_ref[2 * HID : BUNDLE, :]
    kept = []
    grad_head = None
    for part in range(2):
        features = []
        slopes = []
        for rep in range(2 * part, 2 * part + 2):
            flipped = turned[rep]
            for slot in range(CAP):
                angle = None
                for c in range(3):
                    lanes = [POINT_LANES[9 * slot + 3 * number + c] for number in range(3)]
                    high, middle, low = [flipped[lane : lane + 1] for lane in lanes]
                    term = spread_ref[c] * (high + middle + low)
                    angle = term if angle is None else angle + term
                features.append(sine_of(angle + spread_ref[3]).astype(BF16))
                base = SLOPE_LANE + 8 * slot
                slopes.append(flipped[base : base + 8])
        feature = jnp.concatenate(features, axis=1)
        slopes = jnp.concatenate(slopes, axis=1)
        slopes = jnp.concatenate([slopes, jnp.zeros_like(slopes)], axis=0).astype(BF16)
        value_one, slope_one = silu_pair(dot_tn(first, feature))
        hidden_one = value_one.astype(BF16)
        value_two, slope_two = silu_pair(dot_tn(second, hidden_one))
        hidden_two = value_two.astype(BF16)
        back_two = (dot_tn(head, slopes) * slope_two).astype(BF16)
        back_one = (dot_nn(second, back_two) * slope_one).astype(BF16)
        kept.append((feature, back_one, hidden_one, back_two))
        term = dot_nt(slopes, hidden_two)
        grad_head = term if grad_head is None else grad_head + term
    feature, back_one, hidden_one, back_two = [
        jnp.concatenate(pair, axis=1) for pair in zip(*kept)
    ]
    grad_head_ref[0] = grad_head[0:4]
    head_out.start()
    grad_second_ref[0] = dot_nt(hidden_one, back_two)
    second_out.start()
    grad_first_ref[0] = dot_nt(feature, back_one)
    first_out.start()
    for copy in (normal_out, force_out, head_out, second_out, first_out):
        copy.wait()


def call(kernel, out_shape, *args, hbm=(), unread=(), hbm_out=False, scratch=(), cost=0, room=8):
    def spec(number):
        if number in unread:
            return pl.BlockSpec(memory_space=pl.ANY)
        return pl.BlockSpec(memory_space=pltpu.HBM if number in hbm else pltpu.VMEM)

    place = pltpu.HBM if hbm_out else pltpu.VMEM
    args = [
        pltpu.with_memory_space_constraint(arg, pltpu.HBM) if number in hbm else arg
        for number, arg in enumerate(args)
    ]
    estimate = pl.CostEstimate(flops=cost, transcendentals=0, bytes_accessed=1 << 20)
    return pl.pallas_call(
        kernel,
        out_shape=out_shape,
        cost_estimate=estimate if cost else None,
        in_specs=[spec(number) for number in range(len(args))],
        out_specs=jax.tree.map(lambda _: pl.BlockSpec(memory_space=place), out_shape),
        scratch_shapes=list(scratch),
        compiler_params=pltpu.CompilerParams(vmem_limit_bytes=room * 1024 * 1024),
    )(*args)


def shape(*dims, dtype=F32):
    return jax.ShapeDtypeStruct(dims, dtype)


def exchange(value, axes="expert", groups=None):
    return lax.all_to_all(
        value, axes, split_axis=0, concat_axis=0, tiled=True, axis_index_groups=groups
    )


def per_device(
    positions,
    frequencies,
    phases,
    w_first,
    w_second,
    w_head,
    spacing,
    expert_ids,
    ray_lengths,
    target,
    cam_owner,
    cam_slot,
):
    ids_row = expert_ids.reshape(1, SAMP)
    square = shape(PEERS, PEERS, dtype=BF16)
    room = pltpu.VMEM((PEERS, PEERS), F32)
    arguments = (
        ids_row,
        positions,
        spacing.reshape(1, SAMP),
        ray_lengths,
        target,
        cam_owner.reshape(1, RAYS),
        cam_slot.reshape(1, RAYS),
        frequencies,
        phases.reshape(1, HID),
        w_first,
        w_second,
        w_head,
    )
    outgoing, *loaded = call(
        prep_kernel,
        (square, *(pltpu.VMEM(array.shape, array.dtype) for array in arguments)),
        *arguments,
        hbm=range(12),
        scratch=[pltpu.VMEM((PEERS, SAMP), F32), pltpu.SemaphoreType.DMA((12,))],
    )
    base, wide, ray, wave, hot, member, camera, bundle = call(
        setup_kernel,
        (
            pltpu.VMEM((PEERS, PEERS), F32),
            pltpu.VMEM((16, LANES), F32),
            pltpu.VMEM((8, PEERS), F32),
            pltpu.VMEM((8, HID), F32),
            pltpu.VMEM((PEERS, LANES), BF16),
            pltpu.VMEM((RAYS, LANES), BF16),
            pltpu.VMEM((PEERS, PEERS), BF16),
            shape(BUNDLE, HID, dtype=BF16),
        ),
        *loaded,
        scratch=[pltpu.VMEM((PEERS, LANES), F32)],
        cost=1 << 33,
    )
    same_core = [[2 * pair + core for pair in range(HALF)] for core in range(2)]
    chips = [[2 * pair, 2 * pair + 1] for pair in range(HALF)]
    both = lax.all_gather(bundle, "expert", axis=0, tiled=True, axis_index_groups=chips)
    points = exchange(outgoing, groups=same_core)
    fields = call(forward_kernel, square, points, wave, both, scratch=[room, room])
    returned = exchange(fields, groups=same_core)
    message = call(
        device_kernel,
        square,
        returned,
        wide,
        ray,
        hot,
        member,
        camera,
        base,
        scratch=[
            pltpu.VMEM((24, LANES), F32),
            pltpu.VMEM((PEERS, PEERS), F32),
            pltpu.VMEM((PEERS, LANES), F32),
        ],
    )
    arrived = exchange(message, groups=same_core)
    relayed = call(
        relay_kernel,
        shape(REPS * PEERS, PEERS, dtype=BF16),
        arrived,
        scratch=[room],
    )
    around = [
        [rep * PEERS + 2 * pair + core for rep in range(REPS) for core in range(2)]
        for pair in range(HALF)
    ]
    rows = REPS * CAP * PEERS
    everything = exchange(relayed, ("rep", "expert"), around)
    return call(
        final_kernel,
        (
            shape(1, HID, HID),
            shape(1, HID, HID),
            shape(1, 4, HID),
            shape(36, CAM_DEV),
            shape(6, CAM_DEV),
        ),
        everything,
        wave,
        bundle,
        hbm_out=True,
        room=32,
        scratch=[
            pltpu.VMEM((1, HID, HID), F32),
            pltpu.VMEM((1, HID, HID), F32),
            pltpu.VMEM((1, 4, HID), F32),
            pltpu.VMEM((36, CAM_DEV), F32),
            pltpu.VMEM((6, CAM_DEV), F32),
            pltpu.VMEM((4, HID, PEERS), F32),
            pltpu.VMEM((48 * (CAM_DEV // LOW), REPS * CAPC * PEERS), BF16),
            pltpu.SemaphoreType.DMA((5,)),
        ],
    )


def solution(mesh):
    in_specs = (
        P(None, ("rep", "expert")),
        P(),
        P(),
        P("expert", None, None),
        P("expert", None, None),
        P("expert", None, None),
        P(("rep", "expert")),
        P(("rep", "expert"), None),
        P(("rep", "expert"), None),
        P(None, ("rep", "expert")),
        P(("rep", "expert"), None),
        P(("rep", "expert")),
    )
    out_specs = (
        P("expert", None, None),
        P("expert", None, None),
        P("expert", None, None),
        P(None, "expert"),
        P(None, "expert"),
    )
    return jax.shard_map(
        per_device, mesh=mesh, in_specs=in_specs, out_specs=out_specs, check_vma=False
    )
```
